512 devices in a mesh: gx: 16 (over z_hi, y, core), gy: 32 (over z_lo, x).
Axes of the slice: x: 4, y: 4, z: 16 (z_hi: 2, z_lo: 8; z = z_hi * 8 + z_lo), core: 2. Of those that a mesh axis runs over, the one named last changes fastest.
Arguments:
- load: float32 [2, 512, 512, 128], P(None, 'gx', 'gy'), may hold values from -8 to 8
- zones: int32 [512, 512, 128], P('gx', 'gy'), may hold values from 0 to 7
- conductance: float32 [2, 8], replicated, may hold values from 0.2 to 1
- capacity: float32 [2, 8], replicated, may hold values from 0.5 to 2
- coupling: float32 [8], replicated, may hold values from 0.2 to 0.8
Outputs:
- solution: float32 [2, 512, 512, 128], P(None, 'gx', 'gy')
- residual: float32 [2, 512, 512, 128], P(None, 'gx', 'gy')
The draws below stay inside these ranges and needn't reach their ends.
All inputs are finite; a program needn't handle non-finite values.
Results may differ from the reference program's by a relative error of at most 0.006.
Values sent between devices are 32-bit elements; how exact they have to be, the bound alone decides.
A program may use at most 64 MiB of HBM per device.

```python
import math
import jax
import jax.numpy as jnp
from jax import lax

BOX = 16
ZONES = 8
ITERS = 2
NX = 512
NY = 512
NZ = 128


def draw_load(key, part):
    first_key = jax.random.fold_in(key, 0)
    place_x = (jnp.arange(NX, dtype=jnp.float32) + 0.5) / NX
    place_y = (jnp.arange(NY, dtype=jnp.float32) + 0.5) / NY
    scale = jnp.sqrt((1.0 + place_x)[:, None, None] * (1.0 + place_y)[None, :, None])
    values = jax.random.normal(first_key, (2, NX, NY, NZ), jnp.float32) * scale[None]
    return jnp.clip(values, -8.0, 8.0).astype(jnp.float32)


def plant(values, rng, least, high):
    spot = [jax.random.randint(jax.random.fold_in(rng, axis), (), 0, length) for axis, length in enumerate(values.shape)]
    longest = values.shape.index(max(values.shape))
    next_to = spot[:longest] + [(spot[longest] + 1) % values.shape[longest]] + spot[longest + 1:]
    return values.at[tuple(spot)].set(least).at[tuple(next_to)].set(high)


def setup_inputs(seed: int = 0) -> dict:
    key_of = jax.random.split(jax.random.key(seed), 6)
    load = draw_load(jax.random.fold_in(key_of[5], 71), 0)
    zones = plant(jax.random.randint(key_of[1], (NX, NY, NZ), 0, ZONES), jax.random.fold_in(key_of[1], 1), 0, ZONES - 1).astype(jnp.int32)
    conductance = jnp.clip(jnp.exp(jax.random.uniform(key_of[2], (2, ZONES), jnp.float32, math.log(0.2), math.log(1.0))), 0.2, 1.0)
    capacity = jnp.clip(jnp.exp(jax.random.uniform(key_of[3], (2, ZONES), jnp.float32, math.log(0.5), math.log(2.0))), 0.5, 2.0)
    coupling = jnp.clip(jax.random.uniform(key_of[4], (ZONES,), jnp.float32, 0.2, 0.8), 0.2, 0.8)
    return {"load": load, "zones": zones, "conductance": conductance, "capacity": capacity, "coupling": coupling}


NEIGHBOURS = ((1, 0, 0), (-1, 0, 0), (0, 1, 0), (0, -1, 0), (0, 0, 1), (0, 0, -1))

def neighbour(array, offset_x, offset_y, offset_z):
    size_x, size_y, size_z = array.shape[-3:]
    return array[..., 1 + offset_x:size_x - 1 + offset_x, 1 + offset_y:size_y - 1 + offset_y, 1 + offset_z:size_z - 1 + offset_z]

def apply_operator(field, padded, kpadded, inside, mass):
    center = kpadded[:, 1:-1, 1:-1, 1:-1]
    flux = jnp.zeros_like(field)
    for offset_x, offset_y, offset_z in NEIGHBOURS:
        other_k = neighbour(kpadded, offset_x, offset_y, offset_z)
        other_in = neighbour(inside, offset_x, offset_y, offset_z)
        face = 0.5 * (center + jnp.where(other_in[None], other_k, center))
        flux = flux + face * (field - neighbour(padded, offset_x, offset_y, offset_z))
    first = mass[0] * field[0] + mass[2] * field[1] + flux[0]
    second = mass[2] * field[0] + mass[1] * field[1] + flux[1]
    return jnp.stack([first, second])

def box_matrix(cells):
    span = BOX + 2
    count = cells // BOX
    rows = jnp.arange(count * span)
    block_of = rows // span
    mode_of = rows % span
    columns = jnp.arange(cells + 2)
    offset = columns[None, :] - BOX * block_of[:, None]
    valid = (offset >= 0) & (offset < span)
    angle_arg = jnp.pi * (offset + 1).astype(jnp.float32) * (mode_of[:, None] + 1).astype(jnp.float32) / (span + 1)
    basis = jnp.sqrt(2.0 / (span + 1)) * jnp.sin(angle_arg)
    return jnp.where(valid, basis, 0.0).astype(jnp.float32)

def box_eigen():
    span = BOX + 2
    modes = jnp.arange(span).astype(jnp.float32)
    return 4.0 * jnp.sin(jnp.pi * (modes + 1.0) / (2.0 * (span + 1))) ** 2

def box_means(values):
    fields, size_x, size_y, size_z = values.shape
    shaped = values.reshape(fields, size_x // BOX, BOX, size_y // BOX, BOX, size_z // BOX, BOX)
    return lax.optimization_barrier(jnp.mean(shaped, axis=(2, 4, 6)))

def solve_boxes(padded, cbar, kbar):
    highest = lax.Precision.HIGHEST
    fields, length_x, length_y, length_z = padded.shape
    matrix_x = box_matrix(length_x - 2)
    matrix_y = box_matrix(length_y - 2)
    matrix_z = box_matrix(length_z - 2)
    spectral = jnp.einsum('am,fmyz->fayz', matrix_x, padded, precision=highest)
    spectral = jnp.einsum('bn,fanz->fabz', matrix_y, spectral, precision=highest)
    spectral = jnp.einsum('co,fabo->fabc', matrix_z, spectral, precision=highest)
    boxes_x, boxes_y, boxes_z = cbar.shape[1:]
    span = BOX + 2
    eigen = box_eigen()
    summed = eigen[:, None, None] + eigen[None, :, None] + eigen[None, None, :]
    divisor = cbar[:, :, None, :, None, :, None] + kbar[:, :, None, :, None, :, None] * summed[None, None, :, None, :, None, :]
    spectral = spectral.reshape(fields, boxes_x, span, boxes_y, span, boxes_z, span) / divisor
    spectral = spectral.reshape(fields, boxes_x * span, boxes_y * span, boxes_z * span)
    spectral = jnp.einsum('co,fabc->fabo', matrix_z, spectral, precision=highest)
    spectral = jnp.einsum('bn,fabo->fano', matrix_y, spectral, precision=highest)
    return jnp.einsum('am,fano->fmno', matrix_x, spectral, precision=highest)

def reference(load, zones, conductance, capacity, coupling):
    cross = coupling * jnp.sqrt(capacity[0] * capacity[1])
    tables = jnp.concatenate([conductance, capacity, cross[None]], axis=0)
    marks = jnp.pad(zones + 1, 1)
    inside = marks > 0
    safe_marks = jnp.maximum(marks - 1, 0).astype(jnp.int32)
    kpadded = jnp.where(inside[None], jnp.take(tables[0:2], safe_marks, axis=1), 0.0)
    plain = zones.astype(jnp.int32)
    mass = jnp.take(tables[2:5], plain, axis=1)
    cbar = box_means(mass[0:2])
    kbar = box_means(kpadded[:, 1:-1, 1:-1, 1:-1])
    widths = ((0, 0), (1, 1), (1, 1), (1, 1))

    def operate(field):
        return apply_operator(field, jnp.pad(field, widths), kpadded, inside, mass)

    def precondition(vector):
        padded = jnp.pad(vector, widths)
        parts = []
        for field_index in range(2):
            result = solve_boxes(padded[field_index:field_index + 1], cbar[field_index:field_index + 1], kbar[field_index:field_index + 1])
            parts.append(result[0, 1:-1, 1:-1, 1:-1])
        return jnp.stack(parts)
    solution = jnp.zeros_like(load)
    residual = load
    direction = load
    previous = jnp.float32(1.0)
    for iteration in range(ITERS):
        precond = precondition(residual)
        product = jnp.sum(residual * precond)
        if iteration == 0:
            direction = precond
        else:
            direction = precond + product / previous * direction
        image = operate(direction)
        alpha = product / jnp.sum(direction * image)
        solution = solution + alpha * direction
        residual = residual - alpha * image
        previous = product
    return (solution, residual)
```

```python
import functools

import jax
import jax.numpy as jnp
import numpy as np
from jax import lax
from jax.experimental import pallas as pl
from jax.experimental.pallas import tpu as pltpu
from jax.sharding import PartitionSpec as P

BOX = 16
SPAN = BOX + 2
BX = 32
BY = 16
NZ = 128
ZONES = 8
LX = BX + 4
PX = 40
MODES = 336
OWN = SPAN * BY
KIN = OWN + 48
MOUT = OWN + 144
F32 = jnp.float32
BF16 = jnp.bfloat16
MESH = pl.DeviceIdType.MESH


def split3(matrix):
    high = np.asarray(matrix, np.float32).astype(jnp.bfloat16)
    low = (np.asarray(matrix, np.float32) - high.astype(np.float32)).astype(jnp.bfloat16)
    return high, low


def constants():
    index = np.arange(SPAN)
    basis = np.sqrt(2.0 / (SPAN + 1)) * np.sin(np.pi * np.outer(index + 1, index + 1) / (SPAN + 1))
    lam = 4.0 * np.sin(np.pi * (index + 1) / (2.0 * (SPAN + 1))) ** 2
    forward = np.zeros((SPAN, SPAN, KIN))
    inner = np.einsum("ix,jy->ijxy", basis, basis[:, 1:17])
    forward[:, :, :OWN] = inner.reshape(SPAN, SPAN, OWN)
    for side, row in ((0, 0), (1, 17)):
        start = OWN + 24 * side + 1
        forward[:, :, start : start + SPAN] = np.einsum("ix,j->ijx", basis, basis[:, row])
    full = np.zeros((MODES, KIN))
    full[: SPAN * SPAN] = forward.reshape(SPAN * SPAN, KIN)
    high, low = split3(full)
    to_modes = np.concatenate([high, high, low], axis=1)
    inverse = np.zeros((MOUT, SPAN, SPAN))
    inverse[:OWN] = np.einsum("xi,yj->xyij", basis, basis[1:17]).reshape(OWN, SPAN, SPAN)
    for place, row in enumerate((0, 1, 2, 15, 16, 17)):
        start = OWN + 24 * place + 1
        inverse[start : start + SPAN] = np.einsum("xi,j->xij", basis, basis[row])
    full = np.zeros((MOUT, MODES))
    full[:, : SPAN * SPAN] = inverse.reshape(MOUT, SPAN * SPAN)
    high, low = split3(full)
    from_modes = np.concatenate([high, high, low], axis=1)
    boxes = NZ // BOX
    count = boxes * SPAN
    banded = np.zeros((NZ, count))
    for box in range(boxes):
        for offset in range(SPAN):
            cell = BOX * box + offset - 1
            if 0 <= cell < NZ:
                banded[cell, box * SPAN : (box + 1) * SPAN] = basis[:, offset]
    rest = count - 128
    lanes = np.concatenate([np.arange(128)] + [128 + np.arange(rest)] * 3)
    wide = np.zeros((NZ, 256))
    wide[:, : lanes.size] = banded[:, lanes]
    high, low = split3(wide)
    z_forward = np.concatenate([high, high, low], axis=0)
    high, low = split3(banded.T)
    tail = np.zeros((128, NZ), jnp.bfloat16)
    tail[:rest] = high[128:]
    tail[rest : 2 * rest] = high[128:]
    tail[2 * rest : 3 * rest] = low[128:]
    z_inverse = np.concatenate([high[:128], high[:128], low[:128], tail], axis=0)
    summed = np.zeros((MODES, 256), np.float32)
    plane = (lam[:, None] + lam[None, :]).reshape(-1)
    summed[: SPAN * SPAN, : lanes.size] = plane[:, None] + lam[lanes % SPAN][None, :]
    group = np.zeros((NZ, 256))
    group[:, : lanes.size] = (np.arange(NZ)[:, None] // BOX) == (lanes // SPAN)[None, :]
    group = np.concatenate([group] * 3, axis=0).astype(jnp.bfloat16)
    return to_modes, from_modes, z_forward, z_inverse, summed, group


def lookup(zone, table):
    bit0 = (zone & 1) != 0
    bit1 = (zone & 2) != 0
    bit2 = (zone & 4) != 0

    def pick(values):
        a = jnp.where(bit0, values[1], values[0])
        b = jnp.where(bit0, values[3], values[2])
        c = jnp.where(bit0, values[5], values[4])
        d = jnp.where(bit0, values[7], values[6])
        return jnp.where(bit2, jnp.where(bit1, d, c), jnp.where(bit1, b, a))

    return [pick(values) for values in table]


def halves(value):
    high = value.astype(BF16)
    low = (value - high.astype(F32)).astype(BF16)
    return high, low


def dot(a, b):
    return jnp.dot(a, b, preferred_element_type=F32)


def body(
    nx, ny,
    load_ref, zones_ref, cond_ref, cap_ref, coup_ref,
    tf_hbm, ti_hbm, zf_hbm, zi_hbm, lam_hbm, group_hbm,
    x_out, r_out,
    tf, ti, zf, zi, lam, group,
    r_own, r_pk, zone, zone_pk, zone_send, zone_recv,
    r_send, r_recv, r_corner_send, r_corner,
    k_own, k_pk, c_own, c_pk, cross, cross_pk,
    fx, fym, fyp, fzm, fzp, diag, diag_pk, dinv,
    u1, p1, v1, zp, q_own, q_pk, u2, p2, v2, wp, u_vec,
    xl1, xc1, xcs1, yr1, dg1, dgs1, xl2, xc2, xcs2, yr2, dg2, dgs2,
    ar1, ar2,
    local_sem, send_sem, recv_sem, ar_send, ar_recv,
):
    gx = lax.axis_index("gx")
    gy = lax.axis_index("gy")
    has = {"xm": gx > 0, "xp": gx < nx - 1, "ym": gy > 0, "yp": gy < ny - 1}
    ax, ay = min(8, nx // 2), min(4, ny // 2)
    plane, depth = ax * ay, (nx // ax) * (ny // ay)
    here = (gx % ax) * ay + gy % ay
    level = (gx // ax) * (ny // ay) + gy // ay

    def plane_id(k):
        t = (here + k) % plane
        return ((gx // ax) * ax + t // ay, (gy // ay) * ay + t % ay)

    def depth_id(k):
        t = (level + k) % depth
        return ((t // (ny // ay)) * ax + gx % ax, (t % (ny // ay)) * ay + gy % ay)

    sides = [
        ("xm", has["xm"], (gx - 1, gy)),
        ("xp", has["xp"], (gx + 1, gy)),
        ("ym", has["ym"], (gx, gy - 1)),
        ("yp", has["yp"], (gx, gy + 1)),
        ("mm", jnp.logical_and(has["xm"], has["ym"]), (gx - 1, gy - 1)),
        ("pp", jnp.logical_and(has["xp"], has["yp"]), (gx + 1, gy + 1)),
        ("mp", jnp.logical_and(has["xm"], has["yp"]), (gx - 1, gy + 1)),
        ("pm", jnp.logical_and(has["xp"], has["ym"]), (gx + 1, gy - 1)),
    ]

    loads = [
        pltpu.make_async_copy(load_ref.at[0], r_own.at[0, 2:34], local_sem.at[0]),
        pltpu.make_async_copy(load_ref.at[1], r_own.at[1, 2:34], local_sem.at[1]),
        pltpu.make_async_copy(zones_ref, zone.at[2:34], local_sem.at[2]),
    ]
    weights = [
        pltpu.make_async_copy(source, target, local_sem.at[3 + n])
        for n, (source, target) in enumerate(
            ((tf_hbm, tf), (zf_hbm, zf), (group_hbm, group), (lam_hbm, lam), (zi_hbm, zi), (ti_hbm, ti))
        )
    ]
    for copy in loads + weights:
        copy.start()

    barrier = pltpu.get_barrier_semaphore()
    for _, present, device in sides:

        @pl.when(present)
        def _():
            pl.semaphore_signal(barrier, inc=1, device_id=device, device_id_type=MESH)

    def greet_plane(k, carry):
        pl.semaphore_signal(barrier, inc=1, device_id=plane_id(k), device_id_type=MESH)
        return carry

    def greet_depth(k, carry):
        pl.semaphore_signal(barrier, inc=1, device_id=depth_id(k), device_id_type=MESH)
        return carry

    lax.fori_loop(1, plane, greet_plane, 0)
    lax.fori_loop(1, depth, greet_depth, 0)

    def clear(*refs):
        for ref in refs:
            ref[...] = jnp.zeros(ref.shape, ref.dtype)

    r_pk[...] = jnp.zeros(r_pk.shape, F32)
    for side, name in enumerate(("xm", "xp")):

        @pl.when(jnp.logical_not(has[name]))
        def _():
            clear(r_own.at[0, 1 + 33 * side], r_own.at[1, 1 + 33 * side])
            clear(xl1.at[side], xc1.at[side], xl2.at[side], xc2.at[side])

    for side, name in enumerate(("ym", "yp")):

        @pl.when(jnp.logical_not(has[name]))
        def _():
            clear(r_recv.at[side], yr1.at[side], yr2.at[side])

    for corner in range(4):

        @pl.when(jnp.logical_not(sides[4 + corner][1]))
        def _():
            clear(r_corner.at[corner], dg1.at[corner], dg2.at[corner])

    for copy in loads:
        copy.wait()

    for field in range(2):
        r_send[0, field] = r_own[field, 2:34, 0]
        r_send[1, field] = r_own[field, 2:34, BY - 1]
    for corner, (layer, row) in enumerate(((2, 0), (33, 15), (2, 15), (33, 0))):
        for field in range(2):
            r_corner_send[corner, field : field + 1] = r_own[field, layer, row : row + 1]

    members = jnp.int32(plane - 1 + depth - 1)
    for _, present, _ in sides:
        members = members + present.astype(jnp.int32)
    pl.semaphore_wait(barrier, members)

    def remote(number, source, target, slot):
        _, present, device = sides[number]
        return present, pltpu.make_async_remote_copy(
            src_ref=source,
            dst_ref=target,
            send_sem=send_sem.at[slot],
            recv_sem=recv_sem.at[slot],
            device_id=device,
            device_id_type=MESH,
        )

    def start(copies):
        for present, copy in copies:

            @pl.when(present)
            def _():
                copy.start()

    def finish_recv(copies, arrives):
        for (_, copy), number in zip(copies, arrives):

            @pl.when(sides[number][1])
            def _():
                copy.wait_recv()

    def finish_send(copies):
        for present, copy in copies:

            @pl.when(present)
            def _():
                copy.wait_send()

    first = [
        remote(0, r_own.at[:, 2], r_own.at[:, 34], 0),
        remote(1, r_own.at[:, 33], r_own.at[:, 1], 1),
        remote(2, r_send.at[0], r_recv.at[1], 2),
        remote(3, r_send.at[1], r_recv.at[0], 3),
        remote(4, r_corner_send.at[0], r_corner.at[1], 4),
        remote(5, r_corner_send.at[1], r_corner.at[0], 5),
        remote(6, r_corner_send.at[2], r_corner.at[3], 6),
        remote(7, r_corner_send.at[3], r_corner.at[2], 7),
    ]
    origin = [1, 0, 3, 2, 5, 4, 7, 6]
    start(first)
    zone_x = [
        remote(0, zone.at[2:4], zone.at[34:36], 8),
        remote(1, zone.at[32:34], zone.at[0:2], 9),
    ]
    start(zone_x)

    table = [[ref[f, q] for q in range(ZONES)] for ref in (cond_ref, cap_ref) for f in range(2)]
    table.append([coup_ref[q] for q in range(ZONES)])

    def own_coefficients(layer, sums):
        k0, k1, c0, c1, share = lookup(zone[layer], table)
        k_own[layer, 8:24] = k0
        k_own[LX + layer, 8:24] = k1
        c_own[0, layer] = c0
        c_own[1, layer] = c1
        cross[layer] = share * jnp.sqrt(c0 * c1)
        return tuple(s + v[:8] + v[8:] for s, v in zip(sums, (c0, c1, k0, k1)))

    zero = jnp.zeros((8, NZ), F32)
    pieces = []
    for box in range(2):
        sums = lax.fori_loop(2 + BOX * box, 2 + BOX * (box + 1), own_coefficients, (zero,) * 4)
        pieces.extend(jnp.sum(s, axis=0, keepdims=True) for s in sums)
    total = jnp.concatenate(pieces, axis=0)
    part0 = total.astype(BF16)
    rest = total - part0.astype(F32)
    part1 = rest.astype(BF16)
    part2 = (rest - part1.astype(F32)).astype(BF16)
    for copy in weights:
        copy.wait()
    means = dot(jnp.concatenate([part0, part1, part2], axis=1), group[...]) * (1.0 / BOX**3)
    lane = lax.broadcasted_iota(jnp.int32, (1, 256), 1)
    unused = jnp.where(lane >= 128 + 48, 1.0, 0.0)
    for box in range(2):
        for field in range(2):
            cbar = means[4 * box + field : 4 * box + field + 1] + unused
            kbar = means[4 * box + 2 + field : 4 * box + 3 + field]
            dinv[2 * box + field] = 1.0 / (cbar + kbar * lam[...])

    lane_tail = lax.broadcasted_iota(jnp.int32, (1, 128), 1)
    low_lanes = jnp.logical_and(lane_tail >= 16, lane_tail < 32)

    def apply_boxes(own, packed, out, out_pk):
        for box in range(2):
            columns = []
            for field in range(2):
                inner = own[field, 1 + BOX * box : 1 + BOX * box + SPAN].reshape(OWN, NZ)
                edge = [packed[side, field, BOX * box : BOX * box + 24] for side in range(2)]
                columns.append(jnp.concatenate([inner] + edge, axis=0))
            high, low = halves(jnp.concatenate(columns, axis=1))
            modes = dot(tf[...], jnp.concatenate([high, low, high], axis=0))
            columns = []
            for field in range(2):
                high, low = halves(modes[:, NZ * field : NZ * (field + 1)])
                deep = dot(jnp.concatenate([high, low, high], axis=1), zf[...])
                deep = deep * dinv[2 * box + field]
                high, low = halves(deep[:, :128])
                tail = deep[:, 128:]
                tail_high = tail.astype(BF16).astype(F32)
                tail = jnp.where(low_lanes, tail - tail_high, tail_high).astype(BF16)
                columns.append(dot(jnp.concatenate([high, low, high, tail], axis=1), zi[...]))
            high, low = halves(jnp.concatenate(columns, axis=1))
            cells = dot(ti[...], jnp.concatenate([high, low, high], axis=0))
            for field in range(2):
                mine = cells[:, NZ * field : NZ * (field + 1)]
                inner = mine[:OWN].reshape(SPAN, BY, NZ)
                edge = mine[OWN:].reshape(6, 24, NZ)
                if box == 0:
                    out[field, 1:19] = inner
                    out_pk[:, field, 0:24] = edge
                else:
                    out[field, 17:19] += inner[:2]
                    out[field, 19:35] = inner[2:]
                    out_pk[:, field, 16:24] += edge[:, :8]
                    out_pk[:, field, 24:40] = edge[:, 8:]

    for (present, copy), number in zip(first, origin):

        @pl.when(sides[number][1])
        def _():
            copy.wait_recv()

    for side in range(2):
        for field in range(2):
            r_pk[side, field, 2:34] = r_recv[side, field]
    for corner, (side, spot) in enumerate(((0, 1), (1, 34), (1, 1), (0, 34))):
        for field in range(2):
            r_pk[side, field, spot : spot + 1] = r_corner[corner, field : field + 1]
    apply_boxes(r_own, r_pk, u1, p1)
    finish_send(first)

    def exchange(width, own, packed, x_layers, x_corner, x_corner_send, y_rows, corners, corners_send, slot):
        low_layer = 1
        high_layer = 35 - width
        rows_low = packed.at[0:width]
        rows_high = packed.at[6 - width : 6]
        for side in range(2):
            for place, row in enumerate((0, 5)):
                x_corner_send[side, place] = packed[row, :, 32 * side : 32 * side + 4]
        for corner, (x_side, y_side) in enumerate(((0, 0), (1, 1), (0, 1), (1, 0))):
            start_row = (6 - width) * y_side
            for place in range(width):
                corners_send[corner, place] = packed[start_row + place, :, 32 * x_side : 32 * x_side + 4]
        return [
            remote(0, own.at[:, low_layer : low_layer + width], x_layers.at[1], slot),
            remote(1, own.at[:, high_layer : high_layer + width], x_layers.at[0], slot + 1),
            remote(2, rows_low, y_rows.at[1], slot + 2),
            remote(3, rows_high, y_rows.at[0], slot + 3),
            remote(4, corners_send.at[0], corners.at[1], slot + 4),
            remote(5, corners_send.at[1], corners.at[0], slot + 5),
            remote(6, corners_send.at[2], corners.at[3], slot + 6),
            remote(7, corners_send.at[3], corners.at[2], slot + 7),
            remote(0, x_corner_send.at[0], x_corner.at[1], slot + 8),
            remote(1, x_corner_send.at[1], x_corner.at[0], slot + 9),
        ]

    origin10 = origin + [1, 0]
    second = exchange(3, u1, p1, xl1, xc1, xcs1, yr1, dg1, dgs1, 12)
    start(second)

    for (present, copy), number in zip(zone_x, origin[:2]):

        @pl.when(sides[number][1])
        def _():
            copy.wait_recv()

    finish_send(zone_x)
    for side, name in enumerate(("xm", "xp")):

        @pl.when(jnp.logical_not(has[name]))
        def _():
            edge = zone[2 + 31 * side]
            zone[34 * side] = edge
            zone[34 * side + 1] = edge

    for place, row in enumerate((0, 1, 14, 15)):
        zone_send[place] = jnp.zeros((PX, NZ), jnp.int32)
        zone_send[place, 0:LX] = zone[:, row]
    zone_y = [
        remote(2, zone_send.at[0:2], zone_recv.at[1], 10),
        remote(3, zone_send.at[2:4], zone_recv.at[0], 11),
    ]
    start(zone_y)
    for layer in (0, 1, 34, 35):
        k0, k1, c0, c1, share = lookup(zone[layer], table)
        k_own[layer, 8:24] = k0
        k_own[LX + layer, 8:24] = k1
        c_own[0, layer] = c0
        c_own[1, layer] = c1
        cross[layer] = share * jnp.sqrt(c0 * c1)
    for (present, copy), number in zip(zone_y, origin[2:4]):

        @pl.when(sides[number][1])
        def _():
            copy.wait_recv()

    finish_send(zone_y)
    for side, name in enumerate(("ym", "yp")):

        @pl.when(jnp.logical_not(has[name]))
        def _():
            edge = zone_send[3 * side]
            zone_recv[side, 0] = edge
            zone_recv[side, 1] = edge

    for place in range(6):
        packed_zone = (
            zone_recv[0, place] if place < 2
            else zone_send[0] if place == 2
            else zone_send[3] if place == 3
            else zone_recv[1, place - 4]
        )
        k0, k1, c0, c1, share = lookup(packed_zone, table)
        k_pk[place, 0] = k0
        k_pk[place, 1] = k1
        if place in (1, 4):
            side = 0 if place == 1 else 1
            c_pk[side, 0] = c0
            c_pk[side, 1] = c1
            cross_pk[side] = share * jnp.sqrt(c0 * c1)
            for field, value in enumerate((k0, k1)):
                k_own[LX * field : LX * (field + 1), 7 if side == 0 else 24] = value[:LX]

    lanes = lax.broadcasted_iota(jnp.int32, (BY, NZ), 1)
    first_lane, last_lane = lanes == 0, lanes == NZ - 1
    for field in range(2):
        fx[field, 0] = 0.5 * (k_own[LX * field, 8:24] + k_own[LX * field + 1, 8:24])

    def faces(layer, carry):
        for field in range(2):
            spot = LX * field + layer
            center = k_own[spot, 8:24]
            x_low = fx[field, layer - 1]
            x_high = 0.5 * (center + k_own[spot + 1, 8:24])
            fx[field, layer] = x_high
            y_low = 0.5 * (center + k_own[spot, 7:23])
            y_high = 0.5 * (center + k_own[spot, 9:25])
            z_low = 0.5 * (center + jnp.where(first_lane, center, pltpu.roll(center, 1, axis=1)))
            z_high = 0.5 * (center + jnp.where(last_lane, center, pltpu.roll(center, NZ - 1, axis=1)))
            fym[field, layer] = y_low
            fyp[field, layer] = y_high
            fzm[field, layer] = jnp.where(first_lane, 0.0, z_low)
            fzp[field, layer] = jnp.where(last_lane, 0.0, z_high)
            diag[field, layer] = c_own[field, layer] + (
                (x_low + x_high) + (y_low + y_high) + (z_low + z_high)
            )
        return carry

    lax.fori_loop(1, 35, faces, 0)

    lanes_pk = lax.broadcasted_iota(jnp.int32, (PX, NZ), 1)
    first_pk, last_pk = lanes_pk == 0, lanes_pk == NZ - 1
    rows_pk = lax.broadcasted_iota(jnp.int32, (PX, NZ), 0)

    def rim_faces(side, field):
        center = k_pk[1 + 3 * side, field]
        x_low = 0.5 * (center + pltpu.roll(center, 1, axis=0))
        x_high = 0.5 * (center + pltpu.roll(center, PX - 1, axis=0))
        y_low = 0.5 * (center + k_pk[3 * side, field])
        y_high = 0.5 * (center + k_pk[3 * side + 2, field])
        z_low = 0.5 * (center + jnp.where(first_pk, center, pltpu.roll(center, 1, axis=1)))
        z_high = 0.5 * (center + jnp.where(last_pk, center, pltpu.roll(center, NZ - 1, axis=1)))
        return x_low, x_high, y_low, y_high, z_low, z_high

    def outside(value, present):
        return jnp.where(present, value, 0.0)

    for (present, copy), number in zip(second, origin10):

        @pl.when(sides[number][1])
        def _():
            copy.wait_recv()

    def assemble(width, own, packed, x_layers, x_corner, y_rows, corners, total_v, total_pk, margin):
        low0, high0 = 3 - width, 33
        for field in range(2):
            base = LX * field

            def copy_layer(layer, carry):
                total_v[base + layer, 8:24] = own[field, layer]
                return carry

            lax.fori_loop(3, 33, copy_layer, 0)
            for step in range(width):
                layer = low0 + step
                value = x_layers[0, field, step]
                if layer >= 1:
                    value = value + own[field, layer]
                if layer < 2:
                    value = outside(value, has["xm"])
                total_v[base + layer, 8:24] = value
                layer = high0 + step
                value = x_layers[1, field, step]
                if layer <= 34:
                    value = value + own[field, layer]
                if layer > 33:
                    value = outside(value, has["xp"])
                total_v[base + layer, 8:24] = value
        for side in range(2):
            for step in range(width):
                y = 1 - width + step if side == 0 else 15 + step
                place = y + 2 if side == 0 else y - 12
                total_pk[place] = y_rows[side, step]
                minus, plus = (0, 3) if side == 0 else (2, 1)
                total_pk[place, :, 0:4] += corners[minus, step]
                total_pk[place, :, 32:36] += corners[plus, step]
                if y == -1 or y == 16:
                    total_pk[place] += packed[5 * side]
                    total_pk[place, :, 0:4] += x_corner[0, side]
                    total_pk[place, :, 32:36] += x_corner[1, side]
                if y < 0 or y > 15:
                    present = has["ym"] if side == 0 else has["yp"]
                    low_x = jnp.logical_and(rows_pk < 2, jnp.logical_not(has["xm"]))
                    high_x = jnp.logical_and(rows_pk > 33, jnp.logical_not(has["xp"]))
                    drop = jnp.logical_or(jnp.logical_or(low_x, high_x), jnp.logical_not(present))
                    for field in range(2):
                        total_pk[place, field] = jnp.where(drop, 0.0, total_pk[place, field])
        for field in range(2):
            lo = 2 - margin
            count = BX + 2 * margin
            for side, row, halo in ((0, 8, 7), (1, 23, 24)):
                place = 2 if side == 0 else 3
                window = slice(LX * field + lo, LX * field + lo + count)
                added = total_pk[place, field, lo : lo + count]
                spots = lax.broadcasted_iota(jnp.int32, (count, NZ), 0) + lo
                low_x = jnp.logical_and(spots < 2, jnp.logical_not(has["xm"]))
                high_x = jnp.logical_and(spots > 33, jnp.logical_not(has["xp"]))
                added = jnp.where(jnp.logical_or(low_x, high_x), 0.0, added)
                edge = total_v[window, row] + added
                total_v[window, row] = edge
                if margin > 1:
                    total_pk[place, field, lo : lo + count] = edge
                outer = 1 if side == 0 else 4
                total_v[window, halo] = total_pk[outer, field, lo : lo + count]

    assemble(3, u1, p1, xl1, xc1, yr1, dg1, v1, zp, 2)

    def operate(vec, layer, field):
        spot = LX * field + layer
        center = vec[spot, 8:24]
        value = diag[field, layer] * center + cross[layer] * vec[LX * (1 - field) + layer, 8:24]
        value = value - fx[field, layer - 1] * vec[spot - 1, 8:24] - fx[field, layer] * vec[spot + 1, 8:24]
        value = value - fym[field, layer] * vec[spot, 7:23] - fyp[field, layer] * vec[spot, 9:25]
        value = value - fzm[field, layer] * pltpu.roll(center, 1, axis=1)
        return value - fzp[field, layer] * pltpu.roll(center, NZ - 1, axis=1), center

    def fold(value):
        return value[:8] + value[8:]

    def first_image(layer, carry):
        rz, pq = carry
        for field in range(2):
            value, center = operate(v1, layer, field)
            q_own[field, layer] = value
            rz = rz + fold(r_own[field, layer] * center)
            pq = pq + fold(center * value)
        return rz, pq

    rz, pq = lax.fori_loop(2, 34, first_image, (zero, zero))
    for layer, name in ((1, "xm"), (34, "xp")):
        for field in range(2):
            value, _ = operate(v1, layer, field)
            q_own[field, layer] = outside(value, has[name])
    for side, name in enumerate(("ym", "yp")):
        center_place = 1 + 3 * side
        for field in range(2):
            x_low, x_high, y_low, y_high, z_low, z_high = rim_faces(side, field)
            center = zp[center_place, field]
            value = c_pk[side, field] + ((x_low + x_high) + (y_low + y_high) + (z_low + z_high))
            value = value * center + cross_pk[side] * zp[center_place, 1 - field]
            value = value - x_low * pltpu.roll(center, 1, axis=0) - x_high * pltpu.roll(center, PX - 1, axis=0)
            value = value - y_low * zp[3 * side, field] - y_high * zp[3 * side + 2, field]
            value = value - jnp.where(first_pk, 0.0, z_low) * pltpu.roll(center, 1, axis=1)
            value = value - jnp.where(last_pk, 0.0, z_high) * pltpu.roll(center, NZ - 1, axis=1)
            low_x = jnp.logical_and(rows_pk < 2, jnp.logical_not(has["xm"]))
            high_x = jnp.logical_and(rows_pk > 33, jnp.logical_not(has["xp"]))
            drop = jnp.logical_or(jnp.logical_or(low_x, high_x), jnp.logical_not(has[name]))
            unused_rows = jnp.logical_or(rows_pk < 1, rows_pk > 34)
            q_pk[side, field] = jnp.where(jnp.logical_or(drop, unused_rows), 0.0, value)

    apply_boxes(q_own, q_pk, u2, p2)
    third = exchange(2, u2, p2, xl2, xc2, xcs2, yr2, dg2, dgs2, 22)
    start(third)
    finish_send(second)
    for (present, copy), number in zip(third, origin10):

        @pl.when(sides[number][1])
        def _():
            copy.wait_recv()

    assemble(2, u2, p2, xl2, xc2, yr2, dg2, v2, wp, 1)

    def second_image(layer, carry):
        rw, qw, zu, wu = carry
        for field in range(2):
            value, center = operate(v2, layer, field)
            u_vec[field, layer] = value
            rw = rw + fold(r_own[field, layer] * center)
            qw = qw + fold(q_own[field, layer] * center)
            zu = zu + fold(v1[LX * field + layer, 8:24] * value)
            wu = wu + fold(center * value)
        return rw, qw, zu, wu

    rw, qw, zu, wu = lax.fori_loop(2, 34, second_image, (zero,) * 4)
    finish_send(third)

    sums = [jnp.sum(v, axis=0, keepdims=True) for v in (rz, pq, rw, qw, zu, wu)]
    ar1[0] = jnp.concatenate(sums + [jnp.zeros((2, NZ), F32)], axis=0)

    def all_reduce(slots, count, device_of, number):
        def send(k, carry):
            pltpu.make_async_remote_copy(
                src_ref=slots.at[0],
                dst_ref=slots.at[k],
                send_sem=ar_send.at[number],
                recv_sem=ar_recv.at[number],
                device_id=device_of(k),
                device_id_type=MESH,
            ).start()
            return carry

        lax.fori_loop(1, count, send, 0)
        others = slots.at[1:count]
        pltpu.make_async_copy(others, others, ar_recv.at[number]).wait()
        pltpu.make_async_copy(others, others, ar_send.at[number]).wait()
        return jnp.sum(slots[...], axis=0)

    ar2[0] = all_reduce(ar1, plane, plane_id, 0)
    products = jnp.sum(all_reduce(ar2, depth, depth_id, 1), axis=1, keepdims=True)
    rz, pq, rw, qw, zu, wu = (products[n : n + 1] for n in range(6))
    alpha = rz / pq
    rz2 = rz - alpha * (rw + pq) + alpha * alpha * qw
    grow = 1.0 + rz2 / rz
    curve = grow * grow * pq - grow * alpha * (zu + qw) + alpha * alpha * wu
    alpha2 = rz2 / curve
    by_z = jnp.broadcast_to(alpha + alpha2 * grow, (BY, NZ))
    by_w = jnp.broadcast_to(alpha2 * alpha, (BY, NZ))

    def finish(layer, carry):
        for field in range(2):
            spot = LX * field + layer
            x_out[field, layer - 2] = by_z * v1[spot, 8:24] - by_w * v2[spot, 8:24]
            r_out[field, layer - 2] = (
                r_own[field, layer] - by_z * q_own[field, layer] + by_w * u_vec[field, layer]
            )
        return carry

    lax.fori_loop(2, 34, finish, 0)


def shards(nx, ny, load, zones, conductance, capacity, coupling):
    to_modes, from_modes, z_forward, z_inverse, summed, group = constants()
    ax, ay = min(8, nx // 2), min(4, ny // 2)
    plane, depth = ax * ay, (nx // ax) * (ny // ay)
    vmem = lambda *shape, dtype=F32: pltpu.VMEM(shape, dtype)
    scratch = [
        vmem(*to_modes.shape, dtype=BF16), vmem(*from_modes.shape, dtype=BF16),
        vmem(*z_forward.shape, dtype=BF16), vmem(*z_inverse.shape, dtype=BF16),
        vmem(*summed.shape), vmem(*group.shape, dtype=BF16),
        vmem(2, LX, BY, NZ), vmem(2, 2, PX, NZ),
        vmem(LX, BY, NZ, dtype=jnp.int32), vmem(8, NZ, dtype=jnp.int32),
        vmem(4, PX, NZ, dtype=jnp.int32), vmem(2, 2, PX, NZ, dtype=jnp.int32),
        vmem(2, 2, BX, NZ), vmem(2, 2, BX, NZ), vmem(4, 2, NZ), vmem(4, 2, NZ),
        vmem(2 * LX, 32, NZ), vmem(6, 2, PX, NZ), vmem(2, LX, BY, NZ), vmem(2, 2, PX, NZ),
        vmem(LX, BY, NZ), vmem(2, PX, NZ),
        vmem(2, LX, BY, NZ), vmem(2, LX, BY, NZ), vmem(2, LX, BY, NZ), vmem(2, LX, BY, NZ),
        vmem(2, LX, BY, NZ), vmem(2, LX, BY, NZ), vmem(8, NZ), vmem(4, MODES, 256),
        vmem(2, LX, BY, NZ), vmem(6, 2, PX, NZ), vmem(2 * LX, 32, NZ), vmem(6, 2, PX, NZ),
        vmem(2, LX, BY, NZ), vmem(2, 2, PX, NZ),
        vmem(2, LX, BY, NZ), vmem(6, 2, PX, NZ), vmem(2 * LX, 32, NZ), vmem(6, 2, PX, NZ),
        vmem(2, LX, BY, NZ),
    ]
    for width in (3, 2):
        scratch += [
            vmem(2, 2, width, BY, NZ), vmem(2, 2, 2, 4, NZ), vmem(2, 2, 2, 4, NZ),
            vmem(2, width, 2, PX, NZ), vmem(4, width, 2, 4, NZ), vmem(4, width, 2, 4, NZ),
        ]
    scratch += [
        vmem(plane, 8, NZ), vmem(depth, 8, NZ),
        pltpu.SemaphoreType.DMA((9,)), pltpu.SemaphoreType.DMA((32,)), pltpu.SemaphoreType.DMA((32,)),
        pltpu.SemaphoreType.DMA((2,)), pltpu.SemaphoreType.DMA((2,)),
    ]
    any_spec = pl.BlockSpec(memory_space=pl.ANY)
    smem = pl.BlockSpec(memory_space=pltpu.SMEM)
    out = pl.BlockSpec(memory_space=pltpu.VMEM)
    shape = jax.ShapeDtypeStruct((2, BX, BY, NZ), F32)
    return pl.pallas_call(
        functools.partial(body, nx, ny),
        out_shape=(shape, shape),
        in_specs=[any_spec, any_spec, smem, smem, smem] + [any_spec] * 6,
        out_specs=(out, out),
        scratch_shapes=scratch,
        compiler_params=pltpu.CompilerParams(
            collective_id=0, has_side_effects=True, vmem_limit_bytes=48 * 1024 * 1024
        ),
        name="pcg",
    )(
        load, zones, conductance, capacity, coupling,
        *(jnp.asarray(c) for c in (to_modes, from_modes, z_forward, z_inverse, summed, group)),
    )


def solution(mesh):
    in_specs = (P(None, "gx", "gy", None), P("gx", "gy", None), P(), P(), P())
    out_specs = (P(None, "gx", "gy", None), P(None, "gx", "gy", None))
    run = functools.partial(shards, mesh.shape["gx"], mesh.shape["gy"])
    return jax.shard_map(run, mesh=mesh, in_specs=in_specs, out_specs=out_specs, check_vma=False)
```

```python
import functools

import jax
import jax.numpy as jnp
import numpy as np
from jax import lax
from jax.experimental import pallas as pl
from jax.experimental.pallas import tpu as pltpu
from jax.sharding import PartitionSpec as P

BOX = 16
SPAN = BOX + 2
BX = 32
BY = 16
NZ = 128
ZONES = 8
LX = BX + 4
PX = 40
MODES = 336
OWN = SPAN * BY
KIN = OWN + 48
MOUT = OWN + 144
F32 = jnp.float32
BF16 = jnp.bfloat16
MESH = pl.DeviceIdType.MESH


def split3(matrix):
    high = np.asarray(matrix, np.float32).astype(jnp.bfloat16)
    low = (np.asarray(matrix, np.float32) - high.astype(np.float32)).astype(jnp.bfloat16)
    return high, low


def constants():
    index = np.arange(SPAN)
    basis = np.sqrt(2.0 / (SPAN + 1)) * np.sin(np.pi * np.outer(index + 1, index + 1) / (SPAN + 1))
    lam = 4.0 * np.sin(np.pi * (index + 1) / (2.0 * (SPAN + 1))) ** 2
    forward = np.zeros((SPAN, SPAN, KIN))
    inner = np.einsum("ix,jy->ijxy", basis, basis[:, 1:17])
    forward[:, :, :OWN] = inner.reshape(SPAN, SPAN, OWN)
    for side, row in ((0, 0), (1, 17)):
        start = OWN + 24 * side + 1
        forward[:, :, start : start + SPAN] = np.einsum("ix,j->ijx", basis, basis[:, row])
    full = np.zeros((MODES, KIN))
    full[: SPAN * SPAN] = forward.reshape(SPAN * SPAN, KIN)
    high, low = split3(full)
    to_modes = np.concatenate([high, high, low], axis=1)
    inverse = np.zeros((MOUT, SPAN, SPAN))
    inverse[:OWN] = np.einsum("xi,yj->xyij", basis, basis[1:17]).reshape(OWN, SPAN, SPAN)
    for place, row in enumerate((0, 1, 2, 15, 16, 17)):
        start = OWN + 24 * place + 1
        inverse[start : start + SPAN] = np.einsum("xi,j->xij", basis, basis[row])
    full = np.zeros((MOUT, MODES))
    full[:, : SPAN * SPAN] = inverse.reshape(MOUT, SPAN * SPAN)
    high, low = split3(full)
    from_modes = np.concatenate([high, high, low], axis=1)
    boxes = NZ // BOX
    count = boxes * SPAN
    banded = np.zeros((NZ, count))
    for box in range(boxes):
        for offset in range(SPAN):
            cell = BOX * box + offset - 1
            if 0 <= cell < NZ:
                banded[cell, box * SPAN : (box + 1) * SPAN] = basis[:, offset]
    rest = count - 128
    lanes = np.concatenate([np.arange(128)] + [128 + np.arange(rest)] * 3)
    wide = np.zeros((NZ, 256))
    wide[:, : lanes.size] = banded[:, lanes]
    high, low = split3(wide)
    z_forward = np.concatenate([high, high, low], axis=0)
    high, low = split3(banded.T)
    tail = np.zeros((128, NZ), jnp.bfloat16)
    tail[:rest] = high[128:]
    tail[rest : 2 * rest] = high[128:]
    tail[2 * rest : 3 * rest] = low[128:]
    z_inverse = np.concatenate([high[:128], high[:128], low[:128], tail], axis=0)
    summed = np.zeros((MODES, 256), np.float32)
    plane = (lam[:, None] + lam[None, :]).reshape(-1)
    summed[: SPAN * SPAN, : lanes.size] = plane[:, None] + lam[lanes % SPAN][None, :]
    group = np.zeros((NZ, 256))
    group[:, : lanes.size] = (np.arange(NZ)[:, None] // BOX) == (lanes // SPAN)[None, :]
    group = np.concatenate([group] * 3, axis=0).astype(jnp.bfloat16)
    return to_modes, from_modes, z_forward, z_inverse, summed, group


def lookup(zone, table):
    bit0 = (zone & 1) != 0
    bit1 = (zone & 2) != 0
    bit2 = (zone & 4) != 0

    def pick(values):
        a = jnp.where(bit0, values[1], values[0])
        b = jnp.where(bit0, values[3], values[2])
        c = jnp.where(bit0, values[5], values[4])
        d = jnp.where(bit0, values[7], values[6])
        return jnp.where(bit2, jnp.where(bit1, d, c), jnp.where(bit1, b, a))

    return [pick(values) for values in table]


def halves(value):
    high = value.astype(BF16)
    low = (value - high.astype(F32)).astype(BF16)
    return high, low


def dot(a, b):
    return jnp.dot(a, b, preferred_element_type=F32)


def body(
    nx, ny,
    load_ref, zones_ref, cond_hbm, cap_hbm, coup_hbm,
    tf_hbm, ti_hbm, zf_hbm, zi_hbm, lam_hbm, group_hbm,
    x_out, r_out,
    cond_ref, cap_ref, coup_ref, tf, ti, zf, zi, lam, group,
    r_own, r_pk, zone, zone_pk, zone_send, zone_recv,
    r_send, r_recv, r_corner_send, r_corner,
    k_own, k_pk, c_own, c_pk, cross, cross_pk,
    fx, fym, fyp, fzm, fzp, diag, diag_pk, dinv,
    u1, p1, v1, zp, q_own, q_pk, u2, p2, v2, wp, u_vec,
    xl1, xc1, xcs1, yr1, dg1, dgs1, xl2, xc2, xcs2, yr2, dg2, dgs2,
    ar1, ar2,
    local_sem, send_sem, recv_sem, ar_send, ar_recv,
):
    gx = lax.axis_index("gx")
    gy = lax.axis_index("gy")
    has = {"xm": gx > 0, "xp": gx < nx - 1, "ym": gy > 0, "yp": gy < ny - 1}
    ax, ay = min(8, nx // 2), min(4, ny // 2)
    plane, depth = ax * ay, (nx // ax) * (ny // ay)
    div, rem = lax.div, lax.rem
    across, along = nx // ax, ny // ay
    gx_block, gx_in = div(gx, jnp.int32(ax)), rem(gx, jnp.int32(ax))
    gy_block, gy_in = div(gy, jnp.int32(ay)), rem(gy, jnp.int32(ay))
    here = gx_in * ay + gy_in
    level = gx_block * along + gy_block

    def plane_id(k):
        t = rem(here + k, jnp.int32(plane))
        return (gx_block * ax + div(t, jnp.int32(ay)), gy_block * ay + rem(t, jnp.int32(ay)))

    def depth_id(k):
        t = rem(level + k, jnp.int32(depth))
        return (div(t, jnp.int32(along)) * ax + gx_in, rem(t, jnp.int32(along)) * ay + gy_in)

    sides = [
        ("xm", has["xm"], (gx - 1, gy)),
        ("xp", has["xp"], (gx + 1, gy)),
        ("ym", has["ym"], (gx, gy - 1)),
        ("yp", has["yp"], (gx, gy + 1)),
        ("mm", jnp.logical_and(has["xm"], has["ym"]), (gx - 1, gy - 1)),
        ("pp", jnp.logical_and(has["xp"], has["yp"]), (gx + 1, gy + 1)),
        ("mp", jnp.logical_and(has["xm"], has["yp"]), (gx - 1, gy + 1)),
        ("pm", jnp.logical_and(has["xp"], has["ym"]), (gx + 1, gy - 1)),
    ]

    loads = [
        pltpu.make_async_copy(load_ref.at[0], r_own.at[0, 2:34], local_sem.at[0]),
        pltpu.make_async_copy(load_ref.at[1], r_own.at[1, 2:34], local_sem.at[1]),
        pltpu.make_async_copy(zones_ref, zone.at[2:34], local_sem.at[2]),
        pltpu.make_async_copy(cond_hbm, cond_ref, local_sem.at[9]),
        pltpu.make_async_copy(cap_hbm, cap_ref, local_sem.at[10]),
        pltpu.make_async_copy(coup_hbm, coup_ref, local_sem.at[11]),
    ]
    weights = [
        pltpu.make_async_copy(source, target, local_sem.at[3 + n])
        for n, (source, target) in enumerate(
            ((tf_hbm, tf), (zf_hbm, zf), (group_hbm, group), (lam_hbm, lam), (zi_hbm, zi), (ti_hbm, ti))
        )
    ]
    for copy in loads + weights:
        copy.start()

    barrier = pltpu.get_barrier_semaphore()
    for _, present, device in sides:

        @pl.when(present)
        def _():
            pl.semaphore_signal(barrier, inc=1, device_id=device, device_id_type=MESH)

    def greet_plane(k, carry):
        pl.semaphore_signal(barrier, inc=1, device_id=plane_id(k), device_id_type=MESH)
        return carry

    def greet_depth(k, carry):
        pl.semaphore_signal(barrier, inc=1, device_id=depth_id(k), device_id_type=MESH)
        return carry

    lax.fori_loop(1, plane, greet_plane, 0)
    lax.fori_loop(1, depth, greet_depth, 0)

    def clear(*refs):
        for ref in refs:
            ref[...] = jnp.zeros(ref.shape, ref.dtype)

    r_pk[...] = jnp.zeros(r_pk.shape, F32)
    for side, name in enumerate(("xm", "xp")):

        @pl.when(jnp.logical_not(has[name]))
        def _():
            clear(r_own.at[0, 1 + 33 * side], r_own.at[1, 1 + 33 * side])
            clear(xl1.at[side], xc1.at[side], xl2.at[side], xc2.at[side])

    for side, name in enumerate(("ym", "yp")):

        @pl.when(jnp.logical_not(has[name]))
        def _():
            clear(r_recv.at[side], yr1.at[side], yr2.at[side])

    for corner in range(4):

        @pl.when(jnp.logical_not(sides[4 + corner][1]))
        def _():
            clear(r_corner.at[corner], dg1.at[corner], dg2.at[corner])

    for copy in loads:
        copy.wait()

    for field in range(2):
        r_send[0, field] = r_own[field, 2:34, 0]
        r_send[1, field] = r_own[field, 2:34, BY - 1]
    for corner, (layer, row) in enumerate(((2, 0), (33, 15), (2, 15), (33, 0))):
        for field in range(2):
            r_corner_send[corner, field : field + 1] = r_own[field, layer, row : row + 1]

    members = jnp.int32(plane - 1 + depth - 1)
    for _, present, _ in sides:
        members = members + present.astype(jnp.int32)
    pl.semaphore_wait(barrier, members)

    def remote(number, source, target, slot):
        _, present, device = sides[number]
        return present, pltpu.make_async_remote_copy(
            src_ref=source,
            dst_ref=target,
            send_sem=send_sem.at[slot],
            recv_sem=recv_sem.at[slot],
            device_id=device,
            device_id_type=MESH,
        )

    def start(copies):
        for present, copy in copies:

            @pl.when(present)
            def _():
                copy.start()

    def finish_recv(copies, arrives):
        for (_, copy), number in zip(copies, arrives):

            @pl.when(sides[number][1])
            def _():
                copy.wait_recv()

    def finish_send(copies):
        for present, copy in copies:

            @pl.when(present)
            def _():
                copy.wait_send()

    first = [
        remote(0, r_own.at[:, 2], r_own.at[:, 34], 0),
        remote(1, r_own.at[:, 33], r_own.at[:, 1], 1),
        remote(2, r_send.at[0], r_recv.at[1], 2),
        remote(3, r_send.at[1], r_recv.at[0], 3),
        remote(4, r_corner_send.at[0], r_corner.at[1], 4),
        remote(5, r_corner_send.at[1], r_corner.at[0], 5),
        remote(6, r_corner_send.at[2], r_corner.at[3], 6),
        remote(7, r_corner_send.at[3], r_corner.at[2], 7),
    ]
    origin = [1, 0, 3, 2, 5, 4, 7, 6]
    start(first)
    zone_x = [
        remote(0, zone.at[2:4], zone.at[34:36], 8),
        remote(1, zone.at[32:34], zone.at[0:2], 9),
    ]
    start(zone_x)

    table = [[ref[f, q] for q in range(ZONES)] for ref in (cond_ref, cap_ref) for f in range(2)]
    table.append([coup_ref[q] for q in range(ZONES)])

    def own_coefficients(layer, sums):
        k0, k1, c0, c1, share = lookup(zone[layer], table)
        k_own[layer, 8:24] = k0
        k_own[LX + layer, 8:24] = k1
        c_own[0, layer] = c0
        c_own[1, layer] = c1
        cross[layer] = share * jnp.sqrt(c0 * c1)
        return tuple(s + v[:8] + v[8:] for s, v in zip(sums, (c0, c1, k0, k1)))

    zero = jnp.zeros((8, NZ), F32)
    pieces = []
    for box in range(2):
        sums = lax.fori_loop(2 + BOX * box, 2 + BOX * (box + 1), own_coefficients, (zero,) * 4)
        pieces.extend(jnp.sum(s, axis=0, keepdims=True) for s in sums)
    total = jnp.concatenate(pieces, axis=0)
    part0 = total.astype(BF16)
    rest = total - part0.astype(F32)
    part1 = rest.astype(BF16)
    part2 = (rest - part1.astype(F32)).astype(BF16)
    for copy in weights:
        copy.wait()
    means = dot(jnp.concatenate([part0, part1, part2], axis=1), group[...]) * (1.0 / BOX**3)
    lane = lax.broadcasted_iota(jnp.int32, (1, 256), 1)
    unused = jnp.where(lane >= 128 + 48, 1.0, 0.0)
    for box in range(2):
        for field in range(2):
            cbar = means[4 * box + field : 4 * box + field + 1] + unused
            kbar = means[4 * box + 2 + field : 4 * box + 3 + field]
            dinv[2 * box + field] = 1.0 / (cbar + kbar * lam[...])

    lane_tail = lax.broadcasted_iota(jnp.int32, (1, 128), 1)
    low_lanes = jnp.logical_and(lane_tail >= 16, lane_tail < 32)

    def apply_boxes(own, packed, out, out_pk):
        for box in range(2):
            columns = []
            for field in range(2):
                inner = own[field, 1 + BOX * box : 1 + BOX * box + SPAN].reshape(OWN, NZ)
                edge = [packed[side, field, BOX * box : BOX * box + 24] for side in range(2)]
                columns.append(jnp.concatenate([inner] + edge, axis=0))
            high, low = halves(jnp.concatenate(columns, axis=1))
            modes = dot(tf[...], jnp.concatenate([high, low, high], axis=0))
            columns = []
            for field in range(2):
                high, low = halves(modes[:, NZ * field : NZ * (field + 1)])
                deep = dot(jnp.concatenate([high, low, high], axis=1), zf[...])
                deep = deep * dinv[2 * box + field]
                high, low = halves(deep[:, :128])
                tail = deep[:, 128:]
                tail_high = tail.astype(BF16).astype(F32)
                tail = jnp.where(low_lanes, tail - tail_high, tail_high).astype(BF16)
                columns.append(dot(jnp.concatenate([high, low, high, tail], axis=1), zi[...]))
            high, low = halves(jnp.concatenate(columns, axis=1))
            cells = dot(ti[...], jnp.concatenate([high, low, high], axis=0))
            for field in range(2):
                mine = cells[:, NZ * field : NZ * (field + 1)]
                inner = mine[:OWN].reshape(SPAN, BY, NZ)
                edge = mine[OWN:].reshape(6, 24, NZ)
                if box == 0:
                    out[field, 1:19] = inner
                    out_pk[:, field, 0:24] = edge
                else:
                    out[field, 17:19] += inner[:2]
                    out[field, 19:35] = inner[2:]
                    out_pk[:, field, 16:24] += edge[:, :8]
                    out_pk[:, field, 24:40] = edge[:, 8:]

    for (present, copy), number in zip(first, origin):

        @pl.when(sides[number][1])
        def _():
            copy.wait_recv()

    for side in range(2):
        for field in range(2):
            r_pk[side, field, 2:34] = r_recv[side, field]
    for corner, (side, spot) in enumerate(((0, 1), (1, 34), (1, 1), (0, 34))):
        for field in range(2):
            r_pk[side, field, spot : spot + 1] = r_corner[corner, field : field + 1]
    apply_boxes(r_own, r_pk, u1, p1)
    finish_send(first)

    def exchange(width, own, packed, x_layers, x_corner, x_corner_send, y_rows, corners, corners_send, slot):
        low_layer = 1
        high_layer = 35 - width
        rows_low = packed.at[0:width]
        rows_high = packed.at[6 - width : 6]
        for side in range(2):
            for place, row in enumerate((0, 5)):
                x_corner_send[side, place] = packed[row, :, 32 * side : 32 * side + 4]
        for corner, (x_side, y_side) in enumerate(((0, 0), (1, 1), (0, 1), (1, 0))):
            start_row = (6 - width) * y_side
            for place in range(width):
                corners_send[corner, place] = packed[start_row + place, :, 32 * x_side : 32 * x_side + 4]
        return [
            remote(0, own.at[:, low_layer : low_layer + width], x_layers.at[1], slot),
            remote(1, own.at[:, high_layer : high_layer + width], x_layers.at[0], slot + 1),
            remote(2, rows_low, y_rows.at[1], slot + 2),
            remote(3, rows_high, y_rows.at[0], slot + 3),
            remote(4, corners_send.at[0], corners.at[1], slot + 4),
            remote(5, corners_send.at[1], corners.at[0], slot + 5),
            remote(6, corners_send.at[2], corners.at[3], slot + 6),
            remote(7, corners_send.at[3], corners.at[2], slot + 7),
            remote(0, x_corner_send.at[0], x_corner.at[1], slot + 8),
            remote(1, x_corner_send.at[1], x_corner.at[0], slot + 9),
        ]

    origin10 = origin + [1, 0]

    def start_far_first(copies):
        along_y = copies[2:4]
        others = copies[:2] + copies[8:] + copies[4:8]
        start(others)
        finish_send(others)
        start(along_y)

    second = exchange(3, u1, p1, xl1, xc1, xcs1, yr1, dg1, dgs1, 12)
    start_far_first(second)

    for (present, copy), number in zip(zone_x, origin[:2]):

        @pl.when(sides[number][1])
        def _():
            copy.wait_recv()

    finish_send(zone_x)
    for side, name in enumerate(("xm", "xp")):

        @pl.when(jnp.logical_not(has[name]))
        def _():
            edge = zone[2 + 31 * side]
            zone[34 * side] = edge
            zone[34 * side + 1] = edge

    for place, row in enumerate((0, 1, 14, 15)):
        zone_send[place] = jnp.zeros((PX, NZ), jnp.int32)
        zone_send[place, 0:LX] = zone[:, row]
    zone_y = [
        remote(2, zone_send.at[0:2], zone_recv.at[1], 10),
        remote(3, zone_send.at[2:4], zone_recv.at[0], 11),
    ]
    start(zone_y)
    for layer in (0, 1, 34, 35):
        k0, k1, c0, c1, share = lookup(zone[layer], table)
        k_own[layer, 8:24] = k0
        k_own[LX + layer, 8:24] = k1
        c_own[0, layer] = c0
        c_own[1, layer] = c1
        cross[layer] = share * jnp.sqrt(c0 * c1)
    for (present, copy), number in zip(zone_y, origin[2:4]):

        @pl.when(sides[number][1])
        def _():
            copy.wait_recv()

    finish_send(zone_y)
    for side, name in enumerate(("ym", "yp")):

        @pl.when(jnp.logical_not(has[name]))
        def _():
            edge = zone_send[3 * side]
            zone_recv[side, 0] = edge
            zone_recv[side, 1] = edge

    for place in range(6):
        packed_zone = (
            zone_recv[0, place] if place < 2
            else zone_send[0] if place == 2
            else zone_send[3] if place == 3
            else zone_recv[1, place - 4]
        )
        k0, k1, c0, c1, share = lookup(packed_zone, table)
        k_pk[place, 0] = k0
        k_pk[place, 1] = k1
        if place in (1, 4):
            side = 0 if place == 1 else 1
            c_pk[side, 0] = c0
            c_pk[side, 1] = c1
            cross_pk[side] = share * jnp.sqrt(c0 * c1)
            for field, value in enumerate((k0, k1)):
                k_own[LX * field : LX * (field + 1), 7 if side == 0 else 24] = value[:LX]

    lanes = lax.broadcasted_iota(jnp.int32, (BY, NZ), 1)
    first_lane, last_lane = lanes == 0, lanes == NZ - 1
    for field in range(2):
        fx[field, 0] = 0.5 * (k_own[LX * field, 8:24] + k_own[LX * field + 1, 8:24])

    def faces(layer, carry):
        for field in range(2):
            spot = LX * field + layer
            center = k_own[spot, 8:24]
            x_low = fx[field, layer - 1]
            x_high = 0.5 * (center + k_own[spot + 1, 8:24])
            fx[field, layer] = x_high
            y_low = 0.5 * (center + k_own[spot, 7:23])
            y_high = 0.5 * (center + k_own[spot, 9:25])
            z_low = 0.5 * (center + jnp.where(first_lane, center, pltpu.roll(center, 1, axis=1)))
            z_high = 0.5 * (center + jnp.where(last_lane, center, pltpu.roll(center, NZ - 1, axis=1)))
            fym[field, layer] = y_low
            fyp[field, layer] = y_high
            fzm[field, layer] = jnp.where(first_lane, 0.0, z_low)
            fzp[field, layer] = jnp.where(last_lane, 0.0, z_high)
            diag[field, layer] = c_own[field, layer] + (
                (x_low + x_high) + (y_low + y_high) + (z_low + z_high)
            )
        return carry

    lax.fori_loop(1, 35, faces, 0, unroll=2)

    lanes_pk = lax.broadcasted_iota(jnp.int32, (PX, NZ), 1)
    first_pk, last_pk = lanes_pk == 0, lanes_pk == NZ - 1
    rows_pk = lax.broadcasted_iota(jnp.int32, (PX, NZ), 0)

    def rim_faces(side, field):
        center = k_pk[1 + 3 * side, field]
        x_low = 0.5 * (center + pltpu.roll(center, 1, axis=0))
        x_high = 0.5 * (center + pltpu.roll(center, PX - 1, axis=0))
        y_low = 0.5 * (center + k_pk[3 * side, field])
        y_high = 0.5 * (center + k_pk[3 * side + 2, field])
        z_low = 0.5 * (center + jnp.where(first_pk, center, pltpu.roll(center, 1, axis=1)))
        z_high = 0.5 * (center + jnp.where(last_pk, center, pltpu.roll(center, NZ - 1, axis=1)))
        return x_low, x_high, y_low, y_high, z_low, z_high

    def outside(value, present):
        return jnp.where(present, value, 0.0)

    for (present, copy), number in zip(second, origin10):

        @pl.when(sides[number][1])
        def _():
            copy.wait_recv()

    def assemble(width, own, packed, x_layers, x_corner, y_rows, corners, total_v, total_pk, margin):
        low0, high0 = 3 - width, 33
        for field in range(2):
            base = LX * field

            def copy_layer(layer, carry):
                total_v[base + layer, 8:24] = own[field, layer]
                return carry

            lax.fori_loop(3, 33, copy_layer, 0, unroll=6)
            for step in range(width):
                layer = low0 + step
                value = x_layers[0, field, step]
                if layer >= 1:
                    value = value + own[field, layer]
                if layer < 2:
                    value = outside(value, has["xm"])
                total_v[base + layer, 8:24] = value
                layer = high0 + step
                value = x_layers[1, field, step]
                if layer <= 34:
                    value = value + own[field, layer]
                if layer > 33:
                    value = outside(value, has["xp"])
                total_v[base + layer, 8:24] = value
        for side in range(2):
            for step in range(width):
                y = 1 - width + step if side == 0 else 15 + step
                place = y + 2 if side == 0 else y - 12
                total_pk[place] = y_rows[side, step]
                minus, plus = (0, 3) if side == 0 else (2, 1)
                total_pk[place, :, 0:4] += corners[minus, step]
                total_pk[place, :, 32:36] += corners[plus, step]
                if y == -1 or y == 16:
                    total_pk[place] += packed[5 * side]
                    total_pk[place, :, 0:4] += x_corner[0, side]
                    total_pk[place, :, 32:36] += x_corner[1, side]
                if y < 0 or y > 15:
                    present = has["ym"] if side == 0 else has["yp"]
                    low_x = jnp.logical_and(rows_pk < 2, jnp.logical_not(has["xm"]))
                    high_x = jnp.logical_and(rows_pk > 33, jnp.logical_not(has["xp"]))
                    drop = jnp.logical_or(jnp.logical_or(low_x, high_x), jnp.logical_not(present))
                    for field in range(2):
                        total_pk[place, field] = jnp.where(drop, 0.0, total_pk[place, field])
        for field in range(2):
            lo = 2 - margin
            count = BX + 2 * margin
            for side, row, halo in ((0, 8, 7), (1, 23, 24)):
                place = 2 if side == 0 else 3
                window = slice(LX * field + lo, LX * field + lo + count)
                added = total_pk[place, field, lo : lo + count]
                spots = lax.broadcasted_iota(jnp.int32, (count, NZ), 0) + lo
                low_x = jnp.logical_and(spots < 2, jnp.logical_not(has["xm"]))
                high_x = jnp.logical_and(spots > 33, jnp.logical_not(has["xp"]))
                added = jnp.where(jnp.logical_or(low_x, high_x), 0.0, added)
                edge = total_v[window, row] + added
                total_v[window, row] = edge
                if margin > 1:
                    total_pk[place, field, lo : lo + count] = edge
                outer = 1 if side == 0 else 4
                total_v[window, halo] = total_pk[outer, field, lo : lo + count]

    assemble(3, u1, p1, xl1, xc1, yr1, dg1, v1, zp, 2)

    def operate(vec, layer, field):
        spot = LX * field + layer
        center = vec[spot, 8:24]
        value = diag[field, layer] * center + cross[layer] * vec[LX * (1 - field) + layer, 8:24]
        value = value - fx[field, layer - 1] * vec[spot - 1, 8:24] - fx[field, layer] * vec[spot + 1, 8:24]
        value = value - fym[field, layer] * vec[spot, 7:23] - fyp[field, layer] * vec[spot, 9:25]
        value = value - fzm[field, layer] * pltpu.roll(center, 1, axis=1)
        return value - fzp[field, layer] * pltpu.roll(center, NZ - 1, axis=1), center

    def fold(value):
        return value[:8] + value[8:]

    def first_image(layer, carry):
        rz, pq = carry
        for field in range(2):
            value, center = operate(v1, layer, field)
            q_own[field, layer] = value
            rz = rz + fold(r_own[field, layer] * center)
            pq = pq + fold(center * value)
        return rz, pq

    rz, pq = lax.fori_loop(2, 34, first_image, (zero, zero), unroll=4)
    for layer, name in ((1, "xm"), (34, "xp")):
        for field in range(2):
            value, _ = operate(v1, layer, field)
            q_own[field, layer] = outside(value, has[name])
    for side, name in enumerate(("ym", "yp")):
        center_place = 1 + 3 * side
        for field in range(2):
            x_low, x_high, y_low, y_high, z_low, z_high = rim_faces(side, field)
            center = zp[center_place, field]
            value = c_pk[side, field] + ((x_low + x_high) + (y_low + y_high) + (z_low + z_high))
            value = value * center + cross_pk[side] * zp[center_place, 1 - field]
            value = value - x_low * pltpu.roll(center, 1, axis=0) - x_high * pltpu.roll(center, PX - 1, axis=0)
            value = value - y_low * zp[3 * side, field] - y_high * zp[3 * side + 2, field]
            value = value - jnp.where(first_pk, 0.0, z_low) * pltpu.roll(center, 1, axis=1)
            value = value - jnp.where(last_pk, 0.0, z_high) * pltpu.roll(center, NZ - 1, axis=1)
            low_x = jnp.logical_and(rows_pk < 2, jnp.logical_not(has["xm"]))
            high_x = jnp.logical_and(rows_pk > 33, jnp.logical_not(has["xp"]))
            drop = jnp.logical_or(jnp.logical_or(low_x, high_x), jnp.logical_not(has[name]))
            unused_rows = jnp.logical_or(rows_pk < 1, rows_pk > 34)
            q_pk[side, field] = jnp.where(jnp.logical_or(drop, unused_rows), 0.0, value)

    apply_boxes(q_own, q_pk, u2, p2)
    third = exchange(2, u2, p2, xl2, xc2, xcs2, yr2, dg2, dgs2, 22)
    start_far_first(third)
    finish_send(second[2:4])
    for (present, copy), number in zip(third, origin10):

        @pl.when(sides[number][1])
        def _():
            copy.wait_recv()

    assemble(2, u2, p2, xl2, xc2, yr2, dg2, v2, wp, 1)

    def second_image(layer, carry):
        rw, qw, zu, wu = carry
        for field in range(2):
            value, center = operate(v2, layer, field)
            u_vec[field, layer] = value
            rw = rw + fold(r_own[field, layer] * center)
            qw = qw + fold(q_own[field, layer] * center)
            zu = zu + fold(v1[LX * field + layer, 8:24] * value)
            wu = wu + fold(center * value)
        return rw, qw, zu, wu

    rw, qw, zu, wu = lax.fori_loop(2, 34, second_image, (zero,) * 4, unroll=4)
    finish_send(third[2:4])

    spot = lax.broadcasted_iota(jnp.int32, (1, NZ), 1)
    row = jnp.zeros((1, NZ), F32)
    for place, value in enumerate((rz, pq, rw, qw, zu, wu)):
        row = jnp.where(spot == place, jnp.sum(value), row)
    ar1[0] = row

    def all_reduce(slots, count, device_of, number):
        def send(k, carry):
            pltpu.make_async_remote_copy(
                src_ref=slots.at[0],
                dst_ref=slots.at[k],
                send_sem=ar_send.at[number],
                recv_sem=ar_recv.at[number],
                device_id=device_of(k),
                device_id_type=MESH,
            ).start()
            return carry

        for k in range(1, count):
            send(k, 0)
        others = slots.at[1:count]
        pltpu.make_async_copy(others, others, ar_recv.at[number]).wait()
        pltpu.make_async_copy(others, others, ar_send.at[number]).wait()
        return jnp.sum(slots[...], axis=0)

    ar2[0] = all_reduce(ar1, plane, plane_id, 0)
    products = all_reduce(ar2, depth, depth_id, 1)
    rz, pq, rw, qw, zu, wu = (
        jnp.sum(jnp.where(spot == n, products, 0.0), axis=1, keepdims=True) for n in range(6)
    )
    alpha = rz / pq
    rz2 = rz - alpha * (rw + pq) + alpha * alpha * qw
    grow = 1.0 + rz2 / rz
    curve = grow * grow * pq - grow * alpha * (zu + qw) + alpha * alpha * wu
    alpha2 = rz2 / curve
    by_z = jnp.broadcast_to(alpha + alpha2 * grow, (BY, NZ))
    by_w = jnp.broadcast_to(alpha2 * alpha, (BY, NZ))

    def finish(layer, carry):
        for field in range(2):
            spot = LX * field + layer
            x_out[field, layer - 2] = by_z * v1[spot, 8:24] - by_w * v2[spot, 8:24]
            r_out[field, layer - 2] = (
                r_own[field, layer] - by_z * q_own[field, layer] + by_w * u_vec[field, layer]
            )
        return carry

    lax.fori_loop(2, 34, finish, 0, unroll=4)


def shards(nx, ny, load, zones, conductance, capacity, coupling):
    to_modes, from_modes, z_forward, z_inverse, summed, group = constants()
    ax, ay = min(8, nx // 2), min(4, ny // 2)
    plane, depth = ax * ay, (nx // ax) * (ny // ay)
    vmem = lambda *shape, dtype=F32: pltpu.VMEM(shape, dtype)
    scratch = [
        pltpu.SMEM((2, ZONES), F32), pltpu.SMEM((2, ZONES), F32), pltpu.SMEM((ZONES,), F32),
        vmem(*to_modes.shape, dtype=BF16), vmem(*from_modes.shape, dtype=BF16),
        vmem(*z_forward.shape, dtype=BF16), vmem(*z_inverse.shape, dtype=BF16),
        vmem(*summed.shape), vmem(*group.shape, dtype=BF16),
        vmem(2, LX, BY, NZ), vmem(2, 2, PX, NZ),
        vmem(LX, BY, NZ, dtype=jnp.int32), vmem(8, NZ, dtype=jnp.int32),
        vmem(4, PX, NZ, dtype=jnp.int32), vmem(2, 2, PX, NZ, dtype=jnp.int32),
        vmem(2, 2, BX, NZ), vmem(2, 2, BX, NZ), vmem(4, 2, NZ), vmem(4, 2, NZ),
        vmem(2 * LX, 32, NZ), vmem(6, 2, PX, NZ), vmem(2, LX, BY, NZ), vmem(2, 2, PX, NZ),
        vmem(LX, BY, NZ), vmem(2, PX, NZ),
        vmem(2, LX, BY, NZ), vmem(2, LX, BY, NZ), vmem(2, LX, BY, NZ), vmem(2, LX, BY, NZ),
        vmem(2, LX, BY, NZ), vmem(2, LX, BY, NZ), vmem(8, NZ), vmem(4, MODES, 256),
        vmem(2, LX, BY, NZ), vmem(6, 2, PX, NZ), vmem(2 * LX, 32, NZ), vmem(6, 2, PX, NZ),
        vmem(2, LX, BY, NZ), vmem(2, 2, PX, NZ),
        vmem(2, LX, BY, NZ), vmem(6, 2, PX, NZ), vmem(2 * LX, 32, NZ), vmem(6, 2, PX, NZ),
        vmem(2, LX, BY, NZ),
    ]
    for width in (3, 2):
        scratch += [
            vmem(2, 2, width, BY, NZ), vmem(2, 2, 2, 4, NZ), vmem(2, 2, 2, 4, NZ),
            vmem(2, width, 2, PX, NZ), vmem(4, width, 2, 4, NZ), vmem(4, width, 2, 4, NZ),
        ]
    scratch += [
        vmem(plane, 1, NZ), vmem(depth, 1, NZ),
        pltpu.SemaphoreType.DMA((12,)), pltpu.SemaphoreType.DMA((32,)), pltpu.SemaphoreType.DMA((32,)),
        pltpu.SemaphoreType.DMA((2,)), pltpu.SemaphoreType.DMA((2,)),
    ]
    any_spec = pl.BlockSpec(memory_space=pltpu.HBM)
    out = pl.BlockSpec(memory_space=pltpu.VMEM)
    shape = jax.ShapeDtypeStruct((2, BX, BY, NZ), F32)
    return pl.pallas_call(
        functools.partial(body, nx, ny),
        out_shape=(shape, shape),
        in_specs=[any_spec] * 11,
        out_specs=(out, out),
        scratch_shapes=scratch,
        compiler_params=pltpu.CompilerParams(
            collective_id=0, has_side_effects=True, vmem_limit_bytes=48 * 1024 * 1024
        ),
        name="pcg",
    )(
        *(pltpu.with_memory_space_constraint(a, pltpu.HBM) for a in (load, zones, conductance, capacity, coupling)),
        *(pltpu.with_memory_space_constraint(jnp.asarray(c), pltpu.HBM) for c in (to_modes, from_modes, z_forward, z_inverse, summed, group)),
    )


def solution(mesh):
    in_specs = (P(None, "gx", "gy", None), P("gx", "gy", None), P(), P(), P())
    out_specs = (P(None, "gx", "gy", None), P(None, "gx", "gy", None))
    run = functools.partial(shards, mesh.shape["gx"], mesh.shape["gy"])
    return jax.shard_map(run, mesh=mesh, in_specs=in_specs, out_specs=out_specs, check_vma=False)
```

```python
import functools

import jax
import jax.numpy as jnp
import numpy as np
from jax import lax
from jax.experimental import pallas as pl
from jax.experimental.pallas import tpu as pltpu
from jax.sharding import PartitionSpec as P

BOX = 16
SPAN = BOX + 2
BX = 32
BY = 16
NZ = 128
ZONES = 8
LX = BX + 4
PX = 40
MODES = 336
OWN = SPAN * BY
KIN = OWN + 48
MOUT = OWN + 144
F32 = jnp.float32
BF16 = jnp.bfloat16
MESH = pl.DeviceIdType.MESH


def split3(matrix):
    high = np.asarray(matrix, np.float32).astype(jnp.bfloat16)
    low = (np.asarray(matrix, np.float32) - high.astype(np.float32)).astype(jnp.bfloat16)
    return high, low


def constants():
    index = np.arange(SPAN)
    basis = np.sqrt(2.0 / (SPAN + 1)) * np.sin(np.pi * np.outer(index + 1, index + 1) / (SPAN + 1))
    lam = 4.0 * np.sin(np.pi * (index + 1) / (2.0 * (SPAN + 1))) ** 2
    forward = np.zeros((SPAN, SPAN, KIN))
    inner = np.einsum("ix,jy->ijxy", basis, basis[:, 1:17])
    forward[:, :, :OWN] = inner.reshape(SPAN, SPAN, OWN)
    for side, row in ((0, 0), (1, 17)):
        start = OWN + 24 * side + 1
        forward[:, :, start : start + SPAN] = np.einsum("ix,j->ijx", basis, basis[:, row])
    full = np.zeros((MODES, KIN))
    full[: SPAN * SPAN] = forward.reshape(SPAN * SPAN, KIN)
    high, low = split3(full)
    to_modes = np.concatenate([high, high, low], axis=1)
    inverse = np.zeros((MOUT, SPAN, SPAN))
    inverse[:OWN] = np.einsum("xi,yj->xyij", basis, basis[1:17]).reshape(OWN, SPAN, SPAN)
    for place, row in enumerate((0, 1, 2, 15, 16, 17)):
        start = OWN + 24 * place + 1
        inverse[start : start + SPAN] = np.einsum("xi,j->xij", basis, basis[row])
    full = np.zeros((MOUT, MODES))
    full[:, : SPAN * SPAN] = inverse.reshape(MOUT, SPAN * SPAN)
    high, low = split3(full)
    from_modes = np.concatenate([high, high, low], axis=1)
    boxes = NZ // BOX
    count = boxes * SPAN
    banded = np.zeros((NZ, count))
    for box in range(boxes):
        for offset in range(SPAN):
            cell = BOX * box + offset - 1
            if 0 <= cell < NZ:
                banded[cell, box * SPAN : (box + 1) * SPAN] = basis[:, offset]
    rest = count - 128
    lanes = np.concatenate([np.arange(128)] + [128 + np.arange(rest)] * 3)
    wide = np.zeros((NZ, 256))
    wide[:, : lanes.size] = banded[:, lanes]
    high, low = split3(wide)
    z_forward = np.concatenate([high, high, low], axis=0)
    high, low = split3(banded.T)
    tail = np.zeros((128, NZ), jnp.bfloat16)
    tail[:rest] = high[128:]
    tail[rest : 2 * rest] = high[128:]
    tail[2 * rest : 3 * rest] = low[128:]
    z_inverse = np.concatenate([high[:128], high[:128], low[:128], tail], axis=0)
    summed = np.zeros((MODES, 256), np.float32)
    plane = (lam[:, None] + lam[None, :]).reshape(-1)
    summed[: SPAN * SPAN, : lanes.size] = plane[:, None] + lam[lanes % SPAN][None, :]
    group = np.zeros((NZ, 256))
    group[:, : lanes.size] = (np.arange(NZ)[:, None] // BOX) == (lanes // SPAN)[None, :]
    group = np.concatenate([group] * 3, axis=0).astype(jnp.bfloat16)
    return to_modes, from_modes, z_forward, z_inverse, summed, group


def lookup(zone, table):
    bit0 = (zone & 1) != 0
    bit1 = (zone & 2) != 0
    bit2 = (zone & 4) != 0

    def pick(values):
        a = jnp.where(bit0, values[1], values[0])
        b = jnp.where(bit0, values[3], values[2])
        c = jnp.where(bit0, values[5], values[4])
        d = jnp.where(bit0, values[7], values[6])
        return jnp.where(bit2, jnp.where(bit1, d, c), jnp.where(bit1, b, a))

    return [pick(values) for values in table]


def halves(value):
    high = value.astype(BF16)
    low = (value - high.astype(F32)).astype(BF16)
    return high, low


def dot(a, b):
    return jnp.dot(a, b, preferred_element_type=F32)


def body(
    nx, ny,
    load_ref, zones_ref, cond_hbm, cap_hbm, coup_hbm,
    tf_hbm, ti_hbm, zf_hbm, zi_hbm, lam_hbm, group_hbm,
    x_out, r_out,
    cond_ref, cap_ref, coup_ref, tf, ti, zf, zi, lam, group,
    r_own, r_pk, zone, zone_pk, zone_send, zone_recv,
    r_send, r_recv, r_corner_send, r_corner,
    k_own, k_pk, c_own, c_pk, cross, cross_pk,
    fx, fym, fyp, fzm, fzp, diag, diag_pk, dinv,
    u1, p1, v1, zp, q_own, q_pk, u2, p2, v2, wp, u_vec,
    xl1, xc1, xcs1, yr1, dg1, dgs1, xl2, xc2, xcs2, yr2, dg2, dgs2,
    ar1, ar2,
    local_sem, send_sem, recv_sem, ar_send, ar_recv,
):
    gx = lax.axis_index("gx")
    gy = lax.axis_index("gy")
    has = {"xm": gx > 0, "xp": gx < nx - 1, "ym": gy > 0, "yp": gy < ny - 1}
    ax, ay = min(8, nx // 2), min(4, ny // 2)
    plane, depth = ax * ay, (nx // ax) * (ny // ay)
    div, rem = lax.div, lax.rem
    across, along = nx // ax, ny // ay
    gx_block, gx_in = div(gx, jnp.int32(ax)), rem(gx, jnp.int32(ax))
    gy_block, gy_in = div(gy, jnp.int32(ay)), rem(gy, jnp.int32(ay))
    here = gx_in * ay + gy_in
    level = gx_block * along + gy_block

    def plane_id(k):
        t = rem(here + k, jnp.int32(plane))
        return (gx_block * ax + div(t, jnp.int32(ay)), gy_block * ay + rem(t, jnp.int32(ay)))

    def depth_id(k):
        t = rem(level + k, jnp.int32(depth))
        return (div(t, jnp.int32(along)) * ax + gx_in, rem(t, jnp.int32(along)) * ay + gy_in)

    late = jnp.where(gx_in == 0, 0, 1).astype(jnp.int32)
    near = 1 - late
    near_gx, late_gx = gx + 1 - 2 * late, gx - 1 + 2 * late
    near_here = jnp.logical_and(near_gx >= 0, near_gx < nx)
    late_here = jnp.logical_and(late_gx >= 0, late_gx < nx)
    y_here = (has["ym"], has["yp"])
    sides = [(has["xm"], (gx - 1, gy)), (has["xp"], (gx + 1, gy)), (has["ym"], (gx, gy - 1)), (has["yp"], (gx, gy + 1))]
    for c in range(4):
        present = jnp.logical_and(sides[c // 2][0], y_here[c % 2])
        sides.append((present, (gx - 1 + 2 * (c // 2), gy - 1 + 2 * (c % 2))))

    loads = [
        pltpu.make_async_copy(load_ref.at[0], r_own.at[0, 2:34], local_sem.at[0]),
        pltpu.make_async_copy(load_ref.at[1], r_own.at[1, 2:34], local_sem.at[1]),
        pltpu.make_async_copy(zones_ref, zone.at[2:34], local_sem.at[2]),
        pltpu.make_async_copy(cond_hbm, cond_ref, local_sem.at[9]),
        pltpu.make_async_copy(cap_hbm, cap_ref, local_sem.at[10]),
        pltpu.make_async_copy(coup_hbm, coup_ref, local_sem.at[11]),
    ]
    weights = [
        pltpu.make_async_copy(source, target, local_sem.at[3 + n])
        for n, (source, target) in enumerate(
            ((tf_hbm, tf), (zf_hbm, zf), (group_hbm, group), (lam_hbm, lam), (zi_hbm, zi), (ti_hbm, ti))
        )
    ]
    for copy in loads + weights:
        copy.start()

    barrier = pltpu.get_barrier_semaphore()
    for present, device in sides:

        @pl.when(present)
        def _():
            pl.semaphore_signal(barrier, inc=1, device_id=device, device_id_type=MESH)

    def greet_plane(k, carry):
        pl.semaphore_signal(barrier, inc=1, device_id=plane_id(k), device_id_type=MESH)
        return carry

    def greet_depth(k, carry):
        pl.semaphore_signal(barrier, inc=1, device_id=depth_id(k), device_id_type=MESH)
        return carry

    lax.fori_loop(1, plane, greet_plane, 0)
    lax.fori_loop(1, depth, greet_depth, 0)

    def clear(*refs):
        for ref in refs:
            ref[...] = jnp.zeros(ref.shape, ref.dtype)

    clear(r_pk, u1, p1, u2, p2)
    for side, name in enumerate(("xm", "xp")):

        @pl.when(jnp.logical_not(has[name]))
        def _():
            clear(r_own.at[0, 1 + 33 * side], r_own.at[1, 1 + 33 * side])
            clear(xl1.at[side], xc1.at[side], xl2.at[side], xc2.at[side])

    for side, name in enumerate(("ym", "yp")):

        @pl.when(jnp.logical_not(has[name]))
        def _():
            clear(r_recv.at[side], yr1.at[side], yr2.at[side])

    for corner in range(4):

        @pl.when(jnp.logical_not(sides[4 + corner][0]))
        def _():
            clear(r_corner.at[corner], dg1.at[corner], dg2.at[corner])

    for copy in loads:
        copy.wait()

    for field in range(2):
        r_send[0, field] = r_own[field, 2:34, 0]
        r_send[1, field] = r_own[field, 2:34, BY - 1]
    for corner, (layer, row) in enumerate(((2, 0), (2, 15), (33, 0), (33, 15))):
        for field in range(2):
            r_corner_send[corner, field : field + 1] = r_own[field, layer, row : row + 1]

    members = jnp.int32(plane - 1 + depth - 1)
    for present, _ in sides:
        members = members + present.astype(jnp.int32)
    pl.semaphore_wait(barrier, members)

    def push(present, device, source, target, out_slot, in_slot):
        @pl.when(present)
        def _():
            pltpu.make_async_remote_copy(
                src_ref=source,
                dst_ref=target,
                send_sem=send_sem.at[out_slot],
                recv_sem=recv_sem.at[in_slot],
                device_id=device,
                device_id_type=MESH,
            ).start()

    def pushed(present, source, slot):
        @pl.when(present)
        def _():
            pltpu.make_async_copy(source, source, send_sem.at[slot]).wait()

    def arrived(present, target, slot):
        @pl.when(present)
        def _():
            pltpu.make_async_copy(target, target, recv_sem.at[slot]).wait()

    for n in range(2):
        push(*sides[n], r_own.at[:, 2 + 31 * n], r_own.at[:, 34 - 33 * n], n, 1 - n)
    for c in range(4):
        push(*sides[4 + c], r_corner_send.at[c], r_corner.at[3 - c], 4 + c, 7 - c)
    for n in range(2):
        push(*sides[2 + n], r_send.at[n], r_recv.at[1 - n], 2 + n, 3 - n)
    for n in range(2):
        push(*sides[n], zone.at[2 + 30 * n : 4 + 30 * n], zone.at[34 - 34 * n : 36 - 34 * n], 30 + n, 31 - n)

    table = [[ref[f, q] for q in range(ZONES)] for ref in (cond_ref, cap_ref) for f in range(2)]
    table.append([coup_ref[q] for q in range(ZONES)])

    def own_coefficients(layer, sums):
        k0, k1, c0, c1, share = lookup(zone[layer], table)
        k_own[layer, 8:24] = k0
        k_own[LX + layer, 8:24] = k1
        c_own[0, layer] = c0
        c_own[1, layer] = c1
        cross[layer] = share * jnp.sqrt(c0 * c1)
        return tuple(s + v[:8] + v[8:] for s, v in zip(sums, (c0, c1, k0, k1)))

    zero = jnp.zeros((8, NZ), F32)
    pieces = []
    for box in range(2):
        sums = lax.fori_loop(2 + BOX * box, 2 + BOX * (box + 1), own_coefficients, (zero,) * 4)
        pieces.extend(jnp.sum(s, axis=0, keepdims=True) for s in sums)
    total = jnp.concatenate(pieces, axis=0)
    part0 = total.astype(BF16)
    rest = total - part0.astype(F32)
    part1 = rest.astype(BF16)
    part2 = (rest - part1.astype(F32)).astype(BF16)
    for copy in weights:
        copy.wait()
    means = dot(jnp.concatenate([part0, part1, part2], axis=1), group[...]) * (1.0 / BOX**3)
    lane = lax.broadcasted_iota(jnp.int32, (1, 256), 1)
    unused = jnp.where(lane >= 128 + 48, 1.0, 0.0)
    for box in range(2):
        for field in range(2):
            cbar = means[4 * box + field : 4 * box + field + 1] + unused
            kbar = means[4 * box + 2 + field : 4 * box + 3 + field]
            dinv[2 * box + field] = 1.0 / (cbar + kbar * lam[...])

    lane_tail = lax.broadcasted_iota(jnp.int32, (1, 128), 1)
    low_lanes = jnp.logical_and(lane_tail >= 16, lane_tail < 32)

    def apply_box(own, packed, out, out_pk, box):
        layers = pl.ds(1 + BOX * box, SPAN)
        spots = pl.ds(pl.multiple_of(BOX * box, 8), 24)
        columns = []
        for field in range(2):
            inner = own[field, layers].reshape(OWN, NZ)
            columns.append(jnp.concatenate([inner] + [packed[side, field, spots] for side in range(2)], axis=0))
        high, low = halves(jnp.concatenate(columns, axis=1))
        modes = dot(tf[...], jnp.concatenate([high, low, high], axis=0))
        columns = []
        for field in range(2):
            high, low = halves(modes[:, NZ * field : NZ * (field + 1)])
            deep = dot(jnp.concatenate([high, low, high], axis=1), zf[...])
            deep = deep * dinv[2 * box + field]
            high, low = halves(deep[:, :128])
            tail = deep[:, 128:]
            tail_high = tail.astype(BF16).astype(F32)
            tail = jnp.where(low_lanes, tail - tail_high, tail_high).astype(BF16)
            columns.append(dot(jnp.concatenate([high, low, high, tail], axis=1), zi[...]))
        high, low = halves(jnp.concatenate(columns, axis=1))
        cells = dot(ti[...], jnp.concatenate([high, low, high], axis=0))
        for field in range(2):
            mine = cells[:, NZ * field : NZ * (field + 1)]
            out[field, layers] += mine[:OWN].reshape(SPAN, BY, NZ)
            out_pk[:, field, spots] += mine[OWN:].reshape(6, 24, NZ)

    def tile(side):
        return pl.ds(pl.multiple_of(32 * side, 8), 4)

    def x_messages(width, own, packed, bufs, base, side, present, side_gx, act):
        x_layers, x_corner, x_corner_send, y_rows, corners, corners_send = bufs
        layers = pl.ds(1 + (34 - width) * side, width)
        device = (side_gx, gy)
        if act == "push":
            for place, row in enumerate((0, 5)):
                x_corner_send[side, place] = packed[row, :, tile(side)]
            push(present, device, own.at[:, layers], x_layers.at[1 - side], base + side, base + 1 - side)
            push(present, device, x_corner_send.at[side], x_corner.at[1 - side], base + 8 + side, base + 9 - side)
        elif act == "pushed":
            pushed(present, own.at[:, layers], base + side)
            pushed(present, x_corner_send.at[side], base + 8 + side)
        else:
            arrived(present, x_layers.at[side], base + side)
            arrived(present, x_corner.at[side], base + 8 + side)
        for n in range(2):
            c = 2 * side + n
            both = jnp.logical_and(present, y_here[n])
            if act == "push":
                for place in range(width):
                    corners_send[c, place] = packed[(6 - width) * n + place, :, tile(side)]
                device = (side_gx, gy - 1 + 2 * n)
                push(both, device, corners_send.at[c], corners.at[3 - c], base + 4 + c, base + 7 - c)
            elif act == "pushed":
                pushed(both, corners_send.at[c], base + 4 + c)
            else:
                arrived(both, corners.at[c], base + 4 + c)

    def y_messages(width, packed, bufs, base, act):
        y_rows = bufs[3]
        for n in range(2):
            rows = packed.at[(6 - width) * n : (6 - width) * n + width]
            if act == "push":
                push(*sides[2 + n], rows, y_rows.at[1 - n], base + 2 + n, base + 3 - n)
            elif act == "pushed":
                pushed(y_here[n], rows, base + 2 + n)
            else:
                arrived(y_here[n], y_rows.at[n], base + 2 + n)

    rows_pk = lax.broadcasted_iota(jnp.int32, (PX, NZ), 0)

    def corner_rows(side):
        for n in range(2):
            for field in range(2):
                row = r_corner[2 * side + n, field : field + 1]
                r_pk[n, field] = jnp.where(rows_pk == 1 + 33 * side, row, r_pk[n, field])

    for n in range(2):
        arrived(y_here[n], r_recv.at[n], 2 + n)
        for field in range(2):
            r_pk[n, field, 2:34] = r_recv[n, field]
        arrived(jnp.logical_and(near_here, y_here[n]), r_corner.at[2 * near + n], 4 + 2 * near + n)
    arrived(near_here, r_own.at[:, 1 + 33 * near], near)
    corner_rows(near)
    set1 = (xl1, xc1, xcs1, yr1, dg1, dgs1)
    set2 = (xl2, xc2, xcs2, yr2, dg2, dgs2)
    apply_box(r_own, r_pk, u1, p1, near)
    x_messages(3, u1, p1, set1, 10, near, near_here, near_gx, "push")
    for n in range(2):
        arrived(jnp.logical_and(late_here, y_here[n]), r_corner.at[2 * late + n], 4 + 2 * late + n)
    arrived(late_here, r_own.at[:, 1 + 33 * late], late)
    corner_rows(late)
    apply_box(r_own, r_pk, u1, p1, late)
    x_messages(3, u1, p1, set1, 10, late, late_here, late_gx, "push")

    for n in range(2):
        arrived(sides[n][0], zone.at[34 * n : 34 * n + 2], 30 + n)

        @pl.when(jnp.logical_not(sides[n][0]))
        def _():
            edge = zone[2 + 31 * n]
            zone[34 * n] = edge
            zone[34 * n + 1] = edge

    for place, row in enumerate((0, 1, 14, 15)):
        zone_send[place] = jnp.zeros((PX, NZ), jnp.int32)
        zone_send[place, 0:LX] = zone[:, row]
    for n in range(2):
        push(*sides[2 + n], zone_send.at[2 * n : 2 * n + 2], zone_recv.at[1 - n], 32 + n, 33 - n)
    x_messages(3, u1, p1, set1, 10, late, late_here, late_gx, "pushed")
    y_messages(3, p1, set1, 10, "push")
    for layer in (0, 1, 34, 35):
        k0, k1, c0, c1, share = lookup(zone[layer], table)
        k_own[layer, 8:24] = k0
        k_own[LX + layer, 8:24] = k1
        c_own[0, layer] = c0
        c_own[1, layer] = c1
        cross[layer] = share * jnp.sqrt(c0 * c1)
    for n in range(2):
        arrived(y_here[n], zone_recv.at[n], 32 + n)

        @pl.when(jnp.logical_not(y_here[n]))
        def _():
            edge = zone_send[3 * n]
            zone_recv[n, 0] = edge
            zone_recv[n, 1] = edge

    for place in range(6):
        packed_zone = (
            zone_recv[0, place] if place < 2
            else zone_send[0] if place == 2
            else zone_send[3] if place == 3
            else zone_recv[1, place - 4]
        )
        k0, k1, c0, c1, share = lookup(packed_zone, table)
        k_pk[place, 0] = k0
        k_pk[place, 1] = k1
        if place in (1, 4):
            side = 0 if place == 1 else 1
            c_pk[side, 0] = c0
            c_pk[side, 1] = c1
            cross_pk[side] = share * jnp.sqrt(c0 * c1)
            for field, value in enumerate((k0, k1)):
                k_own[LX * field : LX * (field + 1), 7 if side == 0 else 24] = value[:LX]

    lanes = lax.broadcasted_iota(jnp.int32, (BY, NZ), 1)
    first_lane, last_lane = lanes == 0, lanes == NZ - 1
    for field in range(2):
        fx[field, 0] = 0.5 * (k_own[LX * field, 8:24] + k_own[LX * field + 1, 8:24])

    def faces(layer, carry):
        for field in range(2):
            spot = LX * field + layer
            center = k_own[spot, 8:24]
            x_low = fx[field, layer - 1]
            x_high = 0.5 * (center + k_own[spot + 1, 8:24])
            fx[field, layer] = x_high
            y_low = 0.5 * (center + k_own[spot, 7:23])
            y_high = 0.5 * (center + k_own[spot, 9:25])
            z_low = 0.5 * (center + jnp.where(first_lane, center, pltpu.roll(center, 1, axis=1)))
            z_high = 0.5 * (center + jnp.where(last_lane, center, pltpu.roll(center, NZ - 1, axis=1)))
            fym[field, layer] = y_low
            fyp[field, layer] = y_high
            fzm[field, layer] = jnp.where(first_lane, 0.0, z_low)
            fzp[field, layer] = jnp.where(last_lane, 0.0, z_high)
            diag[field, layer] = c_own[field, layer] + (
                (x_low + x_high) + (y_low + y_high) + (z_low + z_high)
            )
        return carry

    lax.fori_loop(1, 35, faces, 0, unroll=2)

    lanes_pk = lax.broadcasted_iota(jnp.int32, (PX, NZ), 1)
    first_pk, last_pk = lanes_pk == 0, lanes_pk == NZ - 1

    def rim_faces(side, field):
        center = k_pk[1 + 3 * side, field]
        x_low = 0.5 * (center + pltpu.roll(center, 1, axis=0))
        x_high = 0.5 * (center + pltpu.roll(center, PX - 1, axis=0))
        y_low = 0.5 * (center + k_pk[3 * side, field])
        y_high = 0.5 * (center + k_pk[3 * side + 2, field])
        z_low = 0.5 * (center + jnp.where(first_pk, center, pltpu.roll(center, 1, axis=1)))
        z_high = 0.5 * (center + jnp.where(last_pk, center, pltpu.roll(center, NZ - 1, axis=1)))
        return x_low, x_high, y_low, y_high, z_low, z_high

    def assemble_near(width, own, packed, bufs, total_v, total_pk, margin):
        x_layers, x_corner, _, y_rows, corners, _ = bufs
        low0 = 3 - width
        for field in range(2):
            base = LX * field

            def copy_layer(layer, carry):
                total_v[base + layer, 8:24] = own[field, layer]
                return carry

            lax.fori_loop(3, 33, copy_layer, 0, unroll=6)
            for side, present in ((near, near_here), (late, late_here)):
                for step in range(width):
                    layer = low0 + (33 - low0) * side + step
                    value = own[field, layer]
                    if side is near:
                        value = value + x_layers[near, field, step]
                    beyond = jnp.logical_or(layer < 2, layer > 33)
                    drop = jnp.logical_and(beyond, jnp.logical_not(present))
                    total_v[base + layer, 8:24] = jnp.where(drop, 0.0, value)
        low_x = jnp.logical_and(rows_pk < 2, jnp.logical_not(has["xm"]))
        high_x = jnp.logical_and(rows_pk > 33, jnp.logical_not(has["xp"]))
        beyond_x = jnp.logical_or(low_x, high_x)
        for n in range(2):
            for step in range(width):
                y = 1 - width + step if n == 0 else 15 + step
                place = y + 2 if n == 0 else y - 12
                total_pk[place] = y_rows[n, step]
                total_pk[place, :, tile(near)] += corners[2 * near + n, step]
                if y == -1 or y == 16:
                    total_pk[place] += packed[5 * n]
                    total_pk[place, :, tile(near)] += x_corner[near, n]
                drop = beyond_x
                if y < 0 or y > 15:
                    drop = jnp.logical_or(drop, jnp.logical_not(y_here[n]))
                for field in range(2):
                    total_pk[place, field] = jnp.where(drop, 0.0, total_pk[place, field])
        for field in range(2):
            lo = 2 - margin
            count = BX + 2 * margin
            window = slice(LX * field + lo, LX * field + lo + count)
            for place, outer, row, halo in ((2, 1, 8, 7), (3, 4, 23, 24)):
                edge = total_v[window, row] + total_pk[place, field, lo : lo + count]
                total_v[window, row] = edge
                total_pk[place, field, lo : lo + count] = edge
                total_v[window, halo] = total_pk[outer, field, lo : lo + count]

    def assemble_late(width, bufs, total_v, total_pk):
        x_layers, x_corner, _, _, corners, _ = bufs
        low0 = 3 - width
        for field in range(2):
            for step in range(width):
                spot = LX * field + low0 + (33 - low0) * late + step
                total_v[spot, 8:24] += x_layers[late, field, step]
            block = pl.ds(LX * field + 32 * late, 4)
            for n, edge_place, outer, row, halo in ((0, 2, 1, 8, 7), (1, 3, 4, 23, 24)):
                for step in range(width):
                    y = 1 - width + step if n == 0 else 15 + step
                    place = y + 2 if n == 0 else y - 12
                    piece = corners[2 * late + n, step, field]
                    if y == -1 or y == 16:
                        piece = piece + jnp.where(y_here[n], x_corner[late, n, field], 0.0)
                    if place == edge_place:
                        edge = total_v[block, row] + piece
                        total_v[block, row] = edge
                        total_pk[place, field, tile(late)] = edge
                    else:
                        total_pk[place, field, tile(late)] += piece
                total_v[block, halo] = total_pk[outer, field, tile(late)]

    def operate(vec, layer, field):
        spot = LX * field + layer
        center = vec[spot, 8:24]
        value = diag[field, layer] * center + cross[layer] * vec[LX * (1 - field) + layer, 8:24]
        value = value - fx[field, layer - 1] * vec[spot - 1, 8:24] - fx[field, layer] * vec[spot + 1, 8:24]
        value = value - fym[field, layer] * vec[spot, 7:23] - fyp[field, layer] * vec[spot, 9:25]
        value = value - fzm[field, layer] * pltpu.roll(center, 1, axis=1)
        return value - fzp[field, layer] * pltpu.roll(center, NZ - 1, axis=1), center

    def fold(value):
        return value[:8] + value[8:]

    def first_image(layer, carry):
        rz, pq = carry
        for field in range(2):
            value, center = operate(v1, layer, field)
            q_own[field, layer] = value
            rz = rz + fold(r_own[field, layer] * center)
            pq = pq + fold(center * value)
        return rz, pq

    def rim_layer(side, present):
        layer = 1 + 33 * side
        for field in range(2):
            value, _ = operate(v1, layer, field)
            q_own[field, layer] = jnp.where(present, value, 0.0)

    def rim_rows():
        for side in range(2):
            place = 1 + 3 * side
            low_x = jnp.logical_and(rows_pk < 2, jnp.logical_not(has["xm"]))
            high_x = jnp.logical_and(rows_pk > 33, jnp.logical_not(has["xp"]))
            drop = jnp.logical_or(jnp.logical_or(low_x, high_x), jnp.logical_not(y_here[side]))
            drop = jnp.logical_or(drop, jnp.logical_or(rows_pk < 1, rows_pk > 34))
            for field in range(2):
                x_low, x_high, y_low, y_high, z_low, z_high = rim_faces(side, field)
                center = zp[place, field]
                value = c_pk[side, field] + ((x_low + x_high) + (y_low + y_high) + (z_low + z_high))
                value = value * center + cross_pk[side] * zp[place, 1 - field]
                value = value - x_low * pltpu.roll(center, 1, axis=0) - x_high * pltpu.roll(center, PX - 1, axis=0)
                value = value - y_low * zp[3 * side, field] - y_high * zp[3 * side + 2, field]
                value = value - jnp.where(first_pk, 0.0, z_low) * pltpu.roll(center, 1, axis=1)
                value = value - jnp.where(last_pk, 0.0, z_high) * pltpu.roll(center, NZ - 1, axis=1)
                q_pk[side, field] = jnp.where(drop, 0.0, value)

    def inner_layers(step, carry, image):
        return image(4 - 2 * late + step, carry)

    x_messages(3, u1, p1, set1, 10, near, near_here, near_gx, "arrived")
    y_messages(3, p1, set1, 10, "arrived")
    assemble_near(3, u1, p1, set1, v1, zp, 2)
    sums = lax.fori_loop(0, 30, functools.partial(inner_layers, image=first_image), (zero, zero), unroll=3)
    rim_layer(near, near_here)
    rim_rows()
    apply_box(q_own, q_pk, u2, p2, near)
    x_messages(2, u2, p2, set2, 20, near, near_here, near_gx, "push")
    x_messages(3, u1, p1, set1, 10, late, late_here, late_gx, "arrived")
    assemble_late(3, set1, v1, zp)
    for step in range(2):
        sums = first_image(2 + 30 * late + step, sums)
    rz, pq = sums
    rim_layer(late, late_here)
    rim_rows()
    apply_box(q_own, q_pk, u2, p2, late)
    x_messages(2, u2, p2, set2, 20, late, late_here, late_gx, "push")
    x_messages(2, u2, p2, set2, 20, late, late_here, late_gx, "pushed")
    y_messages(2, p2, set2, 20, "push")

    def second_image(layer, carry):
        rw, qw, zu, wu = carry
        for field in range(2):
            value, center = operate(v2, layer, field)
            u_vec[field, layer] = value
            rw = rw + fold(r_own[field, layer] * center)
            qw = qw + fold(q_own[field, layer] * center)
            zu = zu + fold(v1[LX * field + layer, 8:24] * value)
            wu = wu + fold(center * value)
        return rw, qw, zu, wu

    x_messages(2, u2, p2, set2, 20, near, near_here, near_gx, "arrived")
    y_messages(2, p2, set2, 20, "arrived")
    assemble_near(2, u2, p2, set2, v2, wp, 1)
    sums = lax.fori_loop(0, 30, functools.partial(inner_layers, image=second_image), (zero,) * 4, unroll=3)
    for n in range(2):
        pushed(sides[n][0], r_own.at[:, 2 + 31 * n], n)
        pushed(sides[n][0], zone.at[2 + 30 * n : 4 + 30 * n], 30 + n)
        pushed(y_here[n], r_send.at[n], 2 + n)
        pushed(y_here[n], zone_send.at[2 * n : 2 * n + 2], 32 + n)
    for c in range(4):
        pushed(sides[4 + c][0], r_corner_send.at[c], 4 + c)
    x_messages(3, u1, p1, set1, 10, near, near_here, near_gx, "pushed")
    y_messages(3, p1, set1, 10, "pushed")
    x_messages(2, u2, p2, set2, 20, near, near_here, near_gx, "pushed")
    y_messages(2, p2, set2, 20, "pushed")
    x_messages(2, u2, p2, set2, 20, late, late_here, late_gx, "arrived")
    assemble_late(2, set2, v2, wp)
    for step in range(2):
        sums = second_image(2 + 30 * late + step, sums)
    rw, qw, zu, wu = sums

    spot = lax.broadcasted_iota(jnp.int32, (1, NZ), 1)
    row = jnp.zeros((1, NZ), F32)
    for place, value in enumerate((rz, pq, rw, qw, zu, wu)):
        row = jnp.where(spot == place, jnp.sum(value), row)
    ar1[0] = row

    def all_reduce(slots, count, device_of, number):
        def send(k, carry):
            pltpu.make_async_remote_copy(
                src_ref=slots.at[0],
                dst_ref=slots.at[k],
                send_sem=ar_send.at[number],
                recv_sem=ar_recv.at[number],
                device_id=device_of(k),
                device_id_type=MESH,
            ).start()
            return carry

        for k in range(1, count):
            send(k, 0)
        others = slots.at[1:count]
        pltpu.make_async_copy(others, others, ar_recv.at[number]).wait()
        pltpu.make_async_copy(others, others, ar_send.at[number]).wait()
        return jnp.sum(slots[...], axis=0)

    ar2[0] = all_reduce(ar1, plane, plane_id, 0)
    products = all_reduce(ar2, depth, depth_id, 1)
    rz, pq, rw, qw, zu, wu = (
        jnp.sum(jnp.where(spot == n, products, 0.0), axis=1, keepdims=True) for n in range(6)
    )
    alpha = rz / pq
    rz2 = rz - alpha * (rw + pq) + alpha * alpha * qw
    grow = 1.0 + rz2 / rz
    curve = grow * grow * pq - grow * alpha * (zu + qw) + alpha * alpha * wu
    alpha2 = rz2 / curve
    by_z = jnp.broadcast_to(alpha + alpha2 * grow, (BY, NZ))
    by_w = jnp.broadcast_to(alpha2 * alpha, (BY, NZ))

    def finish(layer, carry):
        for field in range(2):
            spot = LX * field + layer
            x_out[field, layer - 2] = by_z * v1[spot, 8:24] - by_w * v2[spot, 8:24]
            r_out[field, layer - 2] = (
                r_own[field, layer] - by_z * q_own[field, layer] + by_w * u_vec[field, layer]
            )
        return carry

    lax.fori_loop(2, 34, finish, 0, unroll=4)


def shards(nx, ny, load, zones, conductance, capacity, coupling):
    to_modes, from_modes, z_forward, z_inverse, summed, group = constants()
    ax, ay = min(8, nx // 2), min(4, ny // 2)
    plane, depth = ax * ay, (nx // ax) * (ny // ay)
    vmem = lambda *shape, dtype=F32: pltpu.VMEM(shape, dtype)
    scratch = [
        pltpu.SMEM((2, ZONES), F32), pltpu.SMEM((2, ZONES), F32), pltpu.SMEM((ZONES,), F32),
        vmem(*to_modes.shape, dtype=BF16), vmem(*from_modes.shape, dtype=BF16),
        vmem(*z_forward.shape, dtype=BF16), vmem(*z_inverse.shape, dtype=BF16),
        vmem(*summed.shape), vmem(*group.shape, dtype=BF16),
        vmem(2, LX, BY, NZ), vmem(2, 2, PX, NZ),
        vmem(LX, BY, NZ, dtype=jnp.int32), vmem(8, NZ, dtype=jnp.int32),
        vmem(4, PX, NZ, dtype=jnp.int32), vmem(2, 2, PX, NZ, dtype=jnp.int32),
        vmem(2, 2, BX, NZ), vmem(2, 2, BX, NZ), vmem(4, 2, NZ), vmem(4, 2, NZ),
        vmem(2 * LX, 32, NZ), vmem(6, 2, PX, NZ), vmem(2, LX, BY, NZ), vmem(2, 2, PX, NZ),
        vmem(LX, BY, NZ), vmem(2, PX, NZ),
        vmem(2, LX, BY, NZ), vmem(2, LX, BY, NZ), vmem(2, LX, BY, NZ), vmem(2, LX, BY, NZ),
        vmem(2, LX, BY, NZ), vmem(2, LX, BY, NZ), vmem(8, NZ), vmem(4, MODES, 256),
        vmem(2, LX, BY, NZ), vmem(6, 2, PX, NZ), vmem(2 * LX, 32, NZ), vmem(6, 2, PX, NZ),
        vmem(2, LX, BY, NZ), vmem(2, 2, PX, NZ),
        vmem(2, LX, BY, NZ), vmem(6, 2, PX, NZ), vmem(2 * LX, 32, NZ), vmem(6, 2, PX, NZ),
        vmem(2, LX, BY, NZ),
    ]
    for width in (3, 2):
        scratch += [
            vmem(2, 2, width, BY, NZ), vmem(2, 2, 2, 4, NZ), vmem(2, 2, 2, 4, NZ),
            vmem(2, width, 2, PX, NZ), vmem(4, width, 2, 4, NZ), vmem(4, width, 2, 4, NZ),
        ]
    scratch += [
        vmem(plane, 1, NZ), vmem(depth, 1, NZ),
        pltpu.SemaphoreType.DMA((12,)), pltpu.SemaphoreType.DMA((34,)), pltpu.SemaphoreType.DMA((34,)),
        pltpu.SemaphoreType.DMA((2,)), pltpu.SemaphoreType.DMA((2,)),
    ]
    any_spec = pl.BlockSpec(memory_space=pltpu.HBM)
    out = pl.BlockSpec(memory_space=pltpu.VMEM)
    shape = jax.ShapeDtypeStruct((2, BX, BY, NZ), F32)
    return pl.pallas_call(
        functools.partial(body, nx, ny),
        out_shape=(shape, shape),
        in_specs=[any_spec] * 11,
        out_specs=(out, out),
        scratch_shapes=scratch,
        compiler_params=pltpu.CompilerParams(
            collective_id=0, has_side_effects=True, vmem_limit_bytes=48 * 1024 * 1024
        ),
        name="pcg",
    )(
        *(pltpu.with_memory_space_constraint(a, pltpu.HBM) for a in (load, zones, conductance, capacity, coupling)),
        *(pltpu.with_memory_space_constraint(jnp.asarray(c), pltpu.HBM) for c in (to_modes, from_modes, z_forward, z_inverse, summed, group)),
    )


def solution(mesh):
    in_specs = (P(None, "gx", "gy", None), P("gx", "gy", None), P(), P(), P())
    out_specs = (P(None, "gx", "gy", None), P(None, "gx", "gy", None))
    run = functools.partial(shards, mesh.shape["gx"], mesh.shape["gy"])
    return jax.shard_map(run, mesh=mesh, in_specs=in_specs, out_specs=out_specs, check_vma=False)
```

```python
import functools

import jax
import jax.numpy as jnp
import numpy as np
from jax import lax
from jax.experimental import pallas as pl
from jax.experimental.pallas import tpu as pltpu
from jax.sharding import PartitionSpec as P

BOX = 16
SPAN = BOX + 2
BX = 32
BY = 16
NZ = 128
ZONES = 8
LX = BX + 4
PX = 40
MODES = 336
OWN = SPAN * BY
KIN = OWN + 48
MOUT = OWN + 144
F32 = jnp.float32
BF16 = jnp.bfloat16
MESH = pl.DeviceIdType.MESH


def split3(matrix):
    high = np.asarray(matrix, np.float32).astype(jnp.bfloat16)
    low = (np.asarray(matrix, np.float32) - high.astype(np.float32)).astype(jnp.bfloat16)
    return high, low


def constants():
    index = np.arange(SPAN)
    basis = np.sqrt(2.0 / (SPAN + 1)) * np.sin(np.pi * np.outer(index + 1, index + 1) / (SPAN + 1))
    lam = 4.0 * np.sin(np.pi * (index + 1) / (2.0 * (SPAN + 1))) ** 2
    forward = np.zeros((SPAN, SPAN, KIN))
    inner = np.einsum("ix,jy->ijxy", basis, basis[:, 1:17])
    forward[:, :, :OWN] = inner.reshape(SPAN, SPAN, OWN)
    for side, row in ((0, 0), (1, 17)):
        start = OWN + 24 * side + 1
        forward[:, :, start : start + SPAN] = np.einsum("ix,j->ijx", basis, basis[:, row])
    full = np.zeros((MODES, KIN))
    full[: SPAN * SPAN] = forward.reshape(SPAN * SPAN, KIN)
    high, low = split3(full)
    to_modes = np.concatenate([high, high, low], axis=1)
    inverse = np.zeros((MOUT, SPAN, SPAN))
    inverse[:OWN] = np.einsum("xi,yj->xyij", basis, basis[1:17]).reshape(OWN, SPAN, SPAN)
    for place, row in enumerate((0, 1, 2, 15, 16, 17)):
        start = OWN + 24 * place + 1
        inverse[start : start + SPAN] = np.einsum("xi,j->xij", basis, basis[row])
    full = np.zeros((MOUT, MODES))
    full[:, : SPAN * SPAN] = inverse.reshape(MOUT, SPAN * SPAN)
    high, low = split3(full)
    from_modes = np.concatenate([high, high, low], axis=1)
    boxes = NZ // BOX
    count = boxes * SPAN
    banded = np.zeros((NZ, count))
    for box in range(boxes):
        for offset in range(SPAN):
            cell = BOX * box + offset - 1
            if 0 <= cell < NZ:
                banded[cell, box * SPAN : (box + 1) * SPAN] = basis[:, offset]
    rest = count - 128
    lanes = np.concatenate([np.arange(128)] + [128 + np.arange(rest)] * 3)
    wide = np.zeros((NZ, 256))
    wide[:, : lanes.size] = banded[:, lanes]
    high, low = split3(wide)
    z_forward = np.concatenate([high, high, low], axis=0)
    high, low = split3(banded.T)
    tail = np.zeros((128, NZ), jnp.bfloat16)
    tail[:rest] = high[128:]
    tail[rest : 2 * rest] = high[128:]
    tail[2 * rest : 3 * rest] = low[128:]
    z_inverse = np.concatenate([high[:128], high[:128], low[:128], tail], axis=0)
    summed = np.zeros((MODES, 256), np.float32)
    plane = (lam[:, None] + lam[None, :]).reshape(-1)
    summed[: SPAN * SPAN, : lanes.size] = plane[:, None] + lam[lanes % SPAN][None, :]
    group = np.zeros((NZ, 256))
    group[:, : lanes.size] = (np.arange(NZ)[:, None] // BOX) == (lanes // SPAN)[None, :]
    group = np.concatenate([group] * 3, axis=0).astype(jnp.bfloat16)
    return to_modes, from_modes, z_forward, z_inverse, summed, group


def lookup(zone, table):
    bit0 = (zone & 1) != 0
    bit1 = (zone & 2) != 0
    bit2 = (zone & 4) != 0

    def pick(values):
        a = jnp.where(bit0, values[1], values[0])
        b = jnp.where(bit0, values[3], values[2])
        c = jnp.where(bit0, values[5], values[4])
        d = jnp.where(bit0, values[7], values[6])
        return jnp.where(bit2, jnp.where(bit1, d, c), jnp.where(bit1, b, a))

    return [pick(values) for values in table]


def halves(value):
    high = value.astype(BF16)
    low = (value - high.astype(F32)).astype(BF16)
    return high, low


def dot(a, b):
    return jnp.dot(a, b, preferred_element_type=F32)


def body(
    nx, ny,
    load_ref, zones_ref, cond_hbm, cap_hbm, coup_hbm,
    tf_hbm, ti_hbm, zf_hbm, zi_hbm, lam_hbm, group_hbm,
    z_out, w_out, q_out, u_out, by_z_out, by_w_out,
    cond_ref, cap_ref, coup_ref, tf, ti, zf, zi, lam, group,
    r_own, r_pk, zone, zone_pk, zone_send, zone_recv,
    r_send, r_recv, r_corner_send, r_corner,
    k_own, k_pk, c_own, c_pk, cross, cross_pk,
    fx, fym, fyp, fzm, fzp, diag, diag_pk, dinv,
    u1, p1, v1, zp, q_own, q_pk, u2, p2, v2, wp,
    xl1, xc1, xcs1, yr1, dg1, dgs1, xl2, xc2, xcs2, yr2, dg2, dgs2,
    ar1, ar2,
    local_sem, send_sem, recv_sem, ar_send, ar_recv,
):
    gx = lax.axis_index("gx")
    gy = lax.axis_index("gy")
    has = {"xm": gx > 0, "xp": gx < nx - 1, "ym": gy > 0, "yp": gy < ny - 1}
    ax, ay = min(8, nx // 2), min(4, ny // 2)
    plane, depth = ax * ay, (nx // ax) * (ny // ay)
    div, rem = lax.div, lax.rem
    across, along = nx // ax, ny // ay
    gx_block, gx_in = div(gx, jnp.int32(ax)), rem(gx, jnp.int32(ax))
    gy_block, gy_in = div(gy, jnp.int32(ay)), rem(gy, jnp.int32(ay))
    here = gx_in * ay + gy_in
    level = gx_block * along + gy_block

    def plane_id(k):
        t = rem(here + k, jnp.int32(plane))
        return (gx_block * ax + div(t, jnp.int32(ay)), gy_block * ay + rem(t, jnp.int32(ay)))

    def depth_id(k):
        t = rem(level + k, jnp.int32(depth))
        return (div(t, jnp.int32(along)) * ax + gx_in, rem(t, jnp.int32(along)) * ay + gy_in)

    late = jnp.where(gx_in == 0, 0, 1).astype(jnp.int32)
    near = 1 - late
    near_gx, late_gx = gx + 1 - 2 * late, gx - 1 + 2 * late
    near_here = jnp.logical_and(near_gx >= 0, near_gx < nx)
    late_here = jnp.logical_and(late_gx >= 0, late_gx < nx)
    y_here = (has["ym"], has["yp"])
    sides = [(has["xm"], (gx - 1, gy)), (has["xp"], (gx + 1, gy)), (has["ym"], (gx, gy - 1)), (has["yp"], (gx, gy + 1))]
    for c in range(4):
        present = jnp.logical_and(sides[c // 2][0], y_here[c % 2])
        sides.append((present, (gx - 1 + 2 * (c // 2), gy - 1 + 2 * (c % 2))))

    loads = [
        pltpu.make_async_copy(load_ref.at[0], r_own.at[0, 2:34], local_sem.at[0]),
        pltpu.make_async_copy(load_ref.at[1], r_own.at[1, 2:34], local_sem.at[1]),
        pltpu.make_async_copy(zones_ref, zone.at[2:34], local_sem.at[2]),
        pltpu.make_async_copy(cond_hbm, cond_ref, local_sem.at[9]),
        pltpu.make_async_copy(cap_hbm, cap_ref, local_sem.at[10]),
        pltpu.make_async_copy(coup_hbm, coup_ref, local_sem.at[11]),
    ]
    weights = [
        pltpu.make_async_copy(source, target, local_sem.at[3 + n])
        for n, (source, target) in enumerate(
            ((tf_hbm, tf), (zf_hbm, zf), (group_hbm, group), (lam_hbm, lam), (zi_hbm, zi), (ti_hbm, ti))
        )
    ]
    barrier = pltpu.get_barrier_semaphore()
    for present, device in sides:

        @pl.when(present)
        def _():
            pl.semaphore_signal(barrier, inc=1, device_id=device, device_id_type=MESH)

    def greet_plane(k, carry):
        pl.semaphore_signal(barrier, inc=1, device_id=plane_id(k), device_id_type=MESH)
        return carry

    def greet_depth(k, carry):
        pl.semaphore_signal(barrier, inc=1, device_id=depth_id(k), device_id_type=MESH)
        return carry

    lax.fori_loop(1, depth, greet_depth, 0)
    for copy in loads + weights:
        copy.start()
    lax.fori_loop(1, plane, greet_plane, 0)

    def clear(*refs):
        for ref in refs:
            ref[...] = jnp.zeros(ref.shape, ref.dtype)

    clear(r_pk, u1, p1, u2, p2)
    for side, name in enumerate(("xm", "xp")):

        @pl.when(jnp.logical_not(has[name]))
        def _():
            clear(r_own.at[0, 1 + 33 * side], r_own.at[1, 1 + 33 * side])
            clear(xl1.at[side], xc1.at[side], xl2.at[side], xc2.at[side])

    for side, name in enumerate(("ym", "yp")):

        @pl.when(jnp.logical_not(has[name]))
        def _():
            clear(r_recv.at[side], yr1.at[side], yr2.at[side])

    for corner in range(4):

        @pl.when(jnp.logical_not(sides[4 + corner][0]))
        def _():
            clear(r_corner.at[corner], dg1.at[corner], dg2.at[corner])

    for copy in loads:
        copy.wait()

    for field in range(2):
        r_send[0, field] = r_own[field, 2:34, 0]
        r_send[1, field] = r_own[field, 2:34, BY - 1]
    for corner, (layer, row) in enumerate(((2, 0), (2, 15), (33, 0), (33, 15))):
        for field in range(2):
            r_corner_send[corner, field : field + 1] = r_own[field, layer, row : row + 1]

    members = jnp.int32(plane - 1 + depth - 1)
    for present, _ in sides:
        members = members + present.astype(jnp.int32)
    pl.semaphore_wait(barrier, members)

    def push(present, device, source, target, out_slot, in_slot):
        @pl.when(present)
        def _():
            pltpu.make_async_remote_copy(
                src_ref=source,
                dst_ref=target,
                send_sem=send_sem.at[out_slot],
                recv_sem=recv_sem.at[in_slot],
                device_id=device,
                device_id_type=MESH,
            ).start()

    def pushed(present, source, slot):
        @pl.when(present)
        def _():
            pltpu.make_async_copy(source, source, send_sem.at[slot]).wait()

    def arrived(present, target, slot):
        @pl.when(present)
        def _():
            pltpu.make_async_copy(target, target, recv_sem.at[slot]).wait()

    for n in range(2):
        push(*sides[n], r_own.at[:, 2 + 31 * n], r_own.at[:, 34 - 33 * n], n, 1 - n)
    for c in range(4):
        push(*sides[4 + c], r_corner_send.at[c], r_corner.at[3 - c], 4 + c, 7 - c)
    for n in range(2):
        push(*sides[2 + n], r_send.at[n], r_recv.at[1 - n], 2 + n, 3 - n)
    for n in range(2):
        push(*sides[n], zone.at[2 + 30 * n : 4 + 30 * n], zone.at[34 - 34 * n : 36 - 34 * n], 30 + n, 31 - n)

    table = [[ref[f, q] for q in range(ZONES)] for ref in (cond_ref, cap_ref) for f in range(2)]
    table.append([coup_ref[q] for q in range(ZONES)])

    def own_coefficients(layer, sums):
        k0, k1, c0, c1, share = lookup(zone[layer], table)
        k_own[layer, 8:24] = k0
        k_own[LX + layer, 8:24] = k1
        c_own[0, layer] = c0
        c_own[1, layer] = c1
        cross[layer] = share * jnp.sqrt(c0 * c1)
        return tuple(s + v[:8] + v[8:] for s, v in zip(sums, (c0, c1, k0, k1)))

    zero = jnp.zeros((8, NZ), F32)
    pieces = []
    for box in range(2):
        sums = lax.fori_loop(2 + BOX * box, 2 + BOX * (box + 1), own_coefficients, (zero,) * 4)
        pieces.extend(jnp.sum(s, axis=0, keepdims=True) for s in sums)
    total = jnp.concatenate(pieces, axis=0)
    part0 = total.astype(BF16)
    rest = total - part0.astype(F32)
    part1 = rest.astype(BF16)
    part2 = (rest - part1.astype(F32)).astype(BF16)
    for copy in weights:
        copy.wait()
    means = dot(jnp.concatenate([part0, part1, part2], axis=1), group[...]) * (1.0 / BOX**3)
    lane = lax.broadcasted_iota(jnp.int32, (1, 256), 1)
    unused = jnp.where(lane >= 128 + 48, 1.0, 0.0)
    for box in range(2):
        for field in range(2):
            cbar = means[4 * box + field : 4 * box + field + 1] + unused
            kbar = means[4 * box + 2 + field : 4 * box + 3 + field]
            dinv[box, MODES * field : MODES * (field + 1)] = 1.0 / (cbar + kbar * lam[...])

    lane_tail = lax.broadcasted_iota(jnp.int32, (1, 128), 1)
    low_lanes = jnp.logical_and(lane_tail >= 16, lane_tail < 32)

    def apply_box(own, packed, out, out_pk, box):
        layers = pl.ds(1 + BOX * box, SPAN)
        spots = pl.ds(pl.multiple_of(BOX * box, 8), 24)
        columns = []
        for field in range(2):
            inner = own[field, layers].reshape(OWN, NZ)
            columns.append(jnp.concatenate([inner] + [packed[side, field, spots] for side in range(2)], axis=0))
        high, low = halves(jnp.concatenate(columns, axis=1))
        modes = dot(tf[...], jnp.concatenate([high, low, high], axis=0))
        high, low = halves(jnp.concatenate([modes[:, :NZ], modes[:, NZ:]], axis=0))
        deep = dot(jnp.concatenate([high, low, high], axis=1), zf[...]) * dinv[box]
        high, low = halves(deep[:, :128])
        tail = deep[:, 128:]
        tail_high = tail.astype(BF16).astype(F32)
        tail = jnp.where(low_lanes, tail - tail_high, tail_high).astype(BF16)
        lines = dot(jnp.concatenate([high, low, high, tail], axis=1), zi[...])
        columns = [lines[:MODES], lines[MODES:]]
        high, low = halves(jnp.concatenate(columns, axis=1))
        cells = dot(ti[...], jnp.concatenate([high, low, high], axis=0))
        for field in range(2):
            mine = cells[:, NZ * field : NZ * (field + 1)]
            out[field, layers] += mine[:OWN].reshape(SPAN, BY, NZ)
            out_pk[:, field, spots] += mine[OWN:].reshape(6, 24, NZ)

    def tile(side):
        return pl.ds(pl.multiple_of(32 * side, 8), 4)

    def x_messages(width, own, packed, bufs, base, side, present, side_gx, act):
        x_layers, x_corner, x_corner_send, y_rows, corners, corners_send = bufs
        layers = pl.ds(1 + (34 - width) * side, width)
        device = (side_gx, gy)
        if act == "push":
            for place, row in enumerate((0, 5)):
                x_corner_send[side, place] = packed[row, :, tile(side)]
            push(present, device, own.at[:, layers], x_layers.at[1 - side], base + side, base + 1 - side)
            push(present, device, x_corner_send.at[side], x_corner.at[1 - side], base + 8 + side, base + 9 - side)
        elif act == "pushed":
            pushed(present, own.at[:, layers], base + side)
            pushed(present, x_corner_send.at[side], base + 8 + side)
        else:
            arrived(present, x_layers.at[side], base + side)
            arrived(present, x_corner.at[side], base + 8 + side)
        for n in range(2):
            c = 2 * side + n
            both = jnp.logical_and(present, y_here[n])
            if act == "push":
                for place in range(width):
                    corners_send[c, place] = packed[(6 - width) * n + place, :, tile(side)]
                device = (side_gx, gy - 1 + 2 * n)
                push(both, device, corners_send.at[c], corners.at[3 - c], base + 4 + c, base + 7 - c)
            elif act == "pushed":
                pushed(both, corners_send.at[c], base + 4 + c)
            else:
                arrived(both, corners.at[c], base + 4 + c)

    def y_messages(width, packed, bufs, base, act):
        y_rows = bufs[3]
        for n in range(2):
            rows = packed.at[(6 - width) * n : (6 - width) * n + width]
            if act == "push":
                push(*sides[2 + n], rows, y_rows.at[1 - n], base + 2 + n, base + 3 - n)
            elif act == "pushed":
                pushed(y_here[n], rows, base + 2 + n)
            else:
                arrived(y_here[n], y_rows.at[n], base + 2 + n)

    rows_pk = lax.broadcasted_iota(jnp.int32, (PX, NZ), 0)

    def corner_rows(side):
        for n in range(2):
            for field in range(2):
                row = r_corner[2 * side + n, field : field + 1]
                r_pk[n, field] = jnp.where(rows_pk == 1 + 33 * side, row, r_pk[n, field])

    for n in range(2):
        arrived(y_here[n], r_recv.at[n], 2 + n)
        for field in range(2):
            r_pk[n, field, 2:34] = r_recv[n, field]
        arrived(jnp.logical_and(near_here, y_here[n]), r_corner.at[2 * near + n], 4 + 2 * near + n)
    arrived(near_here, r_own.at[:, 1 + 33 * near], near)
    corner_rows(near)
    set1 = (xl1, xc1, xcs1, yr1, dg1, dgs1)
    set2 = (xl2, xc2, xcs2, yr2, dg2, dgs2)
    apply_box(r_own, r_pk, u1, p1, near)
    x_messages(3, u1, p1, set1, 10, near, near_here, near_gx, "push")
    for n in range(2):
        arrived(jnp.logical_and(late_here, y_here[n]), r_corner.at[2 * late + n], 4 + 2 * late + n)
    arrived(late_here, r_own.at[:, 1 + 33 * late], late)
    corner_rows(late)
    apply_box(r_own, r_pk, u1, p1, late)
    x_messages(3, u1, p1, set1, 10, late, late_here, late_gx, "push")

    for n in range(2):
        arrived(sides[n][0], zone.at[34 * n : 34 * n + 2], 30 + n)

        @pl.when(jnp.logical_not(sides[n][0]))
        def _():
            edge = zone[2 + 31 * n]
            zone[34 * n] = edge
            zone[34 * n + 1] = edge

    for place, row in enumerate((0, 1, 14, 15)):
        zone_send[place] = jnp.zeros((PX, NZ), jnp.int32)
        zone_send[place, 0:LX] = zone[:, row]
    for n in range(2):
        push(*sides[2 + n], zone_send.at[2 * n : 2 * n + 2], zone_recv.at[1 - n], 32 + n, 33 - n)
    y_messages(3, p1, set1, 10, "push")
    x_messages(3, u1, p1, set1, 10, late, late_here, late_gx, "pushed")
    for layer in (0, 1, 34, 35):
        k0, k1, c0, c1, share = lookup(zone[layer], table)
        k_own[layer, 8:24] = k0
        k_own[LX + layer, 8:24] = k1
        c_own[0, layer] = c0
        c_own[1, layer] = c1
        cross[layer] = share * jnp.sqrt(c0 * c1)
    for n in range(2):
        arrived(y_here[n], zone_recv.at[n], 32 + n)

        @pl.when(jnp.logical_not(y_here[n]))
        def _():
            edge = zone_send[3 * n]
            zone_recv[n, 0] = edge
            zone_recv[n, 1] = edge

    for place in range(6):
        packed_zone = (
            zone_recv[0, place] if place < 2
            else zone_send[0] if place == 2
            else zone_send[3] if place == 3
            else zone_recv[1, place - 4]
        )
        k0, k1, c0, c1, share = lookup(packed_zone, table)
        k_pk[place, 0] = k0
        k_pk[place, 1] = k1
        if place in (1, 4):
            side = 0 if place == 1 else 1
            c_pk[side, 0] = c0
            c_pk[side, 1] = c1
            cross_pk[side] = share * jnp.sqrt(c0 * c1)
            for field, value in enumerate((k0, k1)):
                k_own[LX * field : LX * (field + 1), 7 if side == 0 else 24] = value[:LX]

    lanes = lax.broadcasted_iota(jnp.int32, (BY, NZ), 1)
    first_lane, last_lane = lanes == 0, lanes == NZ - 1
    for field in range(2):
        fx[field, 0] = 0.5 * (k_own[LX * field, 8:24] + k_own[LX * field + 1, 8:24])

    def faces(layer, carry):
        for field in range(2):
            spot = LX * field + layer
            center = k_own[spot, 8:24]
            x_low = fx[field, layer - 1]
            x_high = 0.5 * (center + k_own[spot + 1, 8:24])
            fx[field, layer] = x_high
            y_low = 0.5 * (center + k_own[spot, 7:23])
            y_high = 0.5 * (center + k_own[spot, 9:25])
            z_low = 0.5 * (center + jnp.where(first_lane, center, pltpu.roll(center, 1, axis=1)))
            z_high = 0.5 * (center + jnp.where(last_lane, center, pltpu.roll(center, NZ - 1, axis=1)))
            fym[field, layer] = y_low
            fyp[field, layer] = y_high
            fzm[field, layer] = jnp.where(first_lane, 0.0, z_low)
            fzp[field, layer] = jnp.where(last_lane, 0.0, z_high)
            diag[field, layer] = c_own[field, layer] + (
                (x_low + x_high) + (y_low + y_high) + (z_low + z_high)
            )
        return carry

    lax.fori_loop(1, 35, faces, 0, unroll=2)

    lanes_pk = lax.broadcasted_iota(jnp.int32, (PX, NZ), 1)
    first_pk, last_pk = lanes_pk == 0, lanes_pk == NZ - 1

    def rim_faces(side, field):
        center = k_pk[1 + 3 * side, field]
        x_low = 0.5 * (center + pltpu.roll(center, 1, axis=0))
        x_high = 0.5 * (center + pltpu.roll(center, PX - 1, axis=0))
        y_low = 0.5 * (center + k_pk[3 * side, field])
        y_high = 0.5 * (center + k_pk[3 * side + 2, field])
        z_low = 0.5 * (center + jnp.where(first_pk, center, pltpu.roll(center, 1, axis=1)))
        z_high = 0.5 * (center + jnp.where(last_pk, center, pltpu.roll(center, NZ - 1, axis=1)))
        return x_low, x_high, y_low, y_high, z_low, z_high

    def assemble_near(width, own, packed, bufs, total_v, total_pk, margin):
        x_layers, x_corner, _, y_rows, corners, _ = bufs
        low0 = 3 - width
        for field in range(2):
            base = LX * field

            def copy_layer(layer, carry):
                total_v[base + layer, 8:24] = own[field, layer]
                return carry

            lax.fori_loop(3, 33, copy_layer, 0, unroll=6)
            for side, present in ((near, near_here), (late, late_here)):
                for step in range(width):
                    layer = low0 + (33 - low0) * side + step
                    value = own[field, layer]
                    if side is near:
                        value = value + x_layers[near, field, step]
                    beyond = jnp.logical_or(layer < 2, layer > 33)
                    drop = jnp.logical_and(beyond, jnp.logical_not(present))
                    total_v[base + layer, 8:24] = jnp.where(drop, 0.0, value)
        low_x = jnp.logical_and(rows_pk < 2, jnp.logical_not(has["xm"]))
        high_x = jnp.logical_and(rows_pk > 33, jnp.logical_not(has["xp"]))
        beyond_x = jnp.logical_or(low_x, high_x)
        for n in range(2):
            for step in range(width):
                y = 1 - width + step if n == 0 else 15 + step
                place = y + 2 if n == 0 else y - 12
                total_pk[place] = y_rows[n, step]
                total_pk[place, :, tile(near)] += corners[2 * near + n, step]
                if y == -1 or y == 16:
                    total_pk[place] += packed[5 * n]
                    total_pk[place, :, tile(near)] += x_corner[near, n]
                drop = beyond_x
                if y < 0 or y > 15:
                    drop = jnp.logical_or(drop, jnp.logical_not(y_here[n]))
                for field in range(2):
                    total_pk[place, field] = jnp.where(drop, 0.0, total_pk[place, field])
        for field in range(2):
            lo = 2 - margin
            count = BX + 2 * margin
            window = slice(LX * field + lo, LX * field + lo + count)
            for place, outer, row, halo in ((2, 1, 8, 7), (3, 4, 23, 24)):
                edge = total_v[window, row] + total_pk[place, field, lo : lo + count]
                total_v[window, row] = edge
                total_pk[place, field, lo : lo + count] = edge
                total_v[window, halo] = total_pk[outer, field, lo : lo + count]

    def assemble_late(width, bufs, total_v, total_pk):
        x_layers, x_corner, _, _, corners, _ = bufs
        low0 = 3 - width
        for field in range(2):
            for step in range(width):
                spot = LX * field + low0 + (33 - low0) * late + step
                total_v[spot, 8:24] += x_layers[late, field, step]
            block = pl.ds(LX * field + 32 * late, 4)
            for n, edge_place, outer, row, halo in ((0, 2, 1, 8, 7), (1, 3, 4, 23, 24)):
                for step in range(width):
                    y = 1 - width + step if n == 0 else 15 + step
                    place = y + 2 if n == 0 else y - 12
                    piece = corners[2 * late + n, step, field]
                    if y == -1 or y == 16:
                        piece = piece + jnp.where(y_here[n], x_corner[late, n, field], 0.0)
                    if place == edge_place:
                        edge = total_v[block, row] + piece
                        total_v[block, row] = edge
                        total_pk[place, field, tile(late)] = edge
                    else:
                        total_pk[place, field, tile(late)] += piece
                total_v[block, halo] = total_pk[outer, field, tile(late)]

    def operate(vec, layer, field):
        spot = LX * field + layer
        center = vec[spot, 8:24]
        value = diag[field, layer] * center + cross[layer] * vec[LX * (1 - field) + layer, 8:24]
        value = value - fx[field, layer - 1] * vec[spot - 1, 8:24] - fx[field, layer] * vec[spot + 1, 8:24]
        value = value - fym[field, layer] * vec[spot, 7:23] - fyp[field, layer] * vec[spot, 9:25]
        value = value - fzm[field, layer] * pltpu.roll(center, 1, axis=1)
        return value - fzp[field, layer] * pltpu.roll(center, NZ - 1, axis=1), center

    def fold(value):
        return value[:8] + value[8:]

    def first_image(layer, carry):
        rz, pq = carry
        for field in range(2):
            value, center = operate(v1, layer, field)
            q_own[field, layer] = value
            q_out[field, layer - 2] = value
            z_out[field, layer - 2] = center
            rz = rz + fold(r_own[field, layer] * center)
            pq = pq + fold(center * value)
        return rz, pq

    def rim_layer(side, present):
        layer = 1 + 33 * side
        for field in range(2):
            value, _ = operate(v1, layer, field)
            q_own[field, layer] = jnp.where(present, value, 0.0)

    def rim_rows():
        for side in range(2):
            place = 1 + 3 * side
            low_x = jnp.logical_and(rows_pk < 2, jnp.logical_not(has["xm"]))
            high_x = jnp.logical_and(rows_pk > 33, jnp.logical_not(has["xp"]))
            drop = jnp.logical_or(jnp.logical_or(low_x, high_x), jnp.logical_not(y_here[side]))
            drop = jnp.logical_or(drop, jnp.logical_or(rows_pk < 1, rows_pk > 34))
            for field in range(2):
                x_low, x_high, y_low, y_high, z_low, z_high = rim_faces(side, field)
                center = zp[place, field]
                value = c_pk[side, field] + ((x_low + x_high) + (y_low + y_high) + (z_low + z_high))
                value = value * center + cross_pk[side] * zp[place, 1 - field]
                value = value - x_low * pltpu.roll(center, 1, axis=0) - x_high * pltpu.roll(center, PX - 1, axis=0)
                value = value - y_low * zp[3 * side, field] - y_high * zp[3 * side + 2, field]
                value = value - jnp.where(first_pk, 0.0, z_low) * pltpu.roll(center, 1, axis=1)
                value = value - jnp.where(last_pk, 0.0, z_high) * pltpu.roll(center, NZ - 1, axis=1)
                q_pk[side, field] = jnp.where(drop, 0.0, value)

    def inner_layers(step, carry, image):
        return image(4 - 2 * late + step, carry)

    x_messages(3, u1, p1, set1, 10, near, near_here, near_gx, "arrived")
    y_messages(3, p1, set1, 10, "arrived")
    assemble_near(3, u1, p1, set1, v1, zp, 2)
    sums = lax.fori_loop(0, 30, functools.partial(inner_layers, image=first_image), (zero, zero), unroll=3)
    rim_layer(near, near_here)
    rim_rows()
    apply_box(q_own, q_pk, u2, p2, near)
    x_messages(2, u2, p2, set2, 20, near, near_here, near_gx, "push")
    x_messages(3, u1, p1, set1, 10, late, late_here, late_gx, "arrived")
    assemble_late(3, set1, v1, zp)
    for step in range(2):
        sums = first_image(2 + 30 * late + step, sums)
    rz, pq = sums
    rim_layer(late, late_here)
    rim_rows()
    apply_box(q_own, q_pk, u2, p2, late)
    x_messages(2, u2, p2, set2, 20, late, late_here, late_gx, "push")
    x_messages(2, u2, p2, set2, 20, late, late_here, late_gx, "pushed")
    y_messages(2, p2, set2, 20, "push")

    def second_image(layer, carry):
        rw, qw, zu, wu = carry
        for field in range(2):
            value, center = operate(v2, layer, field)
            u_out[field, layer - 2] = value
            w_out[field, layer - 2] = center
            rw = rw + fold(r_own[field, layer] * center)
            qw = qw + fold(q_own[field, layer] * center)
            zu = zu + fold(v1[LX * field + layer, 8:24] * value)
            wu = wu + fold(center * value)
        return rw, qw, zu, wu

    x_messages(2, u2, p2, set2, 20, near, near_here, near_gx, "arrived")
    y_messages(2, p2, set2, 20, "arrived")
    assemble_near(2, u2, p2, set2, v2, wp, 1)
    sums = lax.fori_loop(0, 30, functools.partial(inner_layers, image=second_image), (zero,) * 4, unroll=3)
    for n in range(2):
        pushed(sides[n][0], r_own.at[:, 2 + 31 * n], n)
        pushed(sides[n][0], zone.at[2 + 30 * n : 4 + 30 * n], 30 + n)
        pushed(y_here[n], r_send.at[n], 2 + n)
        pushed(y_here[n], zone_send.at[2 * n : 2 * n + 2], 32 + n)
    for c in range(4):
        pushed(sides[4 + c][0], r_corner_send.at[c], 4 + c)
    x_messages(3, u1, p1, set1, 10, near, near_here, near_gx, "pushed")
    y_messages(3, p1, set1, 10, "pushed")
    x_messages(2, u2, p2, set2, 20, near, near_here, near_gx, "pushed")
    y_messages(2, p2, set2, 20, "pushed")
    x_messages(2, u2, p2, set2, 20, late, late_here, late_gx, "arrived")
    assemble_late(2, set2, v2, wp)
    for step in range(2):
        sums = second_image(2 + 30 * late + step, sums)
    rw, qw, zu, wu = sums

    rows = [jnp.sum(v, axis=0, keepdims=True) for v in (rz, pq, rw, qw, zu, wu)]
    stack = jnp.concatenate(rows + [jnp.zeros((2, NZ), F32)], axis=0)
    for shift in (64, 32, 16):
        stack = stack + pltpu.roll(stack, shift, axis=1)
    group_of = lax.broadcasted_iota(jnp.int32, (8, NZ), 1) // 16
    mine = group_of == lax.broadcasted_iota(jnp.int32, (8, NZ), 0)
    spot = lax.broadcasted_iota(jnp.int32, (1, NZ), 1) // 16
    row = jnp.sum(jnp.where(mine, stack, 0.0), axis=0, keepdims=True)
    ar1[0] = row

    def all_reduce(slots, count, device_of, number):
        def send(k, carry):
            pltpu.make_async_remote_copy(
                src_ref=slots.at[0],
                dst_ref=slots.at[k],
                send_sem=ar_send.at[number],
                recv_sem=ar_recv.at[number],
                device_id=device_of(k),
                device_id_type=MESH,
            ).start()
            return carry

        for k in sorted(range(1, count), key=lambda k: -min(k, count - k)):
            send(k, 0)
        others = slots.at[1:count]
        pltpu.make_async_copy(others, others, ar_recv.at[number]).wait()
        pltpu.make_async_copy(others, others, ar_send.at[number]).wait()
        return jnp.sum(slots[...], axis=0)

    ar2[0] = all_reduce(ar1, plane, plane_id, 0)
    products = all_reduce(ar2, depth, depth_id, 1)
    rz, pq, rw, qw, zu, wu = (
        jnp.sum(jnp.where(spot == n, products, 0.0), axis=1, keepdims=True) for n in range(6)
    )
    alpha = rz / pq
    rz2 = rz - alpha * (rw + pq) + alpha * alpha * qw
    grow = 1.0 + rz2 / rz
    curve = grow * grow * pq - grow * alpha * (zu + qw) + alpha * alpha * wu
    alpha2 = rz2 / curve
    by_z_out[...] = jnp.broadcast_to(alpha + alpha2 * grow, (1, NZ))
    by_w_out[...] = jnp.broadcast_to(alpha2 * alpha, (1, NZ))


def shards(nx, ny, load, zones, conductance, capacity, coupling):
    to_modes, from_modes, z_forward, z_inverse, summed, group = constants()
    ax, ay = min(8, nx // 2), min(4, ny // 2)
    plane, depth = ax * ay, (nx // ax) * (ny // ay)
    vmem = lambda *shape, dtype=F32: pltpu.VMEM(shape, dtype)
    scratch = [
        pltpu.SMEM((2, ZONES), F32), pltpu.SMEM((2, ZONES), F32), pltpu.SMEM((ZONES,), F32),
        vmem(*to_modes.shape, dtype=BF16), vmem(*from_modes.shape, dtype=BF16),
        vmem(*z_forward.shape, dtype=BF16), vmem(*z_inverse.shape, dtype=BF16),
        vmem(*summed.shape), vmem(*group.shape, dtype=BF16),
        vmem(2, LX, BY, NZ), vmem(2, 2, PX, NZ),
        vmem(LX, BY, NZ, dtype=jnp.int32), vmem(8, NZ, dtype=jnp.int32),
        vmem(4, PX, NZ, dtype=jnp.int32), vmem(2, 2, PX, NZ, dtype=jnp.int32),
        vmem(2, 2, BX, NZ), vmem(2, 2, BX, NZ), vmem(4, 2, NZ), vmem(4, 2, NZ),
        vmem(2 * LX, 32, NZ), vmem(6, 2, PX, NZ), vmem(2, LX, BY, NZ), vmem(2, 2, PX, NZ),
        vmem(LX, BY, NZ), vmem(2, PX, NZ),
        vmem(2, LX, BY, NZ), vmem(2, LX, BY, NZ), vmem(2, LX, BY, NZ), vmem(2, LX, BY, NZ),
        vmem(2, LX, BY, NZ), vmem(2, LX, BY, NZ), vmem(8, NZ), vmem(2, 2 * MODES, 256),
        vmem(2, LX, BY, NZ), vmem(6, 2, PX, NZ), vmem(2 * LX, 32, NZ), vmem(6, 2, PX, NZ),
        vmem(2, LX, BY, NZ), vmem(2, 2, PX, NZ),
        vmem(2, LX, BY, NZ), vmem(6, 2, PX, NZ), vmem(2 * LX, 32, NZ), vmem(6, 2, PX, NZ),
    ]
    for width in (3, 2):
        scratch += [
            vmem(2, 2, width, BY, NZ), vmem(2, 2, 2, 4, NZ), vmem(2, 2, 2, 4, NZ),
            vmem(2, width, 2, PX, NZ), vmem(4, width, 2, 4, NZ), vmem(4, width, 2, 4, NZ),
        ]
    scratch += [
        vmem(plane, 1, NZ), vmem(depth, 1, NZ),
        pltpu.SemaphoreType.DMA((12,)), pltpu.SemaphoreType.DMA((34,)), pltpu.SemaphoreType.DMA((34,)),
        pltpu.SemaphoreType.DMA((2,)), pltpu.SemaphoreType.DMA((2,)),
    ]
    any_spec = pl.BlockSpec(memory_space=pltpu.HBM)
    out = pl.BlockSpec(memory_space=pltpu.VMEM)
    shape = jax.ShapeDtypeStruct((2, BX, BY, NZ), F32)
    z1, w, q1, u, by_z, by_w = pl.pallas_call(
        functools.partial(body, nx, ny),
        out_shape=(shape,) * 4 + (jax.ShapeDtypeStruct((1, NZ), F32),) * 2,
        in_specs=[any_spec] * 11,
        out_specs=(out,) * 6,
        scratch_shapes=scratch,
        compiler_params=pltpu.CompilerParams(
            collective_id=0, has_side_effects=True, vmem_limit_bytes=48 * 1024 * 1024
        ),
        name="pcg",
    )(
        *(pltpu.with_memory_space_constraint(a, pltpu.HBM) for a in (load, zones, conductance, capacity, coupling)),
        *(pltpu.with_memory_space_constraint(jnp.asarray(c), pltpu.HBM) for c in (to_modes, from_modes, z_forward, z_inverse, summed, group)),
    )
    by_z, by_w = by_z.reshape(NZ), by_w.reshape(NZ)
    return by_z * z1 - by_w * w, load - by_z * q1 + by_w * u


def solution(mesh):
    in_specs = (P(None, "gx", "gy", None), P("gx", "gy", None), P(), P(), P())
    out_specs = (P(None, "gx", "gy", None), P(None, "gx", "gy", None))
    run = functools.partial(shards, mesh.shape["gx"], mesh.shape["gy"])
    return jax.shard_map(run, mesh=mesh, in_specs=in_specs, out_specs=out_specs, check_vma=False)
```

```python
import functools

import jax
import jax.numpy as jnp
import numpy as np
from jax import lax
from jax.experimental import pallas as pl
from jax.experimental.pallas import tpu as pltpu
from jax.sharding import PartitionSpec as P

BOX = 16
SPAN = BOX + 2
BX = 32
BY = 16
NZ = 128
ZONES = 8
LX = BX + 4
PX = 40
MODES = 336
OWN = SPAN * BY
KIN = OWN + 48
MOUT = OWN + 144
F32 = jnp.float32
BF16 = jnp.bfloat16
MESH = pl.DeviceIdType.MESH


def split3(matrix):
    high = np.asarray(matrix, np.float32).astype(jnp.bfloat16)
    low = (np.asarray(matrix, np.float32) - high.astype(np.float32)).astype(jnp.bfloat16)
    return high, low


def constants():
    index = np.arange(SPAN)
    basis = np.sqrt(2.0 / (SPAN + 1)) * np.sin(np.pi * np.outer(index + 1, index + 1) / (SPAN + 1))
    lam = 4.0 * np.sin(np.pi * (index + 1) / (2.0 * (SPAN + 1))) ** 2
    forward = np.zeros((SPAN, SPAN, KIN))
    inner = np.einsum("ix,jy->ijxy", basis, basis[:, 1:17])
    forward[:, :, :OWN] = inner.reshape(SPAN, SPAN, OWN)
    for side, row in ((0, 0), (1, 17)):
        start = OWN + 24 * side + 1
        forward[:, :, start : start + SPAN] = np.einsum("ix,j->ijx", basis, basis[:, row])
    full = np.zeros((MODES, KIN))
    full[: SPAN * SPAN] = forward.reshape(SPAN * SPAN, KIN)
    high, low = split3(full)
    to_modes = np.concatenate([high, high, low], axis=1)
    inverse = np.zeros((MOUT, SPAN, SPAN))
    inverse[:OWN] = np.einsum("xi,yj->xyij", basis, basis[1:17]).reshape(OWN, SPAN, SPAN)
    for place, row in enumerate((0, 1, 2, 15, 16, 17)):
        start = OWN + 24 * place + 1
        inverse[start : start + SPAN] = np.einsum("xi,j->xij", basis, basis[row])
    full = np.zeros((MOUT, MODES))
    full[:, : SPAN * SPAN] = inverse.reshape(MOUT, SPAN * SPAN)
    high, low = split3(full)
    from_modes = np.concatenate([high, high, low], axis=1)
    boxes = NZ // BOX
    count = boxes * SPAN
    banded = np.zeros((NZ, count))
    for box in range(boxes):
        for offset in range(SPAN):
            cell = BOX * box + offset - 1
            if 0 <= cell < NZ:
                banded[cell, box * SPAN : (box + 1) * SPAN] = basis[:, offset]
    rest = count - 128
    lanes = np.concatenate([np.arange(128)] + [128 + np.arange(rest)] * 3)
    wide = np.zeros((NZ, 256))
    wide[:, : lanes.size] = banded[:, lanes]
    high, low = split3(wide)
    z_forward = np.concatenate([high, high, low], axis=0)
    high, low = split3(banded.T)
    tail = np.zeros((128, NZ), jnp.bfloat16)
    tail[:rest] = high[128:]
    tail[rest : 2 * rest] = high[128:]
    tail[2 * rest : 3 * rest] = low[128:]
    z_inverse = np.concatenate([high[:128], high[:128], low[:128], tail], axis=0)
    summed = np.zeros((MODES, 256), np.float32)
    plane = (lam[:, None] + lam[None, :]).reshape(-1)
    summed[: SPAN * SPAN, : lanes.size] = plane[:, None] + lam[lanes % SPAN][None, :]
    group = np.zeros((NZ, 256))
    group[:, : lanes.size] = (np.arange(NZ)[:, None] // BOX) == (lanes // SPAN)[None, :]
    group = np.concatenate([group] * 3, axis=0).astype(jnp.bfloat16)
    return to_modes, from_modes, z_forward, z_inverse, summed, group


def lookup(zone, table):
    bit0 = (zone & 1) != 0
    bit1 = (zone & 2) != 0
    bit2 = (zone & 4) != 0

    def pick(values):
        a = jnp.where(bit0, values[1], values[0])
        b = jnp.where(bit0, values[3], values[2])
        c = jnp.where(bit0, values[5], values[4])
        d = jnp.where(bit0, values[7], values[6])
        return jnp.where(bit2, jnp.where(bit1, d, c), jnp.where(bit1, b, a))

    return [pick(values) for values in table]


def halves(value):
    high = value.astype(BF16)
    low = (value - high.astype(F32)).astype(BF16)
    return high, low


def dot(a, b):
    return jnp.dot(a, b, preferred_element_type=F32)


def body(
    nx, ny,
    load_ref, zones_ref, cond_hbm, cap_hbm, coup_hbm,
    tf_hbm, ti_hbm, zf_hbm, zi_hbm, lam_hbm, group_hbm,
    z_out, w_out, q_out, u_out, by_z_out, by_w_out,
    cond_ref, cap_ref, coup_ref, tf, ti, zf, zi, lam, group,
    r_own, r_pk, zone, zone_pk, zone_send, zone_recv,
    r_send, r_recv, r_corner_send, r_corner,
    k_own, k_pk, c_own, c_pk, cross, cross_pk,
    fx, fym, fyp, fzm, fzp, diag, diag_pk, dinv,
    u1, p1, v1, zp, q_own, q_pk, u2, p2, v2, wp,
    xl1, xc1, xcs1, yr1, dg1, dgs1, xl2, xc2, xcs2, yr2, dg2, dgs2,
    rim, ar1, ar2,
    local_sem, send_sem, recv_sem, ar_send, ar_recv,
):
    gx = lax.axis_index("gx")
    gy = lax.axis_index("gy")
    has = {"xm": gx > 0, "xp": gx < nx - 1, "ym": gy > 0, "yp": gy < ny - 1}
    ax, ay = min(8, nx // 2), min(4, ny // 2)
    plane, depth = ax * ay, (nx // ax) * (ny // ay)
    div, rem = lax.div, lax.rem
    across, along = nx // ax, ny // ay
    gx_block, gx_in = div(gx, jnp.int32(ax)), rem(gx, jnp.int32(ax))
    gy_block, gy_in = div(gy, jnp.int32(ay)), rem(gy, jnp.int32(ay))
    here = gx_in * ay + gy_in
    level = gx_block * along + gy_block

    def plane_id(k):
        t = rem(here + k, jnp.int32(plane))
        return (gx_block * ax + div(t, jnp.int32(ay)), gy_block * ay + rem(t, jnp.int32(ay)))

    def depth_id(k):
        t = rem(level + k, jnp.int32(depth))
        return (div(t, jnp.int32(along)) * ax + gx_in, rem(t, jnp.int32(along)) * ay + gy_in)

    late = jnp.where(gx_in == 0, 0, 1).astype(jnp.int32)
    near = 1 - late
    near_gx, late_gx = gx + 1 - 2 * late, gx - 1 + 2 * late
    near_here = jnp.logical_and(near_gx >= 0, near_gx < nx)
    late_here = jnp.logical_and(late_gx >= 0, late_gx < nx)
    y_here = (has["ym"], has["yp"])
    sides = [(has["xm"], (gx - 1, gy)), (has["xp"], (gx + 1, gy)), (has["ym"], (gx, gy - 1)), (has["yp"], (gx, gy + 1))]
    for c in range(4):
        present = jnp.logical_and(sides[c // 2][0], y_here[c % 2])
        sides.append((present, (gx - 1 + 2 * (c // 2), gy - 1 + 2 * (c % 2))))

    loads = [
        pltpu.make_async_copy(load_ref.at[0], r_own.at[0, 2:34], local_sem.at[0]),
        pltpu.make_async_copy(load_ref.at[1], r_own.at[1, 2:34], local_sem.at[1]),
        pltpu.make_async_copy(zones_ref, zone.at[2:34], local_sem.at[2]),
        pltpu.make_async_copy(cond_hbm, cond_ref, local_sem.at[9]),
        pltpu.make_async_copy(cap_hbm, cap_ref, local_sem.at[10]),
        pltpu.make_async_copy(coup_hbm, coup_ref, local_sem.at[11]),
    ]
    weights = [
        pltpu.make_async_copy(source, target, local_sem.at[3 + n])
        for n, (source, target) in enumerate(
            ((tf_hbm, tf), (zf_hbm, zf), (group_hbm, group), (lam_hbm, lam), (zi_hbm, zi), (ti_hbm, ti))
        )
    ]
    barrier = pltpu.get_barrier_semaphore()
    for present, device in sides:

        @pl.when(present)
        def _():
            pl.semaphore_signal(barrier, inc=1, device_id=device, device_id_type=MESH)

    def greet_plane(k, carry):
        pl.semaphore_signal(barrier, inc=1, device_id=plane_id(k), device_id_type=MESH)
        return carry

    def greet_depth(k, carry):
        pl.semaphore_signal(barrier, inc=1, device_id=depth_id(k), device_id_type=MESH)
        return carry

    lax.fori_loop(1, depth, greet_depth, 0)
    for copy in loads + weights:
        copy.start()
    lax.fori_loop(1, plane, greet_plane, 0)

    def clear(*refs):
        for ref in refs:
            ref[...] = jnp.zeros(ref.shape, ref.dtype)

    clear(r_pk, u1, p1, u2, p2)
    for side, name in enumerate(("xm", "xp")):

        @pl.when(jnp.logical_not(has[name]))
        def _():
            clear(r_own.at[0, 1 + 33 * side], r_own.at[1, 1 + 33 * side])
            clear(xl1.at[side], xc1.at[side], xl2.at[side], xc2.at[side])

    for side, name in enumerate(("ym", "yp")):

        @pl.when(jnp.logical_not(has[name]))
        def _():
            clear(r_recv.at[side], yr1.at[side], yr2.at[side])

    for corner in range(4):

        @pl.when(jnp.logical_not(sides[4 + corner][0]))
        def _():
            clear(r_corner.at[corner], dg1.at[corner], dg2.at[corner])

    for copy in loads:
        copy.wait()

    for field in range(2):
        r_send[0, field] = r_own[field, 2:34, 0]
        r_send[1, field] = r_own[field, 2:34, BY - 1]
    for corner, (layer, row) in enumerate(((2, 0), (2, 15), (33, 0), (33, 15))):
        for field in range(2):
            r_corner_send[corner, field : field + 1] = r_own[field, layer, row : row + 1]

    members = jnp.int32(plane - 1 + depth - 1)
    for present, _ in sides:
        members = members + present.astype(jnp.int32)
    pl.semaphore_wait(barrier, members)

    def push(present, device, source, target, out_slot, in_slot):
        @pl.when(present)
        def _():
            pltpu.make_async_remote_copy(
                src_ref=source,
                dst_ref=target,
                send_sem=send_sem.at[out_slot],
                recv_sem=recv_sem.at[in_slot],
                device_id=device,
                device_id_type=MESH,
            ).start()

    def pushed(present, source, slot):
        @pl.when(present)
        def _():
            pltpu.make_async_copy(source, source, send_sem.at[slot]).wait()

    def arrived(present, target, slot):
        @pl.when(present)
        def _():
            pltpu.make_async_copy(target, target, recv_sem.at[slot]).wait()

    for n in range(2):
        push(*sides[n], r_own.at[:, 2 + 31 * n], r_own.at[:, 34 - 33 * n], n, 1 - n)
    for c in range(4):
        push(*sides[4 + c], r_corner_send.at[c], r_corner.at[3 - c], 4 + c, 7 - c)
    for n in range(2):
        push(*sides[2 + n], r_send.at[n], r_recv.at[1 - n], 2 + n, 3 - n)
    for n in range(2):
        push(*sides[n], zone.at[2 + 30 * n : 4 + 30 * n], zone.at[34 - 34 * n : 36 - 34 * n], 30 + n, 31 - n)

    table = [[ref[f, q] for q in range(ZONES)] for ref in (cond_ref, cap_ref) for f in range(2)]
    table.append([coup_ref[q] for q in range(ZONES)])

    def own_coefficients(layer, sums):
        k0, k1, c0, c1, share = lookup(zone[layer], table)
        k_own[layer, 8:24] = k0
        k_own[LX + layer, 8:24] = k1
        c_own[0, layer] = c0
        c_own[1, layer] = c1
        cross[layer] = share * jnp.sqrt(c0 * c1)
        return tuple(s + v[:8] + v[8:] for s, v in zip(sums, (c0, c1, k0, k1)))

    zero = jnp.zeros((8, NZ), F32)
    pieces = []
    for box in range(2):
        sums = lax.fori_loop(2 + BOX * box, 2 + BOX * (box + 1), own_coefficients, (zero,) * 4)
        pieces.extend(jnp.sum(s, axis=0, keepdims=True) for s in sums)
    total = jnp.concatenate(pieces, axis=0)
    part0 = total.astype(BF16)
    rest = total - part0.astype(F32)
    part1 = rest.astype(BF16)
    part2 = (rest - part1.astype(F32)).astype(BF16)
    for copy in weights:
        copy.wait()
    means = dot(jnp.concatenate([part0, part1, part2], axis=1), group[...]) * (1.0 / BOX**3)
    lane = lax.broadcasted_iota(jnp.int32, (1, 256), 1)
    unused = jnp.where(lane >= 128 + 48, 1.0, 0.0)
    for box in range(2):
        for field in range(2):
            cbar = means[4 * box + field : 4 * box + field + 1] + unused
            kbar = means[4 * box + 2 + field : 4 * box + 3 + field]
            dinv[box, MODES * field : MODES * (field + 1)] = 1.0 / (cbar + kbar * lam[...])

    lane_tail = lax.broadcasted_iota(jnp.int32, (1, 128), 1)
    low_lanes = jnp.logical_and(lane_tail >= 16, lane_tail < 32)

    def apply_box(own, packed, out, out_pk, box):
        layers = pl.ds(1 + BOX * box, SPAN)
        spots = pl.ds(pl.multiple_of(BOX * box, 8), 24)
        columns = []
        for field in range(2):
            inner = own[field, layers].reshape(OWN, NZ)
            columns.append(jnp.concatenate([inner] + [packed[side, field, spots] for side in range(2)], axis=0))
        high, low = halves(jnp.concatenate(columns, axis=1))
        modes = dot(tf[...], jnp.concatenate([high, low, high], axis=0))
        high, low = halves(jnp.concatenate([modes[:, :NZ], modes[:, NZ:]], axis=0))
        deep = dot(jnp.concatenate([high, low, high], axis=1), zf[...]) * dinv[box]
        high, low = halves(deep[:, :128])
        tail = deep[:, 128:]
        tail_high = tail.astype(BF16).astype(F32)
        tail = jnp.where(low_lanes, tail - tail_high, tail_high).astype(BF16)
        lines = dot(jnp.concatenate([high, low, high, tail], axis=1), zi[...])
        columns = [lines[:MODES], lines[MODES:]]
        high, low = halves(jnp.concatenate(columns, axis=1))
        cells = dot(ti[...], jnp.concatenate([high, low, high], axis=0))
        for field in range(2):
            mine = cells[:, NZ * field : NZ * (field + 1)]
            out[field, layers] += mine[:OWN].reshape(SPAN, BY, NZ)
            out_pk[:, field, spots] += mine[OWN:].reshape(6, 24, NZ)

    def tile(side):
        return pl.ds(pl.multiple_of(32 * side, 8), 4)

    def x_messages(width, own, packed, bufs, base, side, present, side_gx, act):
        x_layers, x_corner, x_corner_send, y_rows, corners, corners_send = bufs
        layers = pl.ds(1 + (34 - width) * side, width)
        device = (side_gx, gy)
        if act == "push":
            push(present, device, own.at[:, layers], x_layers.at[1 - side], base + side, base + 1 - side)
            for place, row in enumerate((0, 5)):
                x_corner_send[side, place] = packed[row, :, tile(side)]
            push(present, device, x_corner_send.at[side], x_corner.at[1 - side], base + 8 + side, base + 9 - side)
        elif act == "pushed":
            pushed(present, own.at[:, layers], base + side)
            pushed(present, x_corner_send.at[side], base + 8 + side)
        else:
            arrived(present, x_layers.at[side], base + side)
            arrived(present, x_corner.at[side], base + 8 + side)
        for n in range(2):
            c = 2 * side + n
            both = jnp.logical_and(present, y_here[n])
            if act == "push":
                for place in range(width):
                    corners_send[c, place] = packed[(6 - width) * n + place, :, tile(side)]
                device = (side_gx, gy - 1 + 2 * n)
                push(both, device, corners_send.at[c], corners.at[3 - c], base + 4 + c, base + 7 - c)
            elif act == "pushed":
                pushed(both, corners_send.at[c], base + 4 + c)
            else:
                arrived(both, corners.at[c], base + 4 + c)

    def y_messages(width, packed, bufs, base, act):
        y_rows = bufs[3]
        for n in range(2):
            rows = packed.at[(6 - width) * n : (6 - width) * n + width]
            if act == "push":
                push(*sides[2 + n], rows, y_rows.at[1 - n], base + 2 + n, base + 3 - n)
            elif act == "pushed":
                pushed(y_here[n], rows, base + 2 + n)
            else:
                arrived(y_here[n], y_rows.at[n], base + 2 + n)

    rows_pk = lax.broadcasted_iota(jnp.int32, (PX, NZ), 0)

    def corner_rows(side):
        for n in range(2):
            for field in range(2):
                row = r_corner[2 * side + n, field : field + 1]
                r_pk[n, field] = jnp.where(rows_pk == 1 + 33 * side, row, r_pk[n, field])

    for n in range(2):
        arrived(y_here[n], r_recv.at[n], 2 + n)
        for field in range(2):
            r_pk[n, field, 2:34] = r_recv[n, field]
        arrived(jnp.logical_and(near_here, y_here[n]), r_corner.at[2 * near + n], 4 + 2 * near + n)
    arrived(near_here, r_own.at[:, 1 + 33 * near], near)
    corner_rows(near)
    set1 = (xl1, xc1, xcs1, yr1, dg1, dgs1)
    set2 = (xl2, xc2, xcs2, yr2, dg2, dgs2)
    apply_box(r_own, r_pk, u1, p1, near)
    x_messages(3, u1, p1, set1, 10, near, near_here, near_gx, "push")
    for n in range(2):
        arrived(jnp.logical_and(late_here, y_here[n]), r_corner.at[2 * late + n], 4 + 2 * late + n)
    arrived(late_here, r_own.at[:, 1 + 33 * late], late)
    corner_rows(late)
    apply_box(r_own, r_pk, u1, p1, late)
    x_messages(3, u1, p1, set1, 10, late, late_here, late_gx, "push")

    for n in range(2):
        arrived(sides[n][0], zone.at[34 * n : 34 * n + 2], 30 + n)

        @pl.when(jnp.logical_not(sides[n][0]))
        def _():
            edge = zone[2 + 31 * n]
            zone[34 * n] = edge
            zone[34 * n + 1] = edge

    for place, row in enumerate((0, 1, 14, 15)):
        zone_send[place] = jnp.zeros((PX, NZ), jnp.int32)
        zone_send[place, 0:LX] = zone[:, row]
    for n in range(2):
        push(*sides[2 + n], zone_send.at[2 * n : 2 * n + 2], zone_recv.at[1 - n], 32 + n, 33 - n)
    y_messages(3, p1, set1, 10, "push")
    x_messages(3, u1, p1, set1, 10, late, late_here, late_gx, "pushed")
    for layer in (0, 1, 34, 35):
        k0, k1, c0, c1, share = lookup(zone[layer], table)
        k_own[layer, 8:24] = k0
        k_own[LX + layer, 8:24] = k1
        c_own[0, layer] = c0
        c_own[1, layer] = c1
        cross[layer] = share * jnp.sqrt(c0 * c1)
    for n in range(2):
        arrived(y_here[n], zone_recv.at[n], 32 + n)

        @pl.when(jnp.logical_not(y_here[n]))
        def _():
            edge = zone_send[3 * n]
            zone_recv[n, 0] = edge
            zone_recv[n, 1] = edge

    for place in range(6):
        packed_zone = (
            zone_recv[0, place] if place < 2
            else zone_send[0] if place == 2
            else zone_send[3] if place == 3
            else zone_recv[1, place - 4]
        )
        k0, k1, c0, c1, share = lookup(packed_zone, table)
        k_pk[place, 0] = k0
        k_pk[place, 1] = k1
        if place in (1, 4):
            side = 0 if place == 1 else 1
            c_pk[side, 0] = c0
            c_pk[side, 1] = c1
            cross_pk[side] = share * jnp.sqrt(c0 * c1)
            for field, value in enumerate((k0, k1)):
                k_own[LX * field : LX * (field + 1), 7 if side == 0 else 24] = value[:LX]

    lanes = lax.broadcasted_iota(jnp.int32, (BY, NZ), 1)
    first_lane, last_lane = lanes == 0, lanes == NZ - 1
    for field in range(2):
        fx[field, 0] = 0.5 * (k_own[LX * field, 8:24] + k_own[LX * field + 1, 8:24])

    def faces(layer, carry):
        for field in range(2):
            spot = LX * field + layer
            center = k_own[spot, 8:24]
            x_low = fx[field, layer - 1]
            x_high = 0.5 * (center + k_own[spot + 1, 8:24])
            fx[field, layer] = x_high
            y_low = 0.5 * (center + k_own[spot, 7:23])
            y_high = 0.5 * (center + k_own[spot, 9:25])
            z_low = 0.5 * (center + jnp.where(first_lane, center, pltpu.roll(center, 1, axis=1)))
            z_high = 0.5 * (center + jnp.where(last_lane, center, pltpu.roll(center, NZ - 1, axis=1)))
            fym[field, layer] = y_low
            fyp[field, layer] = y_high
            fzm[field, layer] = jnp.where(first_lane, 0.0, z_low)
            fzp[field, layer] = jnp.where(last_lane, 0.0, z_high)
            diag[field, layer] = c_own[field, layer] + (
                (x_low + x_high) + (y_low + y_high) + (z_low + z_high)
            )
        return carry

    lax.fori_loop(1, 35, faces, 0, unroll=2)

    lanes_pk = lax.broadcasted_iota(jnp.int32, (PX, NZ), 1)
    first_pk, last_pk = lanes_pk == 0, lanes_pk == NZ - 1

    def rim_faces(side, field):
        center = k_pk[1 + 3 * side, field]
        x_low = 0.5 * (center + pltpu.roll(center, 1, axis=0))
        x_high = 0.5 * (center + pltpu.roll(center, PX - 1, axis=0))
        y_low = 0.5 * (center + k_pk[3 * side, field])
        y_high = 0.5 * (center + k_pk[3 * side + 2, field])
        z_low = 0.5 * (center + jnp.where(first_pk, center, pltpu.roll(center, 1, axis=1)))
        z_high = 0.5 * (center + jnp.where(last_pk, center, pltpu.roll(center, NZ - 1, axis=1)))
        return x_low, x_high, y_low, y_high, z_low, z_high

    for side in range(2):
        for field in range(2):
            values = rim_faces(side, field)
            x_low, x_high, y_low, y_high, z_low, z_high = values
            for place, value in enumerate(values[:4]):
                rim[side, field, place] = value
            rim[side, field, 4] = jnp.where(first_pk, 0.0, z_low)
            rim[side, field, 5] = jnp.where(last_pk, 0.0, z_high)
            rim[side, field, 6] = c_pk[side, field] + (
                (x_low + x_high) + (y_low + y_high) + (z_low + z_high)
            )

    def assemble_near(width, own, packed, bufs, total_v, total_pk, margin):
        x_layers, x_corner, _, y_rows, corners, _ = bufs
        low0 = 3 - width
        for field in range(2):
            base = LX * field

            def copy_layer(layer, carry):
                total_v[base + layer, 8:24] = own[field, layer]
                return carry

            lax.fori_loop(3, 33, copy_layer, 0, unroll=6)
            for side, present in ((near, near_here), (late, late_here)):
                for step in range(width):
                    layer = low0 + (33 - low0) * side + step
                    value = own[field, layer]
                    if side is near:
                        value = value + x_layers[near, field, step]
                    beyond = jnp.logical_or(layer < 2, layer > 33)
                    drop = jnp.logical_and(beyond, jnp.logical_not(present))
                    total_v[base + layer, 8:24] = jnp.where(drop, 0.0, value)
        low_x = jnp.logical_and(rows_pk < 2, jnp.logical_not(has["xm"]))
        high_x = jnp.logical_and(rows_pk > 33, jnp.logical_not(has["xp"]))
        beyond_x = jnp.logical_or(low_x, high_x)
        for n in range(2):
            for step in range(width):
                y = 1 - width + step if n == 0 else 15 + step
                place = y + 2 if n == 0 else y - 12
                total_pk[place] = y_rows[n, step]
                total_pk[place, :, tile(near)] += corners[2 * near + n, step]
                if y == -1 or y == 16:
                    total_pk[place] += packed[5 * n]
                    total_pk[place, :, tile(near)] += x_corner[near, n]
                drop = beyond_x
                if y < 0 or y > 15:
                    drop = jnp.logical_or(drop, jnp.logical_not(y_here[n]))
                for field in range(2):
                    total_pk[place, field] = jnp.where(drop, 0.0, total_pk[place, field])
        for field in range(2):
            lo = 2 - margin
            count = BX + 2 * margin
            window = slice(LX * field + lo, LX * field + lo + count)
            for place, outer, row, halo in ((2, 1, 8, 7), (3, 4, 23, 24)):
                edge = total_v[window, row] + total_pk[place, field, lo : lo + count]
                total_v[window, row] = edge
                total_pk[place, field, lo : lo + count] = edge
                total_v[window, halo] = total_pk[outer, field, lo : lo + count]

    def assemble_late(width, bufs, total_v, total_pk):
        x_layers, x_corner, _, _, corners, _ = bufs
        low0 = 3 - width
        for field in range(2):
            for step in range(width):
                spot = LX * field + low0 + (33 - low0) * late + step
                total_v[spot, 8:24] += x_layers[late, field, step]
            block = pl.ds(LX * field + 32 * late, 4)
            for n, edge_place, outer, row, halo in ((0, 2, 1, 8, 7), (1, 3, 4, 23, 24)):
                for step in range(width):
                    y = 1 - width + step if n == 0 else 15 + step
                    place = y + 2 if n == 0 else y - 12
                    piece = corners[2 * late + n, step, field]
                    if y == -1 or y == 16:
                        piece = piece + jnp.where(y_here[n], x_corner[late, n, field], 0.0)
                    if place == edge_place:
                        edge = total_v[block, row] + piece
                        total_v[block, row] = edge
                        total_pk[place, field, tile(late)] = edge
                    else:
                        total_pk[place, field, tile(late)] += piece
                total_v[block, halo] = total_pk[outer, field, tile(late)]

    def operate(vec, layer, field):
        spot = LX * field + layer
        center = vec[spot, 8:24]
        value = diag[field, layer] * center + cross[layer] * vec[LX * (1 - field) + layer, 8:24]
        value = value - fx[field, layer - 1] * vec[spot - 1, 8:24] - fx[field, layer] * vec[spot + 1, 8:24]
        value = value - fym[field, layer] * vec[spot, 7:23] - fyp[field, layer] * vec[spot, 9:25]
        value = value - fzm[field, layer] * pltpu.roll(center, 1, axis=1)
        return value - fzp[field, layer] * pltpu.roll(center, NZ - 1, axis=1), center

    def fold(value):
        return value[:8] + value[8:]

    def first_image(layer, carry):
        rz, pq = carry
        for field in range(2):
            value, center = operate(v1, layer, field)
            q_own[field, layer] = value
            q_out[field, layer - 2] = value
            z_out[field, layer - 2] = center
            rz = rz + fold(r_own[field, layer] * center)
            pq = pq + fold(center * value)
        return rz, pq

    def rim_layer(side, present):
        layer = 1 + 33 * side
        for field in range(2):
            value, _ = operate(v1, layer, field)
            q_own[field, layer] = jnp.where(present, value, 0.0)

    def rim_rows():
        for side in range(2):
            place = 1 + 3 * side
            low_x = jnp.logical_and(rows_pk < 2, jnp.logical_not(has["xm"]))
            high_x = jnp.logical_and(rows_pk > 33, jnp.logical_not(has["xp"]))
            drop = jnp.logical_or(jnp.logical_or(low_x, high_x), jnp.logical_not(y_here[side]))
            drop = jnp.logical_or(drop, jnp.logical_or(rows_pk < 1, rows_pk > 34))
            for field in range(2):
                x_low, x_high, y_low, y_high, z_low, z_high, main = (rim[side, field, n] for n in range(7))
                center = zp[place, field]
                value = main * center + cross_pk[side] * zp[place, 1 - field]
                value = value - x_low * pltpu.roll(center, 1, axis=0) - x_high * pltpu.roll(center, PX - 1, axis=0)
                value = value - y_low * zp[3 * side, field] - y_high * zp[3 * side + 2, field]
                value = value - z_low * pltpu.roll(center, 1, axis=1)
                value = value - z_high * pltpu.roll(center, NZ - 1, axis=1)
                q_pk[side, field] = jnp.where(drop, 0.0, value)

    def inner_layers(step, carry, image):
        return image(4 - 2 * late + step, carry)

    x_messages(3, u1, p1, set1, 10, near, near_here, near_gx, "arrived")
    y_messages(3, p1, set1, 10, "arrived")
    assemble_near(3, u1, p1, set1, v1, zp, 2)
    sums = lax.fori_loop(0, 30, functools.partial(inner_layers, image=first_image), (zero, zero), unroll=3)
    rim_layer(near, near_here)
    rim_rows()
    apply_box(q_own, q_pk, u2, p2, near)
    x_messages(2, u2, p2, set2, 20, near, near_here, near_gx, "push")
    x_messages(3, u1, p1, set1, 10, late, late_here, late_gx, "arrived")
    assemble_late(3, set1, v1, zp)
    for step in range(2):
        sums = first_image(2 + 30 * late + step, sums)
    rz, pq = sums
    rim_layer(late, late_here)
    rim_rows()
    apply_box(q_own, q_pk, u2, p2, late)
    x_messages(2, u2, p2, set2, 20, late, late_here, late_gx, "push")
    x_messages(2, u2, p2, set2, 20, late, late_here, late_gx, "pushed")
    y_messages(2, p2, set2, 20, "push")

    def second_image(layer, carry):
        rw, qw, zu, wu = carry
        for field in range(2):
            value, center = operate(v2, layer, field)
            u_out[field, layer - 2] = value
            w_out[field, layer - 2] = center
            rw = rw + fold(r_own[field, layer] * center)
            qw = qw + fold(q_own[field, layer] * center)
            zu = zu + fold(v1[LX * field + layer, 8:24] * value)
            wu = wu + fold(center * value)
        return rw, qw, zu, wu

    x_messages(2, u2, p2, set2, 20, near, near_here, near_gx, "arrived")
    y_messages(2, p2, set2, 20, "arrived")
    assemble_near(2, u2, p2, set2, v2, wp, 1)
    sums = lax.fori_loop(0, 30, functools.partial(inner_layers, image=second_image), (zero,) * 4, unroll=3)
    for n in range(2):
        pushed(sides[n][0], r_own.at[:, 2 + 31 * n], n)
        pushed(sides[n][0], zone.at[2 + 30 * n : 4 + 30 * n], 30 + n)
        pushed(y_here[n], r_send.at[n], 2 + n)
        pushed(y_here[n], zone_send.at[2 * n : 2 * n + 2], 32 + n)
    for c in range(4):
        pushed(sides[4 + c][0], r_corner_send.at[c], 4 + c)
    x_messages(3, u1, p1, set1, 10, near, near_here, near_gx, "pushed")
    y_messages(3, p1, set1, 10, "pushed")
    x_messages(2, u2, p2, set2, 20, near, near_here, near_gx, "pushed")
    y_messages(2, p2, set2, 20, "pushed")
    x_messages(2, u2, p2, set2, 20, late, late_here, late_gx, "arrived")
    assemble_late(2, set2, v2, wp)
    for step in range(2):
        sums = second_image(2 + 30 * late + step, sums)
    rw, qw, zu, wu = sums

    rows = [jnp.sum(v, axis=0, keepdims=True) for v in (rz, pq, rw, qw, zu, wu)]
    stack = jnp.concatenate(rows + [jnp.zeros((2, NZ), F32)], axis=0)
    for shift in (64, 32, 16):
        stack = stack + pltpu.roll(stack, shift, axis=1)
    group_of = lax.broadcasted_iota(jnp.int32, (8, NZ), 1) // 16
    mine = group_of == lax.broadcasted_iota(jnp.int32, (8, NZ), 0)
    spot = lax.broadcasted_iota(jnp.int32, (1, NZ), 1) // 16
    row = jnp.sum(jnp.where(mine, stack, 0.0), axis=0, keepdims=True)
    ar1[0] = row

    def all_reduce(slots, count, device_of, number):
        def send(k, carry):
            pltpu.make_async_remote_copy(
                src_ref=slots.at[0],
                dst_ref=slots.at[k],
                send_sem=ar_send.at[number],
                recv_sem=ar_recv.at[number],
                device_id=device_of(k),
                device_id_type=MESH,
            ).start()
            return carry

        for k in sorted(range(1, count), key=lambda k: -min(k, count - k)):
            send(k, 0)
        others = slots.at[1:count]
        pltpu.make_async_copy(others, others, ar_recv.at[number]).wait()
        return jnp.sum(slots[...], axis=0)

    ar2[0] = all_reduce(ar1, plane, plane_id, 0)
    products = all_reduce(ar2, depth, depth_id, 1)
    for slots, count, number in ((ar1, plane, 0), (ar2, depth, 1)):
        sent = slots.at[1:count]
        pltpu.make_async_copy(sent, sent, ar_send.at[number]).wait()
    rz, pq, rw, qw, zu, wu = (
        jnp.sum(jnp.where(spot == n, products, 0.0), axis=1, keepdims=True) for n in range(6)
    )
    alpha = rz / pq
    rz2 = rz - alpha * (rw + pq) + alpha * alpha * qw
    grow = 1.0 + rz2 / rz
    curve = grow * grow * pq - grow * alpha * (zu + qw) + alpha * alpha * wu
    alpha2 = rz2 / curve
    by_z_out[...] = jnp.broadcast_to(alpha + alpha2 * grow, (1, NZ))
    by_w_out[...] = jnp.broadcast_to(alpha2 * alpha, (1, NZ))


def shards(nx, ny, load, zones, conductance, capacity, coupling):
    to_modes, from_modes, z_forward, z_inverse, summed, group = constants()
    ax, ay = min(8, nx // 2), min(4, ny // 2)
    plane, depth = ax * ay, (nx // ax) * (ny // ay)
    vmem = lambda *shape, dtype=F32: pltpu.VMEM(shape, dtype)
    scratch = [
        pltpu.SMEM((2, ZONES), F32), pltpu.SMEM((2, ZONES), F32), pltpu.SMEM((ZONES,), F32),
        vmem(*to_modes.shape, dtype=BF16), vmem(*from_modes.shape, dtype=BF16),
        vmem(*z_forward.shape, dtype=BF16), vmem(*z_inverse.shape, dtype=BF16),
        vmem(*summed.shape), vmem(*group.shape, dtype=BF16),
        vmem(2, LX, BY, NZ), vmem(2, 2, PX, NZ),
        vmem(LX, BY, NZ, dtype=jnp.int32), vmem(8, NZ, dtype=jnp.int32),
        vmem(4, PX, NZ, dtype=jnp.int32), vmem(2, 2, PX, NZ, dtype=jnp.int32),
        vmem(2, 2, BX, NZ), vmem(2, 2, BX, NZ), vmem(4, 2, NZ), vmem(4, 2, NZ),
        vmem(2 * LX, 32, NZ), vmem(6, 2, PX, NZ), vmem(2, LX, BY, NZ), vmem(2, 2, PX, NZ),
        vmem(LX, BY, NZ), vmem(2, PX, NZ),
        vmem(2, LX, BY, NZ), vmem(2, LX, BY, NZ), vmem(2, LX, BY, NZ), vmem(2, LX, BY, NZ),
        vmem(2, LX, BY, NZ), vmem(2, LX, BY, NZ), vmem(8, NZ), vmem(2, 2 * MODES, 256),
        vmem(2, LX, BY, NZ), vmem(6, 2, PX, NZ), vmem(2 * LX, 32, NZ), vmem(6, 2, PX, NZ),
        vmem(2, LX, BY, NZ), vmem(2, 2, PX, NZ),
        vmem(2, LX, BY, NZ), vmem(6, 2, PX, NZ), vmem(2 * LX, 32, NZ), vmem(6, 2, PX, NZ),
    ]
    for width in (3, 2):
        scratch += [
            vmem(2, 2, width, BY, NZ), vmem(2, 2, 2, 4, NZ), vmem(2, 2, 2, 4, NZ),
            vmem(2, width, 2, PX, NZ), vmem(4, width, 2, 4, NZ), vmem(4, width, 2, 4, NZ),
        ]
    scratch += [
        vmem(2, 2, 7, PX, NZ), vmem(plane, 1, NZ), vmem(depth, 1, NZ),
        pltpu.SemaphoreType.DMA((12,)), pltpu.SemaphoreType.DMA((34,)), pltpu.SemaphoreType.DMA((34,)),
        pltpu.SemaphoreType.DMA((2,)), pltpu.SemaphoreType.DMA((2,)),
    ]
    any_spec = pl.BlockSpec(memory_space=pltpu.HBM)
    out = pl.BlockSpec(memory_space=pltpu.VMEM)
    shape = jax.ShapeDtypeStruct((2, BX, BY, NZ), F32)
    z1, w, q1, u, by_z, by_w = pl.pallas_call(
        functools.partial(body, nx, ny),
        out_shape=(shape,) * 4 + (jax.ShapeDtypeStruct((1, NZ), F32),) * 2,
        in_specs=[any_spec] * 11,
        out_specs=(out,) * 6,
        scratch_shapes=scratch,
        compiler_params=pltpu.CompilerParams(
            collective_id=0, has_side_effects=True, vmem_limit_bytes=48 * 1024 * 1024
        ),
        name="pcg",
    )(
        *(pltpu.with_memory_space_constraint(a, pltpu.HBM) for a in (load, zones, conductance, capacity, coupling)),
        *(pltpu.with_memory_space_constraint(jnp.asarray(c), pltpu.HBM) for c in (to_modes, from_modes, z_forward, z_inverse, summed, group)),
    )
    by_z, by_w = by_z.reshape(NZ), by_w.reshape(NZ)
    return by_z * z1 - by_w * w, load - by_z * q1 + by_w * u


def solution(mesh):
    in_specs = (P(None, "gx", "gy", None), P("gx", "gy", None), P(), P(), P())
    out_specs = (P(None, "gx", "gy", None), P(None, "gx", "gy", None))
    run = functools.partial(shards, mesh.shape["gx"], mesh.shape["gy"])
    return jax.shard_map(run, mesh=mesh, in_specs=in_specs, out_specs=out_specs, check_vma=False)
```

```python
import functools

import jax
import jax.numpy as jnp
import numpy as np
from jax import lax
from jax.experimental import pallas as pl
from jax.experimental.pallas import tpu as pltpu
from jax.sharding import PartitionSpec as P

BOX = 16
SPAN = BOX + 2
BX = 32
BY = 16
NZ = 128
ZONES = 8
LX = BX + 4
PX = 40
MODES = 336
OWN = SPAN * BY
KIN = OWN + 48
MOUT = OWN + 144
F32 = jnp.float32
BF16 = jnp.bfloat16
MESH = pl.DeviceIdType.MESH


def split3(matrix):
    high = np.asarray(matrix, np.float32).astype(jnp.bfloat16)
    low = (np.asarray(matrix, np.float32) - high.astype(np.float32)).astype(jnp.bfloat16)
    return high, low


def constants():
    index = np.arange(SPAN)
    basis = np.sqrt(2.0 / (SPAN + 1)) * np.sin(np.pi * np.outer(index + 1, index + 1) / (SPAN + 1))
    lam = 4.0 * np.sin(np.pi * (index + 1) / (2.0 * (SPAN + 1))) ** 2
    forward = np.zeros((SPAN, SPAN, KIN))
    inner = np.einsum("ix,jy->ijxy", basis, basis[:, 1:17])
    forward[:, :, :OWN] = inner.reshape(SPAN, SPAN, OWN)
    for side, row in ((0, 0), (1, 17)):
        start = OWN + 24 * side + 1
        forward[:, :, start : start + SPAN] = np.einsum("ix,j->ijx", basis, basis[:, row])
    full = np.zeros((MODES, KIN))
    full[: SPAN * SPAN] = forward.reshape(SPAN * SPAN, KIN)
    high, low = split3(full)
    to_modes = np.concatenate([high, high, low], axis=1)
    inverse = np.zeros((MOUT, SPAN, SPAN))
    inverse[:OWN] = np.einsum("xi,yj->xyij", basis, basis[1:17]).reshape(OWN, SPAN, SPAN)
    for place, row in enumerate((0, 1, 2, 15, 16, 17)):
        start = OWN + 24 * place + 1
        inverse[start : start + SPAN] = np.einsum("xi,j->xij", basis, basis[row])
    full = np.zeros((MOUT, MODES))
    full[:, : SPAN * SPAN] = inverse.reshape(MOUT, SPAN * SPAN)
    high, low = split3(full)
    from_modes = np.concatenate([high, high, low], axis=1)
    boxes = NZ // BOX
    count = boxes * SPAN
    banded = np.zeros((NZ, count))
    for box in range(boxes):
        for offset in range(SPAN):
            cell = BOX * box + offset - 1
            if 0 <= cell < NZ:
                banded[cell, box * SPAN : (box + 1) * SPAN] = basis[:, offset]
    rest = count - 128
    lanes = np.concatenate([np.arange(128)] + [128 + np.arange(rest)] * 3)
    wide = np.zeros((NZ, 256))
    wide[:, : lanes.size] = banded[:, lanes]
    high, low = split3(wide)
    z_forward = np.concatenate([high, high, low], axis=0)
    high, low = split3(banded.T)
    tail = np.zeros((128, NZ), jnp.bfloat16)
    tail[:rest] = high[128:]
    tail[rest : 2 * rest] = high[128:]
    tail[2 * rest : 3 * rest] = low[128:]
    z_inverse = np.concatenate([high[:128], high[:128], low[:128], tail], axis=0)
    summed = np.zeros((MODES, 256), np.float32)
    plane = (lam[:, None] + lam[None, :]).reshape(-1)
    summed[: SPAN * SPAN, : lanes.size] = plane[:, None] + lam[lanes % SPAN][None, :]
    group = np.zeros((NZ, 256))
    group[:, : lanes.size] = (np.arange(NZ)[:, None] // BOX) == (lanes // SPAN)[None, :]
    group = np.concatenate([group] * 3, axis=0).astype(jnp.bfloat16)
    return to_modes, from_modes, z_forward, z_inverse, summed, group


def lookup(zone, table):
    bit0 = (zone & 1) != 0
    bit1 = (zone & 2) != 0
    bit2 = (zone & 4) != 0

    def pick(values):
        a = jnp.where(bit0, values[1], values[0])
        b = jnp.where(bit0, values[3], values[2])
        c = jnp.where(bit0, values[5], values[4])
        d = jnp.where(bit0, values[7], values[6])
        return jnp.where(bit2, jnp.where(bit1, d, c), jnp.where(bit1, b, a))

    return [pick(values) for values in table]


def halves(value):
    high = value.astype(BF16)
    low = (value - high.astype(F32)).astype(BF16)
    return high, low


def dot(a, b):
    return jnp.dot(a, b, preferred_element_type=F32)


def body(
    nx, ny,
    load_ref, zones_ref, cond_hbm, cap_hbm, coup_hbm,
    tf_hbm, ti_hbm, zf_hbm, zi_hbm, lam_hbm, group_hbm,
    z_out, w_out, q_out, u_out, by_z_out, by_w_out,
    cond_ref, cap_ref, coup_ref, tf, ti, zf, zi, lam, group,
    r_own, r_pk, zone, zone_pk, zone_send, zone_recv,
    r_send, r_recv, r_corner_send, r_corner,
    k_own, k_pk, c_own, c_pk, cross, cross_pk,
    fx, fym, fyp, fzm, fzp, diag, diag_pk, dinv,
    u1, p1, v1, zp, q_own, q_pk, u2, p2, v2, wp,
    xl1, xc1, xcs1, yr1, dg1, dgs1, xl2, xc2, xcs2, yr2, dg2, dgs2,
    ar1, ar2,
    local_sem, send_sem, recv_sem, ar_send, ar_recv,
):
    gx = lax.axis_index("gx")
    gy = lax.axis_index("gy")
    has = {"xm": gx > 0, "xp": gx < nx - 1, "ym": gy > 0, "yp": gy < ny - 1}
    ax, ay = min(8, nx // 2), min(4, ny // 2)
    plane, depth = ax * ay, (nx // ax) * (ny // ay)
    div, rem = lax.div, lax.rem
    across, along = nx // ax, ny // ay
    gx_block, gx_in = div(gx, jnp.int32(ax)), rem(gx, jnp.int32(ax))
    gy_block, gy_in = div(gy, jnp.int32(ay)), rem(gy, jnp.int32(ay))
    here = gx_in * ay + gy_in
    level = gx_block * along + gy_block

    def plane_id(k):
        t = rem(here + k, jnp.int32(plane))
        return (gx_block * ax + div(t, jnp.int32(ay)), gy_block * ay + rem(t, jnp.int32(ay)))

    def depth_id(k):
        t = rem(level + k, jnp.int32(depth))
        return (div(t, jnp.int32(along)) * ax + gx_in, rem(t, jnp.int32(along)) * ay + gy_in)

    late = jnp.where(gx_in == 0, 0, 1).astype(jnp.int32)
    near = 1 - late
    near_gx, late_gx = gx + 1 - 2 * late, gx - 1 + 2 * late
    near_here = jnp.logical_and(near_gx >= 0, near_gx < nx)
    late_here = jnp.logical_and(late_gx >= 0, late_gx < nx)
    y_here = (has["ym"], has["yp"])
    sides = [(has["xm"], (gx - 1, gy)), (has["xp"], (gx + 1, gy)), (has["ym"], (gx, gy - 1)), (has["yp"], (gx, gy + 1))]
    for c in range(4):
        present = jnp.logical_and(sides[c // 2][0], y_here[c % 2])
        sides.append((present, (gx - 1 + 2 * (c // 2), gy - 1 + 2 * (c % 2))))

    loads = [
        pltpu.make_async_copy(load_ref.at[0], r_own.at[0, 2:34], local_sem.at[0]),
        pltpu.make_async_copy(load_ref.at[1], r_own.at[1, 2:34], local_sem.at[1]),
        pltpu.make_async_copy(zones_ref, zone.at[2:34], local_sem.at[2]),
        pltpu.make_async_copy(cond_hbm, cond_ref, local_sem.at[9]),
        pltpu.make_async_copy(cap_hbm, cap_ref, local_sem.at[10]),
        pltpu.make_async_copy(coup_hbm, coup_ref, local_sem.at[11]),
    ]
    weights = [
        pltpu.make_async_copy(source, target, local_sem.at[3 + n])
        for n, (source, target) in enumerate(
            ((tf_hbm, tf), (zf_hbm, zf), (group_hbm, group), (lam_hbm, lam), (zi_hbm, zi), (ti_hbm, ti))
        )
    ]
    barrier = pltpu.get_barrier_semaphore()
    for present, device in sides:

        @pl.when(present)
        def _():
            pl.semaphore_signal(barrier, inc=1, device_id=device, device_id_type=MESH)

    def greet_plane(k, carry):
        pl.semaphore_signal(barrier, inc=1, device_id=plane_id(k), device_id_type=MESH)
        return carry

    def greet_depth(k, carry):
        pl.semaphore_signal(barrier, inc=1, device_id=depth_id(k), device_id_type=MESH)
        return carry

    lax.fori_loop(1, depth, greet_depth, 0)
    for copy in loads + weights:
        copy.start()
    lax.fori_loop(1, plane, greet_plane, 0)

    def clear(*refs):
        for ref in refs:
            ref[...] = jnp.zeros(ref.shape, ref.dtype)

    clear(r_pk, u1, p1, u2, p2)
    for side, name in enumerate(("xm", "xp")):

        @pl.when(jnp.logical_not(has[name]))
        def _():
            clear(r_own.at[0, 1 + 33 * side], r_own.at[1, 1 + 33 * side])
            clear(xl1.at[side], xc1.at[side], xl2.at[side], xc2.at[side])

    for side, name in enumerate(("ym", "yp")):

        @pl.when(jnp.logical_not(has[name]))
        def _():
            clear(r_recv.at[side], yr1.at[side], yr2.at[side])

    for corner in range(4):

        @pl.when(jnp.logical_not(sides[4 + corner][0]))
        def _():
            clear(r_corner.at[corner], dg1.at[corner], dg2.at[corner])

    for copy in loads:
        copy.wait()

    for field in range(2):
        r_send[0, field] = r_own[field, 2:34, 0]
        r_send[1, field] = r_own[field, 2:34, BY - 1]
    for corner, (layer, row) in enumerate(((2, 0), (2, 15), (33, 0), (33, 15))):
        for field in range(2):
            r_corner_send[corner, field : field + 1] = r_own[field, layer, row : row + 1]

    members = jnp.int32(plane - 1 + depth - 1)
    for present, _ in sides:
        members = members + present.astype(jnp.int32)
    pl.semaphore_wait(barrier, members)

    def push(present, device, source, target, out_slot, in_slot):
        @pl.when(present)
        def _():
            pltpu.make_async_remote_copy(
                src_ref=source,
                dst_ref=target,
                send_sem=send_sem.at[out_slot],
                recv_sem=recv_sem.at[in_slot],
                device_id=device,
                device_id_type=MESH,
            ).start()

    def pushed(present, source, slot):
        @pl.when(present)
        def _():
            pltpu.make_async_copy(source, source, send_sem.at[slot]).wait()

    def arrived(present, target, slot):
        @pl.when(present)
        def _():
            pltpu.make_async_copy(target, target, recv_sem.at[slot]).wait()

    for n in range(2):
        push(*sides[n], r_own.at[:, 2 + 31 * n], r_own.at[:, 34 - 33 * n], n, 1 - n)
    for c in range(4):
        push(*sides[4 + c], r_corner_send.at[c], r_corner.at[3 - c], 4 + c, 7 - c)
    for n in range(2):
        push(*sides[2 + n], r_send.at[n], r_recv.at[1 - n], 2 + n, 3 - n)
    for n in range(2):
        push(*sides[n], zone.at[2 + 30 * n : 4 + 30 * n], zone.at[34 - 34 * n : 36 - 34 * n], 30 + n, 31 - n)

    table = [[ref[f, q] for q in range(ZONES)] for ref in (cond_ref, cap_ref) for f in range(2)]
    table.append([coup_ref[q] for q in range(ZONES)])

    def own_coefficients(layer, sums):
        k0, k1, c0, c1, share = lookup(zone[layer], table)
        k_own[layer, 8:24] = k0
        k_own[LX + layer, 8:24] = k1
        c_own[0, layer] = c0
        c_own[1, layer] = c1
        cross[layer] = share * jnp.sqrt(c0 * c1)
        return tuple(s + v[:8] + v[8:] for s, v in zip(sums, (c0, c1, k0, k1)))

    zero = jnp.zeros((8, NZ), F32)
    pieces = []
    for box in range(2):
        sums = lax.fori_loop(2 + BOX * box, 2 + BOX * (box + 1), own_coefficients, (zero,) * 4)
        pieces.extend(jnp.sum(s, axis=0, keepdims=True) for s in sums)
    total = jnp.concatenate(pieces, axis=0)
    part0 = total.astype(BF16)
    rest = total - part0.astype(F32)
    part1 = rest.astype(BF16)
    part2 = (rest - part1.astype(F32)).astype(BF16)
    for copy in weights:
        copy.wait()
    means = dot(jnp.concatenate([part0, part1, part2], axis=1), group[...]) * (1.0 / BOX**3)
    lane = lax.broadcasted_iota(jnp.int32, (1, 256), 1)
    unused = jnp.where(lane >= 128 + 48, 1.0, 0.0)
    for box in range(2):
        for field in range(2):
            cbar = means[4 * box + field : 4 * box + field + 1] + unused
            kbar = means[4 * box + 2 + field : 4 * box + 3 + field]
            dinv[box, MODES * field : MODES * (field + 1)] = 1.0 / (cbar + kbar * lam[...])

    lane_tail = lax.broadcasted_iota(jnp.int32, (1, 128), 1)
    low_lanes = jnp.logical_and(lane_tail >= 16, lane_tail < 32)

    def apply_box(own, packed, out, out_pk, box):
        layers = pl.ds(1 + BOX * box, SPAN)
        spots = pl.ds(pl.multiple_of(BOX * box, 8), 24)
        columns = []
        for field in range(2):
            inner = own[field, layers].reshape(OWN, NZ)
            columns.append(jnp.concatenate([inner] + [packed[side, field, spots] for side in range(2)], axis=0))
        high, low = halves(jnp.concatenate(columns, axis=1))
        modes = dot(tf[...], jnp.concatenate([high, low, high], axis=0))
        high, low = halves(jnp.concatenate([modes[:, :NZ], modes[:, NZ:]], axis=0))
        deep = dot(jnp.concatenate([high, low, high], axis=1), zf[...]) * dinv[box]
        high, low = halves(deep[:, :128])
        tail = deep[:, 128:]
        tail_high = tail.astype(BF16).astype(F32)
        tail = jnp.where(low_lanes, tail - tail_high, tail_high).astype(BF16)
        lines = dot(jnp.concatenate([high, low, high, tail], axis=1), zi[...])
        columns = [lines[:MODES], lines[MODES:]]
        high, low = halves(jnp.concatenate(columns, axis=1))
        cells = dot(ti[...], jnp.concatenate([high, low, high], axis=0))
        for field in range(2):
            mine = cells[:, NZ * field : NZ * (field + 1)]
            out[field, layers] += mine[:OWN].reshape(SPAN, BY, NZ)
            out_pk[:, field, spots] += mine[OWN:].reshape(6, 24, NZ)

    def tile(side):
        return pl.ds(pl.multiple_of(32 * side, 8), 4)

    def x_messages(width, own, packed, bufs, base, side, present, side_gx, act):
        x_layers, x_corner, x_corner_send, y_rows, corners, corners_send = bufs
        layers = pl.ds(1 + (34 - width) * side, width)
        device = (side_gx, gy)
        if act == "push":
            for place, row in enumerate((0, 5)):
                x_corner_send[side, place] = packed[row, :, tile(side)]
            push(present, device, own.at[:, layers], x_layers.at[1 - side], base + side, base + 1 - side)
            push(present, device, x_corner_send.at[side], x_corner.at[1 - side], base + 8 + side, base + 9 - side)
        elif act == "pushed":
            pushed(present, own.at[:, layers], base + side)
            pushed(present, x_corner_send.at[side], base + 8 + side)
        else:
            arrived(present, x_layers.at[side], base + side)
            arrived(present, x_corner.at[side], base + 8 + side)
        for n in range(2):
            c = 2 * side + n
            both = jnp.logical_and(present, y_here[n])
            if act == "push":
                for place in range(width):
                    corners_send[c, place] = packed[(6 - width) * n + place, :, tile(side)]
                device = (side_gx, gy - 1 + 2 * n)
                push(both, device, corners_send.at[c], corners.at[3 - c], base + 4 + c, base + 7 - c)
            elif act == "pushed":
                pushed(both, corners_send.at[c], base + 4 + c)
            else:
                arrived(both, corners.at[c], base + 4 + c)

    def y_messages(width, packed, bufs, base, act):
        y_rows = bufs[3]
        for n in range(2):
            rows = packed.at[(6 - width) * n : (6 - width) * n + width]
            if act == "push":
                push(*sides[2 + n], rows, y_rows.at[1 - n], base + 2 + n, base + 3 - n)
            elif act == "pushed":
                pushed(y_here[n], rows, base + 2 + n)
            else:
                arrived(y_here[n], y_rows.at[n], base + 2 + n)

    rows_pk = lax.broadcasted_iota(jnp.int32, (PX, NZ), 0)

    def corner_rows(side):
        for n in range(2):
            for field in range(2):
                row = r_corner[2 * side + n, field : field + 1]
                r_pk[n, field] = jnp.where(rows_pk == 1 + 33 * side, row, r_pk[n, field])

    for n in range(2):
        arrived(y_here[n], r_recv.at[n], 2 + n)
        for field in range(2):
            r_pk[n, field, 2:34] = r_recv[n, field]
        arrived(jnp.logical_and(near_here, y_here[n]), r_corner.at[2 * near + n], 4 + 2 * near + n)
    arrived(near_here, r_own.at[:, 1 + 33 * near], near)
    corner_rows(near)
    set1 = (xl1, xc1, xcs1, yr1, dg1, dgs1)
    set2 = (xl2, xc2, xcs2, yr2, dg2, dgs2)
    apply_box(r_own, r_pk, u1, p1, near)
    x_messages(3, u1, p1, set1, 10, near, near_here, near_gx, "push")
    for n in range(2):
        arrived(jnp.logical_and(late_here, y_here[n]), r_corner.at[2 * late + n], 4 + 2 * late + n)
    arrived(late_here, r_own.at[:, 1 + 33 * late], late)
    corner_rows(late)
    apply_box(r_own, r_pk, u1, p1, late)
    x_messages(3, u1, p1, set1, 10, late, late_here, late_gx, "push")

    for n in range(2):
        arrived(sides[n][0], zone.at[34 * n : 34 * n + 2], 30 + n)

        @pl.when(jnp.logical_not(sides[n][0]))
        def _():
            edge = zone[2 + 31 * n]
            zone[34 * n] = edge
            zone[34 * n + 1] = edge

    for place, row in enumerate((0, 1, 14, 15)):
        zone_send[place] = jnp.zeros((PX, NZ), jnp.int32)
        zone_send[place, 0:LX] = zone[:, row]
    for n in range(2):
        push(*sides[2 + n], zone_send.at[2 * n : 2 * n + 2], zone_recv.at[1 - n], 32 + n, 33 - n)
    y_messages(3, p1, set1, 10, "push")
    x_messages(3, u1, p1, set1, 10, late, late_here, late_gx, "pushed")
    for layer in (0, 1, 34, 35):
        k0, k1, c0, c1, share = lookup(zone[layer], table)
        k_own[layer, 8:24] = k0
        k_own[LX + layer, 8:24] = k1
        c_own[0, layer] = c0
        c_own[1, layer] = c1
        cross[layer] = share * jnp.sqrt(c0 * c1)
    for n in range(2):
        arrived(y_here[n], zone_recv.at[n], 32 + n)

        @pl.when(jnp.logical_not(y_here[n]))
        def _():
            edge = zone_send[3 * n]
            zone_recv[n, 0] = edge
            zone_recv[n, 1] = edge

    for place in range(6):
        packed_zone = (
            zone_recv[0, place] if place < 2
            else zone_send[0] if place == 2
            else zone_send[3] if place == 3
            else zone_recv[1, place - 4]
        )
        k0, k1, c0, c1, share = lookup(packed_zone, table)
        k_pk[place, 0] = k0
        k_pk[place, 1] = k1
        if place in (1, 4):
            side = 0 if place == 1 else 1
            c_pk[side, 0] = c0
            c_pk[side, 1] = c1
            cross_pk[side] = share * jnp.sqrt(c0 * c1)
            for field, value in enumerate((k0, k1)):
                k_own[LX * field : LX * (field + 1), 7 if side == 0 else 24] = value[:LX]

    lanes = lax.broadcasted_iota(jnp.int32, (BY, NZ), 1)
    first_lane, last_lane = lanes == 0, lanes == NZ - 1
    for field in range(2):
        fx[field, 0] = 0.5 * (k_own[LX * field, 8:24] + k_own[LX * field + 1, 8:24])

    def faces(layer, carry):
        for field in range(2):
            spot = LX * field + layer
            center = k_own[spot, 8:24]
            x_low = fx[field, layer - 1]
            x_high = 0.5 * (center + k_own[spot + 1, 8:24])
            fx[field, layer] = x_high
            y_low = 0.5 * (center + k_own[spot, 7:23])
            y_high = 0.5 * (center + k_own[spot, 9:25])
            z_low = 0.5 * (center + jnp.where(first_lane, center, pltpu.roll(center, 1, axis=1)))
            z_high = 0.5 * (center + jnp.where(last_lane, center, pltpu.roll(center, NZ - 1, axis=1)))
            fym[field, layer] = y_low
            fyp[field, layer] = y_high
            fzm[field, layer] = jnp.where(first_lane, 0.0, z_low)
            fzp[field, layer] = jnp.where(last_lane, 0.0, z_high)
            diag[field, layer] = c_own[field, layer] + (
                (x_low + x_high) + (y_low + y_high) + (z_low + z_high)
            )
        return carry

    lax.fori_loop(1, 35, faces, 0, unroll=2)

    lanes_pk = lax.broadcasted_iota(jnp.int32, (PX, NZ), 1)
    first_pk, last_pk = lanes_pk == 0, lanes_pk == NZ - 1

    def rim_faces(side, field):
        center = k_pk[1 + 3 * side, field]
        x_low = 0.5 * (center + pltpu.roll(center, 1, axis=0))
        x_high = 0.5 * (center + pltpu.roll(center, PX - 1, axis=0))
        y_low = 0.5 * (center + k_pk[3 * side, field])
        y_high = 0.5 * (center + k_pk[3 * side + 2, field])
        z_low = 0.5 * (center + jnp.where(first_pk, center, pltpu.roll(center, 1, axis=1)))
        z_high = 0.5 * (center + jnp.where(last_pk, center, pltpu.roll(center, NZ - 1, axis=1)))
        return x_low, x_high, y_low, y_high, z_low, z_high

    def assemble_near(width, own, packed, bufs, total_v, total_pk, margin):
        x_layers, x_corner, _, y_rows, corners, _ = bufs
        low0 = 3 - width
        for field in range(2):
            base = LX * field

            def copy_layer(layer, carry):
                total_v[base + layer, 8:24] = own[field, layer]
                return carry

            lax.fori_loop(3, 33, copy_layer, 0, unroll=6)
            for side, present in ((near, near_here), (late, late_here)):
                for step in range(width):
                    layer = low0 + (33 - low0) * side + step
                    value = own[field, layer]
                    if side is near:
                        value = value + x_layers[near, field, step]
                    beyond = jnp.logical_or(layer < 2, layer > 33)
                    drop = jnp.logical_and(beyond, jnp.logical_not(present))
                    total_v[base + layer, 8:24] = jnp.where(drop, 0.0, value)
        low_x = jnp.logical_and(rows_pk < 2, jnp.logical_not(has["xm"]))
        high_x = jnp.logical_and(rows_pk > 33, jnp.logical_not(has["xp"]))
        beyond_x = jnp.logical_or(low_x, high_x)
        for n in range(2):
            for step in range(width):
                y = 1 - width + step if n == 0 else 15 + step
                place = y + 2 if n == 0 else y - 12
                total_pk[place] = y_rows[n, step]
                total_pk[place, :, tile(near)] += corners[2 * near + n, step]
                if y == -1 or y == 16:
                    total_pk[place] += packed[5 * n]
                    total_pk[place, :, tile(near)] += x_corner[near, n]
                drop = beyond_x
                if y < 0 or y > 15:
                    drop = jnp.logical_or(drop, jnp.logical_not(y_here[n]))
                for field in range(2):
                    total_pk[place, field] = jnp.where(drop, 0.0, total_pk[place, field])
        for field in range(2):
            lo = 2 - margin
            count = BX + 2 * margin
            window = slice(LX * field + lo, LX * field + lo + count)
            for place, outer, row, halo in ((2, 1, 8, 7), (3, 4, 23, 24)):
                edge = total_v[window, row] + total_pk[place, field, lo : lo + count]
                total_v[window, row] = edge
                total_pk[place, field, lo : lo + count] = edge
                total_v[window, halo] = total_pk[outer, field, lo : lo + count]

    def assemble_late(width, bufs, total_v, total_pk):
        x_layers, x_corner, _, _, corners, _ = bufs
        low0 = 3 - width
        for field in range(2):
            for step in range(width):
                spot = LX * field + low0 + (33 - low0) * late + step
                total_v[spot, 8:24] += x_layers[late, field, step]
            block = pl.ds(LX * field + 32 * late, 4)
            for n, edge_place, outer, row, halo in ((0, 2, 1, 8, 7), (1, 3, 4, 23, 24)):
                for step in range(width):
                    y = 1 - width + step if n == 0 else 15 + step
                    place = y + 2 if n == 0 else y - 12
                    piece = corners[2 * late + n, step, field]
                    if y == -1 or y == 16:
                        piece = piece + jnp.where(y_here[n], x_corner[late, n, field], 0.0)
                    if place == edge_place:
                        edge = total_v[block, row] + piece
                        total_v[block, row] = edge
                        total_pk[place, field, tile(late)] = edge
                    else:
                        total_pk[place, field, tile(late)] += piece
                total_v[block, halo] = total_pk[outer, field, tile(late)]

    def operate(vec, layer, field):
        spot = LX * field + layer
        center = vec[spot, 8:24]
        value = diag[field, layer] * center + cross[layer] * vec[LX * (1 - field) + layer, 8:24]
        value = value - fx[field, layer - 1] * vec[spot - 1, 8:24] - fx[field, layer] * vec[spot + 1, 8:24]
        value = value - fym[field, layer] * vec[spot, 7:23] - fyp[field, layer] * vec[spot, 9:25]
        value = value - fzm[field, layer] * pltpu.roll(center, 1, axis=1)
        return value - fzp[field, layer] * pltpu.roll(center, NZ - 1, axis=1), center

    def fold(value):
        return value[:8] + value[8:]

    def first_image(layer, carry):
        rz, pq = carry
        for field in range(2):
            value, center = operate(v1, layer, field)
            q_own[field, layer] = value
            q_out[field, layer - 2] = value
            z_out[field, layer - 2] = center
            rz = rz + fold(r_own[field, layer] * center)
            pq = pq + fold(center * value)
        return rz, pq

    def rim_layer(side, present):
        layer = 1 + 33 * side
        for field in range(2):
            value, _ = operate(v1, layer, field)
            q_own[field, layer] = jnp.where(present, value, 0.0)

    def rim_rows():
        for side in range(2):
            place = 1 + 3 * side
            low_x = jnp.logical_and(rows_pk < 2, jnp.logical_not(has["xm"]))
            high_x = jnp.logical_and(rows_pk > 33, jnp.logical_not(has["xp"]))
            drop = jnp.logical_or(jnp.logical_or(low_x, high_x), jnp.logical_not(y_here[side]))
            drop = jnp.logical_or(drop, jnp.logical_or(rows_pk < 1, rows_pk > 34))
            for field in range(2):
                x_low, x_high, y_low, y_high, z_low, z_high = rim_faces(side, field)
                center = zp[place, field]
                value = c_pk[side, field] + ((x_low + x_high) + (y_low + y_high) + (z_low + z_high))
                value = value * center + cross_pk[side] * zp[place, 1 - field]
                value = value - x_low * pltpu.roll(center, 1, axis=0) - x_high * pltpu.roll(center, PX - 1, axis=0)
                value = value - y_low * zp[3 * side, field] - y_high * zp[3 * side + 2, field]
                value = value - jnp.where(first_pk, 0.0, z_low) * pltpu.roll(center, 1, axis=1)
                value = value - jnp.where(last_pk, 0.0, z_high) * pltpu.roll(center, NZ - 1, axis=1)
                q_pk[side, field] = jnp.where(drop, 0.0, value)

    def inner_layers(step, carry, image):
        return image(4 - 2 * late + step, carry)

    x_messages(3, u1, p1, set1, 10, near, near_here, near_gx, "arrived")
    y_messages(3, p1, set1, 10, "arrived")
    assemble_near(3, u1, p1, set1, v1, zp, 2)
    sums = lax.fori_loop(0, 30, functools.partial(inner_layers, image=first_image), (zero, zero), unroll=3)
    rim_layer(near, near_here)
    rim_rows()
    apply_box(q_own, q_pk, u2, p2, near)
    x_messages(2, u2, p2, set2, 20, near, near_here, near_gx, "push")
    x_messages(3, u1, p1, set1, 10, late, late_here, late_gx, "arrived")
    assemble_late(3, set1, v1, zp)
    for step in range(2):
        sums = first_image(2 + 30 * late + step, sums)
    rz, pq = sums
    rim_layer(late, late_here)
    rim_rows()
    apply_box(q_own, q_pk, u2, p2, late)
    x_messages(2, u2, p2, set2, 20, late, late_here, late_gx, "push")
    x_messages(2, u2, p2, set2, 20, late, late_here, late_gx, "pushed")
    y_messages(2, p2, set2, 20, "push")

    def second_image(layer, carry):
        rw, qw, zu, wu = carry
        for field in range(2):
            value, center = operate(v2, layer, field)
            u_out[field, layer - 2] = value
            w_out[field, layer - 2] = center
            rw = rw + fold(r_own[field, layer] * center)
            qw = qw + fold(q_own[field, layer] * center)
            zu = zu + fold(v1[LX * field + layer, 8:24] * value)
            wu = wu + fold(center * value)
        return rw, qw, zu, wu

    x_messages(2, u2, p2, set2, 20, near, near_here, near_gx, "arrived")
    y_messages(2, p2, set2, 20, "arrived")
    assemble_near(2, u2, p2, set2, v2, wp, 1)
    sums = lax.fori_loop(0, 30, functools.partial(inner_layers, image=second_image), (zero,) * 4, unroll=3)
    for n in range(2):
        pushed(sides[n][0], r_own.at[:, 2 + 31 * n], n)
        pushed(sides[n][0], zone.at[2 + 30 * n : 4 + 30 * n], 30 + n)
        pushed(y_here[n], r_send.at[n], 2 + n)
        pushed(y_here[n], zone_send.at[2 * n : 2 * n + 2], 32 + n)
    for c in range(4):
        pushed(sides[4 + c][0], r_corner_send.at[c], 4 + c)
    x_messages(3, u1, p1, set1, 10, near, near_here, near_gx, "pushed")
    y_messages(3, p1, set1, 10, "pushed")
    x_messages(2, u2, p2, set2, 20, near, near_here, near_gx, "pushed")
    y_messages(2, p2, set2, 20, "pushed")
    x_messages(2, u2, p2, set2, 20, late, late_here, late_gx, "arrived")
    assemble_late(2, set2, v2, wp)
    for step in range(2):
        sums = second_image(2 + 30 * late + step, sums)
    rw, qw, zu, wu = sums

    rows = [jnp.sum(v, axis=0, keepdims=True) for v in (rz, pq, rw, qw, zu, wu)]
    stack = jnp.concatenate(rows + [jnp.zeros((2, NZ), F32)], axis=0)
    for shift in (64, 32, 16):
        stack = stack + pltpu.roll(stack, shift, axis=1)
    group_of = lax.broadcasted_iota(jnp.int32, (8, NZ), 1) // 16
    mine = group_of == lax.broadcasted_iota(jnp.int32, (8, NZ), 0)
    spot = lax.broadcasted_iota(jnp.int32, (1, NZ), 1) // 16
    row = jnp.sum(jnp.where(mine, stack, 0.0), axis=0, keepdims=True)
    ar1[0] = row

    def all_reduce(slots, count, device_of, number):
        def send(k, carry):
            pltpu.make_async_remote_copy(
                src_ref=slots.at[0],
                dst_ref=slots.at[k],
                send_sem=ar_send.at[number],
                recv_sem=ar_recv.at[number],
                device_id=device_of(k),
                device_id_type=MESH,
            ).start()
            return carry

        far_first = sorted(range(1, count), key=lambda k: -min(k, count - k))
        for k in far_first if number == 1 else range(count - 1, 0, -1):
            send(k, 0)
        others = slots.at[1:count]
        pltpu.make_async_copy(others, others, ar_recv.at[number]).wait()
        pltpu.make_async_copy(others, others, ar_send.at[number]).wait()
        return jnp.sum(slots[...], axis=0)

    ar2[0] = all_reduce(ar1, plane, plane_id, 0)
    products = all_reduce(ar2, depth, depth_id, 1)
    rz, pq, rw, qw, zu, wu = (
        jnp.sum(jnp.where(spot == n, products, 0.0), axis=1, keepdims=True) for n in range(6)
    )
    alpha = rz / pq
    rz2 = rz - alpha * (rw + pq) + alpha * alpha * qw
    grow = 1.0 + rz2 / rz
    curve = grow * grow * pq - grow * alpha * (zu + qw) + alpha * alpha * wu
    alpha2 = rz2 / curve
    by_z_out[...] = jnp.broadcast_to(alpha + alpha2 * grow, (1, NZ))
    by_w_out[...] = jnp.broadcast_to(alpha2 * alpha, (1, NZ))


def shards(nx, ny, load, zones, conductance, capacity, coupling):
    to_modes, from_modes, z_forward, z_inverse, summed, group = constants()
    ax, ay = min(8, nx // 2), min(4, ny // 2)
    plane, depth = ax * ay, (nx // ax) * (ny // ay)
    vmem = lambda *shape, dtype=F32: pltpu.VMEM(shape, dtype)
    scratch = [
        pltpu.SMEM((2, ZONES), F32), pltpu.SMEM((2, ZONES), F32), pltpu.SMEM((ZONES,), F32),
        vmem(*to_modes.shape, dtype=BF16), vmem(*from_modes.shape, dtype=BF16),
        vmem(*z_forward.shape, dtype=BF16), vmem(*z_inverse.shape, dtype=BF16),
        vmem(*summed.shape), vmem(*group.shape, dtype=BF16),
        vmem(2, LX, BY, NZ), vmem(2, 2, PX, NZ),
        vmem(LX, BY, NZ, dtype=jnp.int32), vmem(8, NZ, dtype=jnp.int32),
        vmem(4, PX, NZ, dtype=jnp.int32), vmem(2, 2, PX, NZ, dtype=jnp.int32),
        vmem(2, 2, BX, NZ), vmem(2, 2, BX, NZ), vmem(4, 2, NZ), vmem(4, 2, NZ),
        vmem(2 * LX, 32, NZ), vmem(6, 2, PX, NZ), vmem(2, LX, BY, NZ), vmem(2, 2, PX, NZ),
        vmem(LX, BY, NZ), vmem(2, PX, NZ),
        vmem(2, LX, BY, NZ), vmem(2, LX, BY, NZ), vmem(2, LX, BY, NZ), vmem(2, LX, BY, NZ),
        vmem(2, LX, BY, NZ), vmem(2, LX, BY, NZ), vmem(8, NZ), vmem(2, 2 * MODES, 256),
        vmem(2, LX, BY, NZ), vmem(6, 2, PX, NZ), vmem(2 * LX, 32, NZ), vmem(6, 2, PX, NZ),
        vmem(2, LX, BY, NZ), vmem(2, 2, PX, NZ),
        vmem(2, LX, BY, NZ), vmem(6, 2, PX, NZ), vmem(2 * LX, 32, NZ), vmem(6, 2, PX, NZ),
    ]
    for width in (3, 2):
        scratch += [
            vmem(2, 2, width, BY, NZ), vmem(2, 2, 2, 4, NZ), vmem(2, 2, 2, 4, NZ),
            vmem(2, width, 2, PX, NZ), vmem(4, width, 2, 4, NZ), vmem(4, width, 2, 4, NZ),
        ]
    scratch += [
        vmem(plane, 1, NZ), vmem(depth, 1, NZ),
        pltpu.SemaphoreType.DMA((12,)), pltpu.SemaphoreType.DMA((34,)), pltpu.SemaphoreType.DMA((34,)),
        pltpu.SemaphoreType.DMA((2,)), pltpu.SemaphoreType.DMA((2,)),
    ]
    any_spec = pl.BlockSpec(memory_space=pltpu.HBM)
    out = pl.BlockSpec(memory_space=pltpu.VMEM)
    shape = jax.ShapeDtypeStruct((2, BX, BY, NZ), F32)
    z1, w, q1, u, by_z, by_w = pl.pallas_call(
        functools.partial(body, nx, ny),
        out_shape=(shape,) * 4 + (jax.ShapeDtypeStruct((1, NZ), F32),) * 2,
        in_specs=[any_spec] * 11,
        out_specs=(out,) * 6,
        scratch_shapes=scratch,
        compiler_params=pltpu.CompilerParams(
            collective_id=0, has_side_effects=True, vmem_limit_bytes=48 * 1024 * 1024
        ),
        name="pcg",
    )(
        *(pltpu.with_memory_space_constraint(a, pltpu.HBM) for a in (load, zones, conductance, capacity, coupling)),
        *(pltpu.with_memory_space_constraint(jnp.asarray(c), pltpu.HBM) for c in (to_modes, from_modes, z_forward, z_inverse, summed, group)),
    )
    by_z, by_w = by_z.reshape(NZ), by_w.reshape(NZ)
    return by_z * z1 - by_w * w, load - by_z * q1 + by_w * u


def solution(mesh):
    in_specs = (P(None, "gx", "gy", None), P("gx", "gy", None), P(), P(), P())
    out_specs = (P(None, "gx", "gy", None), P(None, "gx", "gy", None))
    run = functools.partial(shards, mesh.shape["gx"], mesh.shape["gy"])
    return jax.shard_map(run, mesh=mesh, in_specs=in_specs, out_specs=out_specs, check_vma=False)
```
